32 devices in a mesh: ctx: 4 (over z), tp: 4 (over y, x), dp: 2 (over core).
Axes of the slice: x: 2, y: 2, z: 4, core: 2. Of those that a mesh axis runs over, the one named last changes fastest.
Arguments:
- queries: bfloat16 [6144, 2048], P(('dp', 'ctx'), 'tp'), parts along dimension 0, may hold values from -6 to 6
- key_rows: bfloat16 [6144, 2048], P(('dp', 'ctx'), 'tp'), parts along dimension 0, may hold values from -6 to 6
- values: bfloat16 [6144, 2048], P(('dp', 'ctx'), 'tp'), parts along dimension 0, may hold values from -6 to 6
- doc_lengths: int32 [16], P('dp'), parts along dimension 0, may hold values from 1 to 2304, 3072 in all
- in_gate: bfloat16 [6144, 2048], P(('dp', 'ctx'), 'tp'), parts along dimension 0, may hold values from -6 to 6
- out_gate: bfloat16 [6144, 2048], P(('dp', 'ctx'), 'tp'), parts along dimension 0, may hold values from -6 to 6
- filter_taps: float32 [4096, 3072], P(('dp', 'tp'), 'ctx'), parts along dimension 0, may hold values from -0.21875 to 0.21875
Outputs:
- attn_out: bfloat16 [6144, 2048], P(('dp', 'ctx'), 'tp'), parts along dimension 0
- hyena_out: bfloat16 [6144, 2048], P(('dp', 'ctx'), 'tp'), parts along dimension 0
The draws below stay inside these ranges and needn't reach their ends.
There are 2 independent parts, one for each index of `dp`. The reference program is written for one: setup_inputs(seed, part) draws one part's arguments, and reference() takes and returns one part's arrays. A program takes and returns all parts, laid end to end along the dimension named above; each array names one. Nothing has to cross between parts.
Inputs may be any that keep to these rules, and one draw needn't show every extreme that they name: `doc_lengths`: the lengths sum to 3072, and the longest is exactly 2304.
All inputs are finite; a program needn't handle non-finite values.
Results may differ from the reference program's by a relative error of at most 0.012.
Values may be sent and summed in bfloat16 or wider, within the bound.
A program may use at most 192 MiB of HBM per device.

```python
import math
import jax
import jax.numpy as jnp
import numpy as np
from jax import lax

HEADS = 16
HEAD_DIM = 128
TOK_DEV = 768
KV_REACH = 3
CHANNELS = 2048
SEQ = 3072
DOCS = 8
MOST_DOC = 2304


def paired_rows(key):
    folded = jax.random.fold_in(key, 4217)
    query_seed, key_seed = jax.random.split(folded, 2)
    channels = HEADS * HEAD_DIM
    query_draw = jnp.clip(jax.random.normal(query_seed, (SEQ, channels), jnp.float32), -6.0, 6.0)
    key_draw = jnp.clip(jax.random.normal(key_seed, (SEQ, channels), jnp.float32), -6.0, 6.0)
    return (query_draw, key_draw)


def draw_queries(key, part):
    return paired_rows(key)[0].astype(jnp.bfloat16)


def draw_key_rows(key, part):
    return paired_rows(key)[1].astype(jnp.bfloat16)


def levels(rng, shape, cuts, smallest, high):
    factor_of = 1.0
    for position, blocks in cuts:
        heights = jax.random.uniform(jax.random.fold_in(jax.random.fold_in(rng, 6), position), (blocks,), jnp.float32, smallest / len(cuts), high / len(cuts))
        factor_of = factor_of * jnp.repeat(jnp.exp(heights), shape[position] // blocks).reshape((-1,) + (1,) * (len(shape) - 1 - position))
    return factor_of


def split_up(amount, total, bound, slope):
    portions = [(1 << 20) // math.isqrt(grade ** slope) + 1 for grade in range(2, amount + 1)]
    spare, given = total - bound - (amount - 1), [1] * (amount - 1)
    while spare > 0:
        candidates = [i for i in range(amount - 1) if given[i] < bound]
        whole, budget = sum([portions[i] for i in candidates]), spare
        for i in candidates:
            extra = min(bound - given[i], max(1, budget * portions[i] // whole), spare)
            given[i] = given[i] + extra
            spare = spare - extra
    return np.array([bound] + given)


def ragged(key, number_of, total, most, slope):
    if number_of == 2:
        one = jax.random.randint(key, (), max(1, total - most), min(most, total - 1) + 1)
        return jnp.stack([one, total - one])
    tallies = jnp.asarray(split_up(number_of, total, most, slope), jnp.int32)
    twos = (number_of - 1) // 2
    giver, taker = tallies[1:1 + 2 * twos:2], tallies[2:2 + 2 * twos:2]
    room = jnp.minimum(giver - 1, most - taker)
    shifted = jax.random.randint(jax.random.fold_in(key, 1), (twos,), 0, 1 << 20) % (room + 1)
    tallies = tallies.at[1:1 + 2 * twos:2].set(giver - shifted).at[2:2 + 2 * twos:2].set(taker + shifted)
    return tallies[jax.random.permutation(jax.random.fold_in(key, 2), number_of)]


def noise(stream_key, extent, scale, most, cuts=(), held_as=jnp.bfloat16):
    factor_of = levels(stream_key, extent, cuts, -0.22, 0.18) if cuts else 1.0
    entries = jax.random.normal(stream_key, extent, jnp.float32) * scale * factor_of
    return jnp.minimum(jnp.maximum(entries, -most), most).astype(held_as)


def setup_inputs(seed: int = 0, part: int = 0) -> dict:
    key_list = jax.random.split(jax.random.key(seed), 8)
    part_keys = jax.random.split(jax.random.fold_in(key_list[7], part), 8)
    return {
        "queries": draw_queries(jax.random.fold_in(jax.random.fold_in(key_list[7], part), 71), part),
        "key_rows": draw_key_rows(jax.random.fold_in(jax.random.fold_in(key_list[7], part), 71), part),
        "values": noise(part_keys[2], (SEQ, CHANNELS), 1.0, 6.0, ((0, 4), (1, 4))),
        "doc_lengths": ragged(part_keys[3], DOCS, SEQ, MOST_DOC, 2).astype(jnp.int32),
        "in_gate": noise(part_keys[4], (SEQ, CHANNELS), 1.0, 6.0, ((0, 4), (1, 4))),
        "out_gate": noise(part_keys[5], (SEQ, CHANNELS), 1.0, 6.0, ((0, 4), (1, 4))),
        "filter_taps": noise(part_keys[6], (CHANNELS, SEQ), (SEQ // 4) ** -0.5, 0.21875, ((0, 4), (1, 4)), jnp.float32),
    }


masked_score = -1e+30

def doc_of(positions, doc_lengths):
    starts = jnp.cumsum(doc_lengths) - doc_lengths
    inside = (starts[None, :] <= positions[:, None]).astype(jnp.int32)
    return lax.optimization_barrier(jnp.sum(inside, axis=1)) - 1

def reference(queries, key_rows, values, doc_lengths, in_gate, out_gate, filter_taps):
    channels = queries.shape[1]
    head_count = channels // HEAD_DIM
    positions = jnp.arange(SEQ, dtype=jnp.int32)
    doc_index = doc_of(positions, doc_lengths)
    reach = KV_REACH * TOK_DEV
    window = reach + TOK_DEV
    padded_keys = jnp.concatenate([jnp.zeros((reach, channels), jnp.bfloat16), key_rows], axis=0)
    padded_values = jnp.concatenate([jnp.zeros((reach, channels), jnp.bfloat16), values], axis=0)
    padded_docs = jnp.concatenate([jnp.full((reach,), -1, jnp.int32), doc_index])
    padded_pos = jnp.concatenate([jnp.arange(reach, dtype=jnp.int32) - reach, positions])

    def one_block(block_index):
        block_start = (block_index * TOK_DEV).astype(jnp.int32)
        query_block = lax.dynamic_slice_in_dim(queries, block_start, TOK_DEV, 0).astype(jnp.float32).reshape(TOK_DEV, head_count, HEAD_DIM)
        query_pos = lax.dynamic_slice_in_dim(positions, block_start, TOK_DEV, 0)
        query_doc = lax.dynamic_slice_in_dim(doc_index, block_start, TOK_DEV, 0)
        key_block = lax.dynamic_slice_in_dim(padded_keys, block_start, window, 0).astype(jnp.float32).reshape(window, head_count, HEAD_DIM)
        value_block = lax.dynamic_slice_in_dim(padded_values, block_start, window, 0).astype(jnp.float32).reshape(window, head_count, HEAD_DIM)
        key_doc = lax.dynamic_slice_in_dim(padded_docs, block_start, window, 0)
        key_pos = lax.dynamic_slice_in_dim(padded_pos, block_start, window, 0)
        allowed = (key_doc[None, :] == query_doc[:, None]) & (key_pos[None, :] <= query_pos[:, None])
        scores = jnp.einsum('qhd,khd->hqk', query_block, key_block) / math.sqrt(HEAD_DIM)
        scores = jnp.where(allowed[None], scores, masked_score)
        top_score = lax.optimization_barrier(jnp.max(scores, axis=2, keepdims=True))
        exp_scores = jnp.exp(scores - top_score)
        row_total = lax.optimization_barrier(jnp.sum(exp_scores, axis=2))
        rounded = lax.optimization_barrier(exp_scores.astype(jnp.bfloat16)).astype(jnp.float32)
        attended = jnp.einsum('hqk,khd->qhd', rounded, value_block) / row_total.T[:, :, None]
        return attended.reshape(TOK_DEV, channels).astype(jnp.bfloat16)
    blocks = lax.map(one_block, jnp.arange(SEQ // TOK_DEV, dtype=jnp.int32))
    attn_out = blocks.reshape(SEQ, channels)
    gated = in_gate.astype(jnp.float32) * attn_out.astype(jnp.float32)
    length = 2 * SEQ
    spectrum = jnp.fft.rfft(gated, n=length, axis=0) * jnp.fft.rfft(filter_taps.T, n=length, axis=0)
    mixed = jnp.fft.irfft(spectrum, n=length, axis=0)[:SEQ]
    hyena_out = (out_gate.astype(jnp.float32) * mixed).astype(jnp.bfloat16)
    return (attn_out, hyena_out)
```

```python
import math

import jax
import jax.numpy as jnp
import numpy as np
from jax import lax
from jax.experimental import pallas as pl
from jax.experimental.pallas import tpu as pltpu
from jax.sharding import PartitionSpec as P

HEAD_DIM = 128
KV_REACH = 3
BLOCK = 256


masked_score = -1e30


def passed_along(x, axis, by):
    length = lax.axis_size(axis)
    pairs = [(i, i + by) for i in range(length) if 0 <= i + by < length]
    return lax.ppermute(x, axis, pairs)


def doc_of(positions, doc_lengths):
    order = jnp.arange(doc_lengths.shape[0], dtype=jnp.int32)
    before = order[None, :] < order[:, None]
    starts = jnp.sum(jnp.where(before, doc_lengths[None, :], 0), axis=1)
    inside = (starts[None, :] <= positions[:, None]).astype(jnp.int32)
    return jnp.sum(inside, axis=1) - 1


def attend_block(carried, pair, query_heads, allowed):
    running_max, running_sum, weighted = carried
    row_count = query_heads.shape[0]
    key_heads = pair[0].reshape(row_count, -1, HEAD_DIM)
    value_heads = pair[1].reshape(row_count, -1, HEAD_DIM)
    scores = jnp.einsum(
        "qhd,khd->hqk", query_heads, key_heads, preferred_element_type=jnp.float32
    ) / math.sqrt(HEAD_DIM)
    scores = jnp.where(allowed[None], scores, masked_score)
    new_max = jnp.maximum(running_max, jnp.max(scores, axis=2))
    rescale = jnp.exp(running_max - new_max)
    exp_scores = jnp.exp(scores - new_max[:, :, None])
    running_sum = running_sum * rescale + jnp.sum(exp_scores, axis=2)
    weighted = weighted * rescale[:, :, None] + jnp.einsum(
        "hqk,khd->hqd",
        exp_scores.astype(jnp.bfloat16),
        value_heads,
        preferred_element_type=jnp.float32,
    )
    return (new_max, running_sum, weighted)


def split_parts(source):
    high_part = lax.optimization_barrier(source.astype(jnp.bfloat16))
    low_part = (source - high_part.astype(jnp.float32)).astype(jnp.bfloat16)
    return (high_part, low_part)


def split_mul(form, left_parts, right_parts):
    first = jnp.einsum(form, left_parts[0], right_parts[0], preferred_element_type=jnp.float32)
    second = jnp.einsum(form, left_parts[0], right_parts[1], preferred_element_type=jnp.float32)
    third = jnp.einsum(form, left_parts[1], right_parts[0], preferred_element_type=jnp.float32)
    return first + (second + third)


def dft_tables(length):
    inner_len = math.gcd(length, 256)
    outer_len = 2 * length // inner_len
    freq_rows = jnp.arange(outer_len, dtype=jnp.int32)
    time_rows = jnp.arange(outer_len // 2, dtype=jnp.int32)
    inner_index = jnp.arange(inner_len, dtype=jnp.int32)
    angle_outer = (
        2.0
        * math.pi
        / outer_len
        * (freq_rows[:, None] * time_rows[None, :] % outer_len).astype(jnp.float32)
    )
    angle_twist = (
        2.0
        * math.pi
        / (2 * length)
        * (freq_rows[:, None] * inner_index[None, :] % (2 * length)).astype(jnp.float32)
    )
    angle_inner = (
        2.0
        * math.pi
        / inner_len
        * (inner_index[:, None] * inner_index[None, :] % inner_len).astype(jnp.float32)
    )
    return (
        split_parts(jnp.cos(angle_outer)),
        split_parts(-jnp.sin(angle_outer)),
        jnp.cos(angle_twist),
        -jnp.sin(angle_twist),
        split_parts(jnp.cos(angle_inner)),
        split_parts(-jnp.sin(angle_inner)),
    )


def right_mul(left_parts, table_parts):
    return split_mul("cin,nm->cim", left_parts, table_parts)


def forward_dft(samples, tables):
    outer_cos, outer_sin, twist_cos, twist_sin, inner_cos, inner_sin = tables
    item_count = samples.shape[0]
    shaped = split_parts(samples.reshape(item_count, outer_cos[0].shape[1], inner_cos[0].shape[0]))
    section_real = split_mul("ij,cjn->cin", outer_cos, shaped)
    section_imag = split_mul("ij,cjn->cin", outer_sin, shaped)
    turned_real = split_parts(section_real * twist_cos - section_imag * twist_sin)
    turned_imag = split_parts(section_real * twist_sin + section_imag * twist_cos)
    spec_real = right_mul(turned_real, inner_cos) - right_mul(turned_imag, inner_sin)
    spec_imag = right_mul(turned_real, inner_sin) + right_mul(turned_imag, inner_cos)
    return (spec_real, spec_imag)


def inverse_dft(prod_real, prod_imag, tables):
    outer_cos, outer_sin, twist_cos, twist_sin, inner_cos, inner_sin = tables
    item_count = prod_real.shape[0]
    half_len = outer_cos[0].shape[1]
    inner_len = inner_cos[0].shape[0]
    real_parts = split_parts(prod_real)
    imag_parts = split_parts(prod_imag)
    back_real = right_mul(real_parts, inner_cos) + right_mul(imag_parts, inner_sin)
    back_imag = right_mul(imag_parts, inner_cos) - right_mul(real_parts, inner_sin)
    unturn_real = split_parts(back_real * twist_cos + back_imag * twist_sin)
    unturn_imag = split_parts(back_imag * twist_cos - back_real * twist_sin)
    rows_out = split_mul("ij,cin->cjn", outer_cos, unturn_real) + split_mul(
        "ij,cin->cjn", outer_sin, unturn_imag
    )
    return (rows_out * (1.0 / (2 * half_len * inner_len))).reshape(item_count, half_len * inner_len)


def filter_apply(signal, filter_spec, tables):
    sig_real, sig_imag = forward_dft(signal, tables)
    tap_real, tap_imag = filter_spec
    prod_real = sig_real * tap_real - sig_imag * tap_imag
    prod_imag = sig_real * tap_imag + sig_imag * tap_real
    return inverse_dft(prod_real, prod_imag, tables)


def body(queries, key_rows, values, doc_lengths, in_gate, out_gate, filter_taps):
    row_count, channels = queries.shape
    head_count = channels // HEAD_DIM
    group_count = lax.axis_size("ctx")
    per_group = channels // group_count
    seq_len = row_count * group_count
    tables = dft_tables(seq_len)
    taps_grouped = filter_taps.reshape(group_count, per_group, row_count)
    query_pos = lax.axis_index("ctx") * row_count + jnp.arange(row_count, dtype=jnp.int32)
    query_doc = doc_of(query_pos, doc_lengths)
    query_heads = queries.reshape(row_count, head_count, HEAD_DIM)
    carried = (
        jnp.full((head_count, row_count), masked_score, jnp.float32),
        jnp.zeros((head_count, row_count), jnp.float32),
        jnp.zeros((head_count, row_count, HEAD_DIM), jnp.float32),
    )

    def visit(state_now, pair, distance):
        key_pos = query_pos - distance * row_count
        key_doc = doc_of(key_pos, doc_lengths)
        allowed = (key_doc[None, :] == query_doc[:, None]) & (
            key_pos[None, :] <= query_pos[:, None]
        )
        return lax.cond(
            jnp.any(allowed),
            lambda state_in: attend_block(state_in, pair, query_heads, allowed),
            lambda state_in: state_in,
            state_now,
        )

    own_pair = jnp.stack((key_rows, values))
    carried = visit(carried, own_pair, 0)
    moving = own_pair
    for distance in range(1, KV_REACH + 1):
        moving = passed_along(moving, "ctx", 1)
        carried = visit(carried, moving, distance)
    running_max, running_sum, weighted = carried
    attended = (
        (weighted / running_sum[:, :, None])
        .transpose(1, 0, 2)
        .reshape(row_count, channels)
        .astype(jnp.bfloat16)
    )
    gated = (in_gate.astype(jnp.float32) * attended.astype(jnp.float32)).T
    gated_grouped = gated.reshape(group_count, per_group, row_count)
    pair = (
        lax.all_to_all(
            gated_grouped.astype(jnp.bfloat16), "ctx", split_axis=0, concat_axis=2, tiled=True
        ).astype(gated_grouped.dtype),
        lax.all_to_all(
            taps_grouped.astype(jnp.bfloat16), "ctx", split_axis=0, concat_axis=2, tiled=True
        ).astype(taps_grouped.dtype),
    )
    item_count = pair[0].shape[1]
    signal = pair[0].reshape(item_count, -1)
    taps = pair[1].reshape(item_count, -1)
    result = filter_apply(signal, forward_dft(taps, tables), tables)
    mixed = result.reshape(1, item_count, -1)
    returned = lax.all_to_all(
        mixed.astype(jnp.bfloat16), "ctx", split_axis=2, concat_axis=0, tiled=True
    ).astype(mixed.dtype)
    hyena_out = (out_gate.astype(jnp.float32) * returned.reshape(channels, row_count).T).astype(
        jnp.bfloat16
    )
    return (attended, hyena_out)


def block_tables(block):
    freq = np.arange(block)
    time = np.arange(block)
    angle = np.pi / (2 * block) * ((2 * freq[:, None] + 1) * time[None, :] % (4 * block))
    forward = np.concatenate((np.cos(angle), -np.sin(angle)), axis=0)
    inverse = forward.T / block
    return (jnp.asarray(forward, jnp.bfloat16), jnp.asarray(inverse, jnp.bfloat16))


def only_when(condition, action):
    @pl.when(condition)
    def _():
        action()


def fused_kernel(
    docs_ref,
    query_ref,
    key_ref,
    value_ref,
    gate_ref,
    taps_ref,
    forward_ref,
    inverse_ref,
    attn_ref,
    mixed_back,
    own_query,
    own_key,
    own_value,
    own_gate,
    prev_key,
    prev_value,
    far_query,
    far_out,
    far_stat,
    low_out,
    low_stat,
    own_out,
    own_top,
    own_sum,
    attn_buf,
    gated_buf,
    wide_taps,
    half_taps,
    forward_buf,
    inverse_buf,
    all_gate,
    all_taps,
    score_buf,
    sig_spec,
    tap_spec,
    prod_spec,
    mixed_buf,
    send_sem,
    recv_sem,
    local_sem,
):
    rows, channels = query_ref.shape
    length = all_gate.shape[0]
    groups = length // rows
    width = channels // groups
    heads = groups
    half = groups // 2
    block = inverse_ref.shape[0]
    blocks = length // block
    per_row = rows // block
    me = lax.axis_index("ctx")
    low = me < half
    high = me >= half
    second = half - 1
    odd = lax.rem(me, 2) == 1
    scale = math.log2(math.e) / math.sqrt(HEAD_DIM)

    def rows_of(group):
        return pl.ds(pl.multiple_of(group * rows, rows), rows)

    def cols_of(head):
        return pl.ds(pl.multiple_of(head * width, width), width)

    def home_of(head):
        return second + head // 2

    barrier = pltpu.get_barrier_semaphore()
    for step in range(1, groups):
        peer = lax.rem(me + step, groups)
        pl.semaphore_signal(
            barrier, inc=1, device_id={"ctx": peer}, device_id_type=pl.DeviceIdType.MESH
        )
    pl.semaphore_wait(barrier, groups - 1)

    def remote(kind, head, place, source, target, device):
        return pltpu.make_async_remote_copy(
            src_ref=source,
            dst_ref=target,
            send_sem=send_sem.at[kind, head, place],
            recv_sem=recv_sem.at[kind, head, place],
            device_id={"ctx": device},
            device_id_type=pl.DeviceIdType.MESH,
        )

    following = lax.rem(me + 1, groups)

    def key_copy(head):
        cols = cols_of(head)
        return remote(0, head, 0, key_ref.at[:, cols], prev_key.at[:, cols], following)

    def value_copy(head):
        cols = cols_of(head)
        return remote(1, head, 0, value_ref.at[:, cols], prev_value.at[:, cols], following)

    def query_copy(head, which):
        cols = cols_of(head)
        return remote(
            2, head, half + which, query_ref.at[:, cols], far_query.at[which, :, cols], second
        )

    def taps_refs(head, group):
        return (
            half_taps.at[cols_of(head), :],
            all_taps.at[cols_of(head % 2), rows_of(group)],
        )

    def gated_refs(head, group):
        return (
            gated_buf.at[:, cols_of(head)],
            all_gate.at[rows_of(group), cols_of(head % 2)],
        )

    def mixed_refs(head, group):
        return (
            mixed_buf.at[rows_of(group), cols_of(head % 2)],
            mixed_back.at[:, cols_of(head)],
        )

    refs_of = {3: taps_refs, 4: gated_refs, 7: mixed_refs}

    def hop(kind, head, group, device):
        return remote(kind, head, group, *refs_of[kind](head, group), device)

    def stay(kind, head, group):
        return pltpu.make_async_copy(
            *refs_of[kind](head, group), recv_sem.at[kind, head, group]
        )

    def send_home(kind, head):
        home = home_of(head)
        only_when(me != home, lambda: hop(kind, head, me, home).start())
        only_when(me == home, lambda: stay(kind, head, me).start())

    def wait_home(kind, head):
        for group in range(groups):
            only_when(me != group, lambda: hop(kind, head, group, second).wait_recv())
            only_when(me == group, lambda: stay(kind, head, group).wait())

    def out_copy(head, which):
        cols = cols_of(head)
        return remote(
            5, head, half + which, far_out.at[which, :, cols], low_out.at[:, cols], half + which
        )

    def stat_copy(head, which):
        return remote(
            6, head, half + which, far_stat.at[which, head], low_stat.at[head], half + which
        )

    taps_in = pltpu.make_async_copy(taps_ref, wide_taps, local_sem.at[4])
    taps_in.start()

    @pl.when(me == half)
    def _():
        for head in range(heads):
            query_copy(head, 0).start()

    @pl.when(me == groups - 1)
    def _():
        query_copy(0, 1).start()

    @pl.when(jnp.logical_not(odd))
    def _():
        key_copy(0).start()
        value_copy(0).start()

    loads = []
    for place, (source, target) in enumerate(
        (
            (query_ref, own_query),
            (key_ref, own_key),
            (value_ref, own_value),
            (gate_ref, own_gate),
        )
    ):
        loads.append(pltpu.make_async_copy(source, target, local_sem.at[place]))
    loads.append(pltpu.make_async_copy(forward_ref, forward_buf, local_sem.at[5]))
    loads.append(pltpu.make_async_copy(inverse_ref, inverse_buf, local_sem.at[6]))
    for load in loads:
        load.start()
    taps_in.wait()

    def round_body(at, carry):
        part = pl.ds(pl.multiple_of(at * 64, 64), 64)
        half_taps[part, :] = wide_taps[part, :].astype(jnp.bfloat16)
        return carry

    lax.fori_loop(0, half_taps.shape[0] // 64, round_body, 0)

    @pl.when(me == 0)
    def _():
        send_home(3, 2)
        key_copy(1).start()
        value_copy(1).start()
        send_home(3, 3)
        for head in range(2, heads):
            key_copy(head).start()
            value_copy(head).start()
        send_home(3, 0)
        send_home(3, 1)

    @pl.when(me == second)
    def _():
        for head in (2, 3, 0, 1):
            send_home(3, head)

    @pl.when(me == half)
    def _():
        for head in range(1, heads):
            key_copy(head).start()
            value_copy(head).start()
        for head in (0, 1, 2, 3):
            send_home(3, head)

    @pl.when(me == groups - 1)
    def _():
        for head in (2, 3):
            send_home(3, head)

    for load in loads:
        load.wait()

    starts = []
    total = 0
    for doc in range(docs_ref.shape[0]):
        starts.append(total)
        total = total + docs_ref[doc]

    def attend(query, first_pos, chunks):
        row_pos = lax.broadcasted_iota(jnp.int32, (block, width), 0) + first_pos
        row_start = jnp.zeros((block, width), jnp.int32)
        for start in starts:
            row_start = jnp.where(row_pos >= start, start, row_start)
        row_pos = row_pos[:, :1]
        row_start = row_start[:, :1]
        lane_pos = lax.broadcasted_iota(jnp.int32, (block, rows), 1)
        top = jnp.full((block, width), masked_score, jnp.float32)
        for place, (key, _, base, causal) in enumerate(chunks):
            scores = lax.dot_general(
                query,
                key,
                (((1,), (1,)), ((), ())),
                preferred_element_type=jnp.float32,
            )
            allowed = lane_pos >= row_start - base
            if causal:
                allowed = allowed & (lane_pos <= row_pos - base)
            scores = jnp.where(allowed, scores, masked_score)
            score_buf[place] = scores
            for part in range(0, rows, width):
                top = jnp.maximum(top, scores[:, part : part + width])
        top = jnp.max(top, axis=1, keepdims=True)
        running = jnp.zeros((block, width), jnp.float32)
        weighted = jnp.zeros((block, width), jnp.float32)
        for place, (_, value, _, _) in enumerate(chunks):
            weight = jnp.exp2((score_buf[place] - top) * scale)
            for part in range(0, rows, width):
                running = running + weight[:, part : part + width]
            weighted = weighted + jnp.dot(
                weight.astype(jnp.bfloat16), value, preferred_element_type=jnp.float32
            )
        return (top * scale, jnp.sum(running, axis=1, keepdims=True), weighted)

    diagonal = lax.broadcasted_iota(jnp.int32, (width, width), 0) == lax.broadcasted_iota(
        jnp.int32, (width, width), 1
    )

    def as_rows(column):
        at_row = lax.broadcasted_iota(jnp.int32, (8, width), 0)
        packed = jnp.zeros((8, width), jnp.float32)
        for piece in range(block // width):
            spread = jnp.where(diagonal, column[piece * width : (piece + 1) * width, :], 0.0)
            packed = jnp.where(at_row == piece, jnp.sum(spread, axis=0, keepdims=True), packed)
        return packed

    def as_column(packed):
        pieces = []
        for piece in range(block // width):
            spread = jnp.where(diagonal, packed[piece : piece + 1, :], 0.0)
            pieces.append(jnp.sum(spread, axis=1, keepdims=True))
        return jnp.concatenate(pieces, axis=0)

    def part_of(at):
        return pl.ds(pl.multiple_of(at * block, block), block)

    def far_tiles(head):
        cols = cols_of(head)

        def which_body(turn, carry):
            which = 1 - turn
            query_copy(head, which).wait_recv()

            def tile_body(at, carry):
                part = part_of(at)
                top, total_weight, weighted = attend(
                    far_query[which, part, cols],
                    (half + which) * rows + at * block,
                    (
                        (prev_key[:, cols], prev_value[:, cols], 0, False),
                        (own_key[:, cols], own_value[:, cols], rows, False),
                    ),
                )
                far_out[which, part, cols] = (weighted / total_weight).astype(jnp.bfloat16)
                far_stat[which, head, at] = as_rows(
                    top + jnp.log(total_weight) * math.log2(math.e)
                )
                return carry

            lax.fori_loop(0, per_row, tile_body, 0)
            out_copy(head, which).start()
            stat_copy(head, which).start()
            return carry

        lax.fori_loop(0, groups - half, which_body, 0)

    def own_tiles(head, with_prev):
        cols = cols_of(head)

        def tile_body(at, carry):
            part = part_of(at)
            chunks = ((own_key[:, cols], own_value[:, cols], me * rows, True),)
            if with_prev:
                chunks = (
                    (prev_key[:, cols], prev_value[:, cols], (me - 1) * rows, False),
                ) + chunks
            top, total_weight, weighted = attend(
                own_query[part, cols], me * rows + at * block, chunks
            )
            own_out[part, cols] = weighted
            own_top[head, part, :] = jnp.broadcast_to(top, (block, width))
            own_sum[head, part, :] = jnp.broadcast_to(total_weight, (block, width))
            return carry

        lax.fori_loop(0, per_row, tile_body, 0)

    def finish(head, merged):
        cols = cols_of(head)

        def tile_body(at, carry):
            part = part_of(at)
            weighted = own_out[part, cols]
            total_weight = own_sum[head, part, :]
            if merged:
                own_level = own_top[head, part, :]
                low_level = jnp.broadcast_to(as_column(low_stat[head, at]), (block, width))
                level = jnp.maximum(own_level, low_level)
                own_share = jnp.exp2(own_level - level)
                low_share = jnp.exp2(low_level - level)
                total_weight = total_weight * own_share + low_share
                weighted = weighted * own_share + low_share * low_out[part, cols].astype(
                    jnp.float32
                )
            attended = (weighted / total_weight).astype(jnp.bfloat16)
            attn_buf[part, cols] = attended
            gated_buf[part, cols] = (
                own_gate[part, cols].astype(jnp.float32) * attended.astype(jnp.float32)
            ).astype(jnp.bfloat16)
            return carry

        lax.fori_loop(0, per_row, tile_body, 0)
        send_home(4, head)

    def head_body(head, carry):
        @pl.when(odd)
        def _():
            key_copy(head).wait_recv()
            value_copy(head).wait_recv()

        @pl.when((me == groups - 1) & (head < heads - 1))
        def _():
            query_copy(head + 1, 1).start()

        only_when(me == second, lambda: far_tiles(head))
        only_when(odd, lambda: own_tiles(head, True))
        only_when(jnp.logical_not(odd), lambda: own_tiles(head, False))
        only_when(low, lambda: finish(head, False))
        return carry

    lax.fori_loop(0, heads, head_body, 0)

    @pl.when(me == groups - 1)
    def _():
        for head in (0, 1):
            send_home(3, head)

    def merge_body(head, carry):
        out_copy(head, me - half).wait_recv()
        stat_copy(head, me - half).wait_recv()
        finish(head, True)
        return carry

    only_when(high, lambda: lax.fori_loop(0, heads, merge_body, 0))

    attn_done = pltpu.make_async_copy(attn_buf, attn_ref, local_sem.at[7])
    attn_done.start()

    lift = 8

    def convolve(lane, carry):
        head = (me - second) * 2 + lane
        cols = cols_of(lane)
        wait_home(3, head)

        def tap_body(at, carry):
            tap_spec[at] = lax.dot_general(
                forward_buf[...],
                all_taps[cols, part_of(at)],
                (((1,), (1,)), ((), ())),
                preferred_element_type=jnp.float32,
            )
            return carry

        lax.fori_loop(0, blocks, tap_body, 0)
        wait_home(4, head)

        def signal_body(at, carry):
            sig_spec[at] = jnp.dot(
                forward_buf[...], all_gate[part_of(at), cols], preferred_element_type=jnp.float32
            )
            return carry

        lax.fori_loop(0, blocks, signal_body, 0)

        def product_body(at, carry):
            real = pl.ds(pl.multiple_of(at * lift, lift), lift)
            imag = pl.ds(pl.multiple_of(block + at * lift, lift), lift)
            uneven = lax.rem(lax.broadcasted_iota(jnp.int32, (lift, width), 0), 2) == 1
            sign = jnp.where(uneven, -1.0, 1.0).astype(jnp.float32)
            tap_real = []
            tap_imag = []
            for k in range(blocks):
                now_real = tap_spec[k, real, :]
                now_imag = tap_spec[k, imag, :]
                if k > 0:
                    now_real = now_real - sign * tap_spec[k - 1, imag, :]
                    now_imag = now_imag + sign * tap_spec[k - 1, real, :]
                tap_real.append(now_real)
                tap_imag.append(now_imag)
            for out in range(blocks):
                sum_real = jnp.zeros((lift, width), jnp.float32)
                sum_imag = jnp.zeros((lift, width), jnp.float32)
                for j in range(out + 1):
                    sig_real = sig_spec[j, real, :]
                    sig_imag = sig_spec[j, imag, :]
                    sum_real = (
                        sum_real + sig_real * tap_real[out - j] - sig_imag * tap_imag[out - j]
                    )
                    sum_imag = (
                        sum_imag + sig_real * tap_imag[out - j] + sig_imag * tap_real[out - j]
                    )
                prod_spec[out, real, :] = sum_real
                prod_spec[out, imag, :] = sum_imag
            return carry

        lax.fori_loop(0, block // lift, product_body, 0)

        def group_body(turn, carry):
            group = groups - 1 - turn

            def inverse_body(at, carry):
                index = group * per_row + at
                mixed_buf[part_of(index), cols] = jnp.dot(
                    inverse_buf[...],
                    prod_spec[index].astype(jnp.bfloat16),
                    preferred_element_type=jnp.float32,
                ).astype(jnp.bfloat16)
                return carry

            lax.fori_loop(0, per_row, inverse_body, 0)
            only_when(me != group, lambda: hop(7, head, group, group).start())
            only_when(me == group, lambda: stay(7, head, group).start())
            return carry

        lax.fori_loop(0, groups, group_body, 0)
        return carry

    is_home = (me == second) | (me == half)
    only_when(is_home, lambda: lax.fori_loop(0, 2, convolve, 0))

    for head in range(heads):
        home = home_of(head)
        only_when(me != home, lambda: hop(7, head, me, home).wait_recv())
        only_when(me == home, lambda: stay(7, head, me).wait())
    attn_done.wait()

    for head in range(heads):
        home = home_of(head)

        @pl.when(jnp.logical_not(odd))
        def _():
            key_copy(head).wait_send()
            value_copy(head).wait_send()

        only_when(high, lambda: query_copy(head, me - half).wait_send())

        @pl.when(me != home)
        def _():
            hop(3, head, me, home).wait_send()
            hop(4, head, me, home).wait_send()

        for which in range(groups - half):

            @pl.when(me == second)
            def _():
                out_copy(head, which).wait_send()
                stat_copy(head, which).wait_send()

        for group in range(groups):
            if group != home:
                only_when(me == home, lambda: hop(7, head, group, group).wait_send())


def fused_body(queries, key_rows, values, doc_lengths, in_gate, out_gate, filter_taps):
    rows, channels = queries.shape
    groups = lax.axis_size("ctx")
    width = channels // groups
    length = rows * groups
    block = BLOCK
    blocks = length // block
    per_row = rows // block
    heads = groups
    half_groups = groups // 2
    forward, inverse = block_tables(block)
    anywhere = pl.BlockSpec(memory_space=pl.ANY)
    half = jnp.bfloat16
    full = jnp.float32
    flat = (rows, channels)
    attended, mixed = pl.pallas_call(
        fused_kernel,
        out_shape=(
            jax.ShapeDtypeStruct(flat, half),
            jax.ShapeDtypeStruct(flat, half),
        ),
        in_specs=[pl.BlockSpec(memory_space=pltpu.SMEM)] + [anywhere] * 7,
        out_specs=(anywhere, anywhere),
        scratch_shapes=[
            pltpu.VMEM(flat, half),
            pltpu.VMEM(flat, half),
            pltpu.VMEM(flat, half),
            pltpu.VMEM(flat, half),
            pltpu.VMEM(flat, half),
            pltpu.VMEM(flat, half),
            pltpu.VMEM((half_groups,) + flat, half),
            pltpu.VMEM((half_groups,) + flat, half),
            pltpu.VMEM((half_groups, heads, per_row, 8, width), full),
            pltpu.VMEM(flat, half),
            pltpu.VMEM((heads, per_row, 8, width), full),
            pltpu.VMEM(flat, full),
            pltpu.VMEM((heads, rows, width), full),
            pltpu.VMEM((heads, rows, width), full),
            pltpu.VMEM(flat, half),
            pltpu.VMEM(flat, half),
            pltpu.VMEM(filter_taps.shape, full),
            pltpu.VMEM(filter_taps.shape, half),
            pltpu.VMEM(forward.shape, half),
            pltpu.VMEM(inverse.shape, half),
            pltpu.VMEM((length, 2 * width), half),
            pltpu.VMEM((2 * width, length), half),
            pltpu.VMEM((2, block, rows), full),
            pltpu.VMEM((blocks, 2 * block, width), full),
            pltpu.VMEM((blocks, 2 * block, width), full),
            pltpu.VMEM((blocks, 2 * block, width), full),
            pltpu.VMEM((length, 2 * width), half),
            pltpu.SemaphoreType.DMA((8, heads, groups)),
            pltpu.SemaphoreType.DMA((8, heads, groups)),
            pltpu.SemaphoreType.DMA((8,)),
        ],
        compiler_params=pltpu.CompilerParams(
            collective_id=0, has_side_effects=True, vmem_limit_bytes=67043328
        ),
        name="fused_window",
    )(
        doc_lengths,
        queries,
        key_rows,
        values,
        in_gate,
        filter_taps,
        forward,
        inverse,
    )
    hyena_out = (out_gate.astype(full) * mixed.astype(full)).astype(half)
    return (attended, hyena_out)


def fits_fused(queries):
    rows, channels = queries.shape
    groups = lax.axis_size("ctx")
    return groups == 4 and channels == groups * HEAD_DIM and rows % BLOCK == 0


def either_body(queries, *rest):
    if fits_fused(queries):
        return fused_body(queries, *rest)
    return body(queries, *rest)


def solution(mesh):
    return jax.shard_map(
        either_body,
        mesh=mesh,
        in_specs=(
            P(("dp", "ctx"), "tp"),
            P(("dp", "ctx"), "tp"),
            P(("dp", "ctx"), "tp"),
            P("dp"),
            P(("dp", "ctx"), "tp"),
            P(("dp", "ctx"), "tp"),
            P(("dp", "tp"), "ctx"),
        ),
        out_specs=(P(("dp", "ctx"), "tp"), P(("dp", "ctx"), "tp")),
        check_vma=False,
    )
```

```python
import math

import jax
import jax.numpy as jnp
import numpy as np
from jax import lax
from jax.experimental import pallas as pl
from jax.experimental.pallas import tpu as pltpu
from jax.sharding import PartitionSpec as P

HEAD_DIM = 128
KV_REACH = 3
BLOCK = 256


masked_score = -1e30


def passed_along(x, axis, by):
    length = lax.axis_size(axis)
    pairs = [(i, i + by) for i in range(length) if 0 <= i + by < length]
    return lax.ppermute(x, axis, pairs)


def doc_of(positions, doc_lengths):
    order = jnp.arange(doc_lengths.shape[0], dtype=jnp.int32)
    before = order[None, :] < order[:, None]
    starts = jnp.sum(jnp.where(before, doc_lengths[None, :], 0), axis=1)
    inside = (starts[None, :] <= positions[:, None]).astype(jnp.int32)
    return jnp.sum(inside, axis=1) - 1


def attend_block(carried, pair, query_heads, allowed):
    running_max, running_sum, weighted = carried
    row_count = query_heads.shape[0]
    key_heads = pair[0].reshape(row_count, -1, HEAD_DIM)
    value_heads = pair[1].reshape(row_count, -1, HEAD_DIM)
    scores = jnp.einsum(
        "qhd,khd->hqk", query_heads, key_heads, preferred_element_type=jnp.float32
    ) / math.sqrt(HEAD_DIM)
    scores = jnp.where(allowed[None], scores, masked_score)
    new_max = jnp.maximum(running_max, jnp.max(scores, axis=2))
    rescale = jnp.exp(running_max - new_max)
    exp_scores = jnp.exp(scores - new_max[:, :, None])
    running_sum = running_sum * rescale + jnp.sum(exp_scores, axis=2)
    weighted = weighted * rescale[:, :, None] + jnp.einsum(
        "hqk,khd->hqd",
        exp_scores.astype(jnp.bfloat16),
        value_heads,
        preferred_element_type=jnp.float32,
    )
    return (new_max, running_sum, weighted)


def split_parts(source):
    high_part = lax.optimization_barrier(source.astype(jnp.bfloat16))
    low_part = (source - high_part.astype(jnp.float32)).astype(jnp.bfloat16)
    return (high_part, low_part)


def split_mul(form, left_parts, right_parts):
    first = jnp.einsum(form, left_parts[0], right_parts[0], preferred_element_type=jnp.float32)
    second = jnp.einsum(form, left_parts[0], right_parts[1], preferred_element_type=jnp.float32)
    third = jnp.einsum(form, left_parts[1], right_parts[0], preferred_element_type=jnp.float32)
    return first + (second + third)


def dft_tables(length):
    inner_len = math.gcd(length, 256)
    outer_len = 2 * length // inner_len
    freq_rows = jnp.arange(outer_len, dtype=jnp.int32)
    time_rows = jnp.arange(outer_len // 2, dtype=jnp.int32)
    inner_index = jnp.arange(inner_len, dtype=jnp.int32)
    angle_outer = (
        2.0
        * math.pi
        / outer_len
        * (freq_rows[:, None] * time_rows[None, :] % outer_len).astype(jnp.float32)
    )
    angle_twist = (
        2.0
        * math.pi
        / (2 * length)
        * (freq_rows[:, None] * inner_index[None, :] % (2 * length)).astype(jnp.float32)
    )
    angle_inner = (
        2.0
        * math.pi
        / inner_len
        * (inner_index[:, None] * inner_index[None, :] % inner_len).astype(jnp.float32)
    )
    return (
        split_parts(jnp.cos(angle_outer)),
        split_parts(-jnp.sin(angle_outer)),
        jnp.cos(angle_twist),
        -jnp.sin(angle_twist),
        split_parts(jnp.cos(angle_inner)),
        split_parts(-jnp.sin(angle_inner)),
    )


def right_mul(left_parts, table_parts):
    return split_mul("cin,nm->cim", left_parts, table_parts)


def forward_dft(samples, tables):
    outer_cos, outer_sin, twist_cos, twist_sin, inner_cos, inner_sin = tables
    item_count = samples.shape[0]
    shaped = split_parts(samples.reshape(item_count, outer_cos[0].shape[1], inner_cos[0].shape[0]))
    section_real = split_mul("ij,cjn->cin", outer_cos, shaped)
    section_imag = split_mul("ij,cjn->cin", outer_sin, shaped)
    turned_real = split_parts(section_real * twist_cos - section_imag * twist_sin)
    turned_imag = split_parts(section_real * twist_sin + section_imag * twist_cos)
    spec_real = right_mul(turned_real, inner_cos) - right_mul(turned_imag, inner_sin)
    spec_imag = right_mul(turned_real, inner_sin) + right_mul(turned_imag, inner_cos)
    return (spec_real, spec_imag)


def inverse_dft(prod_real, prod_imag, tables):
    outer_cos, outer_sin, twist_cos, twist_sin, inner_cos, inner_sin = tables
    item_count = prod_real.shape[0]
    half_len = outer_cos[0].shape[1]
    inner_len = inner_cos[0].shape[0]
    real_parts = split_parts(prod_real)
    imag_parts = split_parts(prod_imag)
    back_real = right_mul(real_parts, inner_cos) + right_mul(imag_parts, inner_sin)
    back_imag = right_mul(imag_parts, inner_cos) - right_mul(real_parts, inner_sin)
    unturn_real = split_parts(back_real * twist_cos + back_imag * twist_sin)
    unturn_imag = split_parts(back_imag * twist_cos - back_real * twist_sin)
    rows_out = split_mul("ij,cin->cjn", outer_cos, unturn_real) + split_mul(
        "ij,cin->cjn", outer_sin, unturn_imag
    )
    return (rows_out * (1.0 / (2 * half_len * inner_len))).reshape(item_count, half_len * inner_len)


def filter_apply(signal, filter_spec, tables):
    sig_real, sig_imag = forward_dft(signal, tables)
    tap_real, tap_imag = filter_spec
    prod_real = sig_real * tap_real - sig_imag * tap_imag
    prod_imag = sig_real * tap_imag + sig_imag * tap_real
    return inverse_dft(prod_real, prod_imag, tables)


def body(queries, key_rows, values, doc_lengths, in_gate, out_gate, filter_taps):
    row_count, channels = queries.shape
    head_count = channels // HEAD_DIM
    group_count = lax.axis_size("ctx")
    per_group = channels // group_count
    seq_len = row_count * group_count
    tables = dft_tables(seq_len)
    taps_grouped = filter_taps.reshape(group_count, per_group, row_count)
    query_pos = lax.axis_index("ctx") * row_count + jnp.arange(row_count, dtype=jnp.int32)
    query_doc = doc_of(query_pos, doc_lengths)
    query_heads = queries.reshape(row_count, head_count, HEAD_DIM)
    carried = (
        jnp.full((head_count, row_count), masked_score, jnp.float32),
        jnp.zeros((head_count, row_count), jnp.float32),
        jnp.zeros((head_count, row_count, HEAD_DIM), jnp.float32),
    )

    def visit(state_now, pair, distance):
        key_pos = query_pos - distance * row_count
        key_doc = doc_of(key_pos, doc_lengths)
        allowed = (key_doc[None, :] == query_doc[:, None]) & (
            key_pos[None, :] <= query_pos[:, None]
        )
        return lax.cond(
            jnp.any(allowed),
            lambda state_in: attend_block(state_in, pair, query_heads, allowed),
            lambda state_in: state_in,
            state_now,
        )

    own_pair = jnp.stack((key_rows, values))
    carried = visit(carried, own_pair, 0)
    moving = own_pair
    for distance in range(1, KV_REACH + 1):
        moving = passed_along(moving, "ctx", 1)
        carried = visit(carried, moving, distance)
    running_max, running_sum, weighted = carried
    attended = (
        (weighted / running_sum[:, :, None])
        .transpose(1, 0, 2)
        .reshape(row_count, channels)
        .astype(jnp.bfloat16)
    )
    gated = (in_gate.astype(jnp.float32) * attended.astype(jnp.float32)).T
    gated_grouped = gated.reshape(group_count, per_group, row_count)
    pair = (
        lax.all_to_all(
            gated_grouped.astype(jnp.bfloat16), "ctx", split_axis=0, concat_axis=2, tiled=True
        ).astype(gated_grouped.dtype),
        lax.all_to_all(
            taps_grouped.astype(jnp.bfloat16), "ctx", split_axis=0, concat_axis=2, tiled=True
        ).astype(taps_grouped.dtype),
    )
    item_count = pair[0].shape[1]
    signal = pair[0].reshape(item_count, -1)
    taps = pair[1].reshape(item_count, -1)
    result = filter_apply(signal, forward_dft(taps, tables), tables)
    mixed = result.reshape(1, item_count, -1)
    returned = lax.all_to_all(
        mixed.astype(jnp.bfloat16), "ctx", split_axis=2, concat_axis=0, tiled=True
    ).astype(mixed.dtype)
    hyena_out = (out_gate.astype(jnp.float32) * returned.reshape(channels, row_count).T).astype(
        jnp.bfloat16
    )
    return (attended, hyena_out)


def block_tables(block):
    freq = np.arange(block)
    time = np.arange(block)
    angle = np.pi / (2 * block) * ((2 * freq[:, None] + 1) * time[None, :] % (4 * block))
    forward = np.concatenate((np.cos(angle), -np.sin(angle)), axis=0)
    inverse = forward.T / block
    return (jnp.asarray(forward, jnp.bfloat16), jnp.asarray(inverse, jnp.bfloat16))


def only_when(condition, action):
    @pl.when(condition)
    def _():
        action()


def fused_kernel(
    docs_ref,
    query_ref,
    key_ref,
    value_ref,
    gate_ref,
    last_ref,
    taps_ref,
    forward_ref,
    inverse_ref,
    attn_ref,
    hyena_ref,
    own_query,
    own_key,
    own_value,
    own_gate,
    final_gate,
    prev_key,
    prev_value,
    far_query,
    far_out,
    far_stat,
    low_out,
    low_stat,
    own_out,
    own_top,
    own_sum,
    row_starts,
    attn_buf,
    gated_buf,
    wide_taps,
    half_taps,
    forward_buf,
    inverse_buf,
    all_gate,
    all_taps,
    score_buf,
    sig_spec,
    tap_spec,
    prod_spec,
    mixed_buf,
    mixed_back,
    hyena_buf,
    send_sem,
    recv_sem,
    local_sem,
    result_sem,
):
    rows, channels = query_ref.shape
    length = all_gate.shape[0]
    groups = length // rows
    width = channels // groups
    heads = groups
    half = groups // 2
    block = inverse_ref.shape[0]
    blocks = length // block
    per_row = rows // block
    me = lax.axis_index("ctx")
    low = me < half
    high = me >= half
    second = half - 1
    odd = lax.rem(me, 2) == 1
    scale = math.log2(math.e) / math.sqrt(HEAD_DIM)

    def rows_of(group):
        return pl.ds(pl.multiple_of(group * rows, rows), rows)

    def cols_of(head):
        return pl.ds(pl.multiple_of(head * width, width), width)

    def home_of(head):
        return second + head // 2

    def part_of(at):
        return pl.ds(pl.multiple_of(at * block, block), block)

    barrier = pltpu.get_barrier_semaphore()
    for step in range(1, groups):
        peer = lax.rem(me + step, groups)
        pl.semaphore_signal(
            barrier, inc=1, device_id={"ctx": peer}, device_id_type=pl.DeviceIdType.MESH
        )
    pl.semaphore_wait(barrier, groups - 1)

    def remote(kind, head, place, source, target, device):
        return pltpu.make_async_remote_copy(
            src_ref=source,
            dst_ref=target,
            send_sem=send_sem.at[kind, head, place],
            recv_sem=recv_sem.at[kind, head, place],
            device_id={"ctx": device},
            device_id_type=pl.DeviceIdType.MESH,
        )

    following = lax.rem(me + 1, groups)

    def key_copy(head):
        cols = cols_of(head)
        return remote(0, head, 0, key_ref.at[:, cols], prev_key.at[:, cols], following)

    def value_copy(head):
        cols = cols_of(head)
        return remote(1, head, 0, value_ref.at[:, cols], prev_value.at[:, cols], following)

    def query_copy(head, which):
        cols = cols_of(head)
        return remote(
            2, head, half + which, query_ref.at[:, cols], far_query.at[which, :, cols], second
        )

    def taps_refs(head, group):
        return (
            half_taps.at[cols_of(head), :],
            all_taps.at[cols_of(head % 2), rows_of(group)],
        )

    def gated_refs(head, group):
        return (
            gated_buf.at[:, cols_of(head)],
            all_gate.at[rows_of(group), cols_of(head % 2)],
        )

    def mixed_refs(head, group):
        return (
            mixed_buf.at[rows_of(group), cols_of(head % 2)],
            mixed_back.at[:, cols_of(head)],
        )

    refs_of = {3: taps_refs, 4: gated_refs, 7: mixed_refs}

    def hop(kind, head, group, device):
        return remote(kind, head, group, *refs_of[kind](head, group), device)

    def stay(kind, head, group):
        return pltpu.make_async_copy(
            *refs_of[kind](head, group), recv_sem.at[kind, head, group]
        )

    def send_home(kind, head):
        home = home_of(head)
        only_when(me != home, lambda: hop(kind, head, me, home).start())
        only_when(me == home, lambda: stay(kind, head, me).start())

    def wait_home(kind, head):
        for group in range(groups):
            only_when(me != group, lambda: hop(kind, head, group, second).wait_recv())
            only_when(me == group, lambda: stay(kind, head, group).wait())

    def out_copy(head, which):
        cols = cols_of(head)
        return remote(
            5, head, half + which, far_out.at[which, :, cols], low_out.at[:, cols], half + which
        )

    def stat_copy(head, which):
        return remote(
            6, head, half + which, far_stat.at[which, head], low_stat.at[head], half + which
        )

    taps_in = pltpu.make_async_copy(taps_ref, wide_taps, local_sem.at[4])
    taps_in.start()

    @pl.when(me == half)
    def _():
        for head in range(heads):
            query_copy(head, 0).start()

    @pl.when(me == groups - 1)
    def _():
        query_copy(0, 1).start()

    @pl.when(jnp.logical_not(odd))
    def _():
        key_copy(0).start()
        value_copy(0).start()

    loads = []
    for place, (source, target) in enumerate(
        (
            (query_ref, own_query),
            (key_ref, own_key),
            (value_ref, own_value),
            (gate_ref, own_gate),
        )
    ):
        loads.append(pltpu.make_async_copy(source, target, local_sem.at[place]))
    loads.append(pltpu.make_async_copy(last_ref, final_gate, local_sem.at[8]))
    loads.append(pltpu.make_async_copy(forward_ref, forward_buf, local_sem.at[5]))
    loads.append(pltpu.make_async_copy(inverse_ref, inverse_buf, local_sem.at[6]))
    for load in loads:
        load.start()
    taps_in.wait()

    def round_body(at, carry):
        part = pl.ds(pl.multiple_of(at * 64, 64), 64)
        half_taps[part, :] = wide_taps[part, :].astype(jnp.bfloat16)
        return carry

    lax.fori_loop(0, half_taps.shape[0] // 64, round_body, 0)

    @pl.when(me == 0)
    def _():
        send_home(3, 2)
        key_copy(1).start()
        value_copy(1).start()
        send_home(3, 3)
        for head in range(2, heads):
            key_copy(head).start()
            value_copy(head).start()
        send_home(3, 0)
        send_home(3, 1)

    @pl.when(me == second)
    def _():
        for head in (2, 3, 0, 1):
            send_home(3, head)

    @pl.when(me == half)
    def _():
        for head in range(1, heads):
            key_copy(head).start()
            value_copy(head).start()
        for head in (0, 1, 2, 3):
            send_home(3, head)

    @pl.when(me == groups - 1)
    def _():
        for head in (2, 3):
            send_home(3, head)

    for load in loads:
        load.wait()

    starts = []
    total = 0
    wide_end = 0
    wide_start = 0
    for doc in range(docs_ref.shape[0]):
        starts.append(total)
        begun = total <= rows
        wide_start = jnp.where(begun, total, wide_start)
        total = total + docs_ref[doc]
        wide_end = jnp.where(begun, total, wide_end)

    def start_body(at, carry):
        row_pos = lax.broadcasted_iota(jnp.int32, (block, width), 0) + (me * rows + at * block)
        row_start = jnp.zeros((block, width), jnp.int32)
        for start in starts:
            row_start = jnp.where(row_pos >= start, start, row_start)
        row_starts[part_of(at), :] = row_start
        return carry

    lax.fori_loop(0, per_row, start_body, 0)
    lane_of = lax.broadcasted_iota(jnp.int32, (block, width), 1)
    row_of = lax.broadcasted_iota(jnp.int32, (block, width), 0)

    def attend(slot, query, chunks):
        top = jnp.full((block, width), masked_score, jnp.float32)
        for place, (key, _, mask) in enumerate(chunks):
            scores = lax.dot_general(
                query,
                key,
                (((1,), (1,)), ((), ())),
                preferred_element_type=jnp.float32,
            )
            for first in range(0, key.shape[0], width):
                piece = mask(scores[:, first : first + width], first)
                score_buf[slot, place, :, first : first + width] = piece
                top = jnp.maximum(top, piece)
        top = jnp.max(top, axis=1, keepdims=True)
        running = jnp.zeros((block, width), jnp.float32)
        weighted = jnp.zeros((block, width), jnp.float32)
        for place, (key, value, _) in enumerate(chunks):
            count = key.shape[0]
            weight = jnp.exp2((score_buf[slot, place, :, :count] - top) * scale)
            for first in range(0, count, width):
                running = running + weight[:, first : first + width]
            weighted = weighted + jnp.dot(
                weight.astype(jnp.bfloat16), value, preferred_element_type=jnp.float32
            )
        return (top * scale, jnp.sum(running, axis=1, keepdims=True), weighted)

    diagonal = lax.broadcasted_iota(jnp.int32, (width, width), 0) == lax.broadcasted_iota(
        jnp.int32, (width, width), 1
    )

    def as_rows(column):
        at_row = lax.broadcasted_iota(jnp.int32, (8, width), 0)
        packed = jnp.zeros((8, width), jnp.float32)
        for piece in range(block // width):
            spread = jnp.where(diagonal, column[piece * width : (piece + 1) * width, :], 0.0)
            packed = jnp.where(at_row == piece, jnp.sum(spread, axis=0, keepdims=True), packed)
        return packed

    def as_column(packed):
        pieces = []
        for piece in range(block // width):
            spread = jnp.where(diagonal, packed[piece : piece + 1, :], 0.0)
            pieces.append(jnp.sum(spread, axis=1, keepdims=True))
        return jnp.concatenate(pieces, axis=0)

    def far_tiles(head):
        cols = cols_of(head)
        first_lane = lax.broadcasted_iota(jnp.int32, (1, rows), 1)
        outside = jnp.where(first_lane >= wide_start, 0.0, masked_score)

        def first_mask(scores, first):
            return scores + outside[:, first : first + width]

        def no_mask(scores, first):
            return scores

        def which_body(turn, carry):
            which = 1 - turn
            query_copy(head, which).wait_recv()
            for at in range(per_row):
                part = pl.ds(at * block, block)
                top, total_weight, weighted = attend(
                    at,
                    far_query[which, part, cols],
                    (
                        (prev_key[:, cols], prev_value[:, cols], first_mask),
                        (own_key[:, cols], own_value[:, cols], no_mask),
                    ),
                )
                far_out[which, part, cols] = (weighted / total_weight).astype(jnp.bfloat16)
                level = top + jnp.log(total_weight) * math.log2(math.e)
                inside = row_of[:, :1] + ((half + which) * rows + at * block) < wide_end
                far_stat[which, head, at] = as_rows(jnp.where(inside, level, masked_score))
            out_copy(head, which).start()
            stat_copy(head, which).start()
            return carry

        lax.fori_loop(0, groups - half, which_body, 0)

    def own_tiles(head, with_prev):
        cols = cols_of(head)
        for at in range(per_row):
            part = pl.ds(at * block, block)
            row_start = row_starts[part, :]
            count = (at + 1) * block

            def own_mask(scores, first, at=at, row_start=row_start):
                allowed = lane_of >= row_start - (me * rows + first)
                if first >= at * block:
                    allowed = allowed & (lane_of <= row_of - (first - at * block))
                return jnp.where(allowed, scores, masked_score)

            def prev_mask(scores, first, row_start=row_start):
                allowed = lane_of >= row_start - ((me - 1) * rows + first)
                return jnp.where(allowed, scores, masked_score)

            chunks = ((own_key[:count, cols], own_value[:count, cols], own_mask),)
            if with_prev:
                chunks = ((prev_key[:, cols], prev_value[:, cols], prev_mask),) + chunks
            top, total_weight, weighted = attend(at, own_query[part, cols], chunks)
            own_out[part, cols] = weighted
            own_top[head, part, :] = jnp.broadcast_to(top, (block, width))
            own_sum[head, part, :] = jnp.broadcast_to(total_weight, (block, width))

    def finish(head, merged):
        cols = cols_of(head)
        for at in range(per_row):
            part = pl.ds(at * block, block)
            weighted = own_out[part, cols]
            total_weight = own_sum[head, part, :]
            if merged:
                own_level = own_top[head, part, :]
                low_level = jnp.broadcast_to(as_column(low_stat[head, at]), (block, width))
                level = jnp.maximum(own_level, low_level)
                own_share = jnp.exp2(own_level - level)
                low_share = jnp.exp2(low_level - level)
                total_weight = total_weight * own_share + low_share
                weighted = weighted * own_share + low_share * low_out[part, cols].astype(
                    jnp.float32
                )
            attended = (weighted / total_weight).astype(jnp.bfloat16)
            attn_buf[part, cols] = attended
            gated_buf[part, cols] = (
                own_gate[part, cols].astype(jnp.float32) * attended.astype(jnp.float32)
            ).astype(jnp.bfloat16)
        send_home(4, head)

    def head_body(head, carry):
        @pl.when(odd)
        def _():
            key_copy(head).wait_recv()
            value_copy(head).wait_recv()

        @pl.when((me == groups - 1) & (head < heads - 1))
        def _():
            query_copy(head + 1, 1).start()

        only_when(me == second, lambda: far_tiles(head))
        only_when(odd, lambda: own_tiles(head, True))
        only_when(jnp.logical_not(odd), lambda: own_tiles(head, False))
        only_when(low, lambda: finish(head, False))
        return carry

    lax.fori_loop(0, heads, head_body, 0)

    @pl.when(me == groups - 1)
    def _():
        for head in (0, 1):
            send_home(3, head)

    def merge_body(head, carry):
        out_copy(head, me - half).wait_recv()
        stat_copy(head, me - half).wait_recv()
        finish(head, True)
        return carry

    only_when(high, lambda: lax.fori_loop(0, heads, merge_body, 0))

    attn_done = pltpu.make_async_copy(attn_buf, attn_ref, local_sem.at[7])
    attn_done.start()

    lift = 8

    batch = 4

    def spectra(target, source_of):
        def body(turn, carry):
            for piece in range(batch):
                at = turn * batch + piece
                target[at] = source_of(at)
            return carry

        lax.fori_loop(0, blocks // batch, body, 0)

    def transform_taps():
        first = (me - second) * 2
        for lane in range(2):
            wait_home(3, first + lane)
        spectra(
            tap_spec,
            lambda at: lax.dot_general(
                forward_buf[...],
                all_taps[:, part_of(at)],
                (((1,), (1,)), ((), ())),
                preferred_element_type=jnp.float32,
            ),
        )

    def convolve(lane, carry):
        head = (me - second) * 2 + lane
        cols = cols_of(lane)
        wait_home(4, head)
        spectra(
            sig_spec,
            lambda at: jnp.dot(
                forward_buf[...], all_gate[part_of(at), cols], preferred_element_type=jnp.float32
            ),
        )

        def product_body(at, carry):
            real = pl.ds(pl.multiple_of(at * lift, lift), lift)
            imag = pl.ds(pl.multiple_of(block + at * lift, lift), lift)
            uneven = lax.rem(lax.broadcasted_iota(jnp.int32, (lift, width), 0), 2) == 1
            sign = jnp.where(uneven, -1.0, 1.0).astype(jnp.float32)
            tap_real = []
            tap_imag = []
            for k in range(blocks):
                now_real = tap_spec[k, real, cols]
                now_imag = tap_spec[k, imag, cols]
                if k > 0:
                    now_real = now_real - sign * tap_spec[k - 1, imag, cols]
                    now_imag = now_imag + sign * tap_spec[k - 1, real, cols]
                tap_real.append(now_real)
                tap_imag.append(now_imag)
            for out in range(blocks):
                sum_real = jnp.zeros((lift, width), jnp.float32)
                sum_imag = jnp.zeros((lift, width), jnp.float32)
                for j in range(out + 1):
                    sig_real = sig_spec[j, real, :]
                    sig_imag = sig_spec[j, imag, :]
                    sum_real = (
                        sum_real + sig_real * tap_real[out - j] - sig_imag * tap_imag[out - j]
                    )
                    sum_imag = (
                        sum_imag + sig_real * tap_imag[out - j] + sig_imag * tap_real[out - j]
                    )
                prod_spec[out, real, :] = sum_real
                prod_spec[out, imag, :] = sum_imag
            return carry

        lax.fori_loop(0, block // lift, product_body, 0)

        def group_body(turn, carry):
            group = groups - 1 - turn

            for at in range(per_row):
                index = group * per_row + at
                mixed_buf[part_of(index), cols] = jnp.dot(
                    inverse_buf[...],
                    prod_spec[index].astype(jnp.bfloat16),
                    preferred_element_type=jnp.float32,
                ).astype(jnp.bfloat16)
            only_when(me != group, lambda: hop(7, head, group, group).start())
            only_when(me == group, lambda: stay(7, head, group).start())
            return carry

        lax.fori_loop(0, groups, group_body, 0)
        return carry

    is_home = (me == second) | (me == half)
    @pl.when(is_home)
    def _():
        transform_taps()
        lax.fori_loop(0, 2, convolve, 0)

    def result_copy(head):
        cols = cols_of(head)
        return pltpu.make_async_copy(
            hyena_buf.at[:, cols], hyena_ref.at[:, cols], result_sem.at[head]
        )

    for head in (0, 2, 1, 3):
        home = home_of(head)
        only_when(me != home, lambda: hop(7, head, me, home).wait_recv())
        only_when(me == home, lambda: stay(7, head, me).wait())
        for at in range(per_row):
            part = pl.ds(at * block, block)
            hyena_buf[part, cols_of(head)] = (
                final_gate[part, cols_of(head)].astype(jnp.float32)
                * mixed_back[part, cols_of(head)].astype(jnp.float32)
            ).astype(jnp.bfloat16)
        result_copy(head).start()
    for head in range(heads):
        result_copy(head).wait()
    attn_done.wait()

    for head in range(heads):
        home = home_of(head)

        @pl.when(jnp.logical_not(odd))
        def _():
            key_copy(head).wait_send()
            value_copy(head).wait_send()

        only_when(high, lambda: query_copy(head, me - half).wait_send())

        @pl.when(me != home)
        def _():
            hop(3, head, me, home).wait_send()
            hop(4, head, me, home).wait_send()

        for which in range(groups - half):

            @pl.when(me == second)
            def _():
                out_copy(head, which).wait_send()
                stat_copy(head, which).wait_send()

        for group in range(groups):
            if group != home:
                only_when(me == home, lambda: hop(7, head, group, group).wait_send())


def fused_body(queries, key_rows, values, doc_lengths, in_gate, out_gate, filter_taps):
    rows, channels = queries.shape
    groups = lax.axis_size("ctx")
    width = channels // groups
    length = rows * groups
    block = BLOCK
    blocks = length // block
    per_row = rows // block
    heads = groups
    half_groups = groups // 2
    forward, inverse = block_tables(block)
    anywhere = pl.BlockSpec(memory_space=pl.ANY)
    half = jnp.bfloat16
    full = jnp.float32
    flat = (rows, channels)
    return pl.pallas_call(
        fused_kernel,
        out_shape=(
            jax.ShapeDtypeStruct(flat, half),
            jax.ShapeDtypeStruct(flat, half),
        ),
        in_specs=[pl.BlockSpec(memory_space=pltpu.SMEM)] + [anywhere] * 8,
        out_specs=(anywhere, anywhere),
        scratch_shapes=[
            pltpu.VMEM(flat, half),
            pltpu.VMEM(flat, half),
            pltpu.VMEM(flat, half),
            pltpu.VMEM(flat, half),
            pltpu.VMEM(flat, half),
            pltpu.VMEM(flat, half),
            pltpu.VMEM(flat, half),
            pltpu.VMEM((half_groups,) + flat, half),
            pltpu.VMEM((half_groups,) + flat, half),
            pltpu.VMEM((half_groups, heads, per_row, 8, width), full),
            pltpu.VMEM(flat, half),
            pltpu.VMEM((heads, per_row, 8, width), full),
            pltpu.VMEM(flat, full),
            pltpu.VMEM((heads, rows, width), full),
            pltpu.VMEM((heads, rows, width), full),
            pltpu.VMEM((rows, width), jnp.int32),
            pltpu.VMEM(flat, half),
            pltpu.VMEM(flat, half),
            pltpu.VMEM(filter_taps.shape, full),
            pltpu.VMEM(filter_taps.shape, half),
            pltpu.VMEM(forward.shape, half),
            pltpu.VMEM(inverse.shape, half),
            pltpu.VMEM((length, 2 * width), half),
            pltpu.VMEM((2 * width, length), half),
            pltpu.VMEM((per_row, 2, block, rows), full),
            pltpu.VMEM((blocks, 2 * block, width), full),
            pltpu.VMEM((blocks, 2 * block, 2 * width), full),
            pltpu.VMEM((blocks, 2 * block, width), full),
            pltpu.VMEM((length, 2 * width), half),
            pltpu.VMEM(flat, half),
            pltpu.VMEM(flat, half),
            pltpu.SemaphoreType.DMA((8, heads, groups)),
            pltpu.SemaphoreType.DMA((8, heads, groups)),
            pltpu.SemaphoreType.DMA((9,)),
            pltpu.SemaphoreType.DMA((heads,)),
        ],
        compiler_params=pltpu.CompilerParams(
            collective_id=0, has_side_effects=True, vmem_limit_bytes=67043328
        ),
        name="fused_window",
    )(
        doc_lengths,
        queries,
        key_rows,
        values,
        in_gate,
        out_gate,
        filter_taps,
        forward,
        inverse,
    )


def fits_fused(queries):
    rows, channels = queries.shape
    groups = lax.axis_size("ctx")
    return groups == 4 and channels == groups * HEAD_DIM and rows % BLOCK == 0


def either_body(queries, *rest):
    if fits_fused(queries):
        return fused_body(queries, *rest)
    return body(queries, *rest)


def solution(mesh):
    return jax.shard_map(
        either_body,
        mesh=mesh,
        in_specs=(
            P(("dp", "ctx"), "tp"),
            P(("dp", "ctx"), "tp"),
            P(("dp", "ctx"), "tp"),
            P("dp"),
            P(("dp", "ctx"), "tp"),
            P(("dp", "ctx"), "tp"),
            P(("dp", "tp"), "ctx"),
        ),
        out_specs=(P(("dp", "ctx"), "tp"), P(("dp", "ctx"), "tp")),
        check_vma=False,
    )
```

```python
import math

import jax
import jax.numpy as jnp
import numpy as np
from jax import lax
from jax.experimental import pallas as pl
from jax.experimental.pallas import tpu as pltpu
from jax.sharding import PartitionSpec as P

HEAD_DIM = 128
KV_REACH = 3
BLOCK = 256


masked_score = -1e30


def passed_along(x, axis, by):
    length = lax.axis_size(axis)
    pairs = [(i, i + by) for i in range(length) if 0 <= i + by < length]
    return lax.ppermute(x, axis, pairs)


def doc_of(positions, doc_lengths):
    order = jnp.arange(doc_lengths.shape[0], dtype=jnp.int32)
    before = order[None, :] < order[:, None]
    starts = jnp.sum(jnp.where(before, doc_lengths[None, :], 0), axis=1)
    inside = (starts[None, :] <= positions[:, None]).astype(jnp.int32)
    return jnp.sum(inside, axis=1) - 1


def attend_block(carried, pair, query_heads, allowed):
    running_max, running_sum, weighted = carried
    row_count = query_heads.shape[0]
    key_heads = pair[0].reshape(row_count, -1, HEAD_DIM)
    value_heads = pair[1].reshape(row_count, -1, HEAD_DIM)
    scores = jnp.einsum(
        "qhd,khd->hqk", query_heads, key_heads, preferred_element_type=jnp.float32
    ) / math.sqrt(HEAD_DIM)
    scores = jnp.where(allowed[None], scores, masked_score)
    new_max = jnp.maximum(running_max, jnp.max(scores, axis=2))
    rescale = jnp.exp(running_max - new_max)
    exp_scores = jnp.exp(scores - new_max[:, :, None])
    running_sum = running_sum * rescale + jnp.sum(exp_scores, axis=2)
    weighted = weighted * rescale[:, :, None] + jnp.einsum(
        "hqk,khd->hqd",
        exp_scores.astype(jnp.bfloat16),
        value_heads,
        preferred_element_type=jnp.float32,
    )
    return (new_max, running_sum, weighted)


def split_parts(source):
    high_part = lax.optimization_barrier(source.astype(jnp.bfloat16))
    low_part = (source - high_part.astype(jnp.float32)).astype(jnp.bfloat16)
    return (high_part, low_part)


def split_mul(form, left_parts, right_parts):
    first = jnp.einsum(form, left_parts[0], right_parts[0], preferred_element_type=jnp.float32)
    second = jnp.einsum(form, left_parts[0], right_parts[1], preferred_element_type=jnp.float32)
    third = jnp.einsum(form, left_parts[1], right_parts[0], preferred_element_type=jnp.float32)
    return first + (second + third)


def dft_tables(length):
    inner_len = math.gcd(length, 256)
    outer_len = 2 * length // inner_len
    freq_rows = jnp.arange(outer_len, dtype=jnp.int32)
    time_rows = jnp.arange(outer_len // 2, dtype=jnp.int32)
    inner_index = jnp.arange(inner_len, dtype=jnp.int32)
    angle_outer = (
        2.0
        * math.pi
        / outer_len
        * (freq_rows[:, None] * time_rows[None, :] % outer_len).astype(jnp.float32)
    )
    angle_twist = (
        2.0
        * math.pi
        / (2 * length)
        * (freq_rows[:, None] * inner_index[None, :] % (2 * length)).astype(jnp.float32)
    )
    angle_inner = (
        2.0
        * math.pi
        / inner_len
        * (inner_index[:, None] * inner_index[None, :] % inner_len).astype(jnp.float32)
    )
    return (
        split_parts(jnp.cos(angle_outer)),
        split_parts(-jnp.sin(angle_outer)),
        jnp.cos(angle_twist),
        -jnp.sin(angle_twist),
        split_parts(jnp.cos(angle_inner)),
        split_parts(-jnp.sin(angle_inner)),
    )


def right_mul(left_parts, table_parts):
    return split_mul("cin,nm->cim", left_parts, table_parts)


def forward_dft(samples, tables):
    outer_cos, outer_sin, twist_cos, twist_sin, inner_cos, inner_sin = tables
    item_count = samples.shape[0]
    shaped = split_parts(samples.reshape(item_count, outer_cos[0].shape[1], inner_cos[0].shape[0]))
    section_real = split_mul("ij,cjn->cin", outer_cos, shaped)
    section_imag = split_mul("ij,cjn->cin", outer_sin, shaped)
    turned_real = split_parts(section_real * twist_cos - section_imag * twist_sin)
    turned_imag = split_parts(section_real * twist_sin + section_imag * twist_cos)
    spec_real = right_mul(turned_real, inner_cos) - right_mul(turned_imag, inner_sin)
    spec_imag = right_mul(turned_real, inner_sin) + right_mul(turned_imag, inner_cos)
    return (spec_real, spec_imag)


def inverse_dft(prod_real, prod_imag, tables):
    outer_cos, outer_sin, twist_cos, twist_sin, inner_cos, inner_sin = tables
    item_count = prod_real.shape[0]
    half_len = outer_cos[0].shape[1]
    inner_len = inner_cos[0].shape[0]
    real_parts = split_parts(prod_real)
    imag_parts = split_parts(prod_imag)
    back_real = right_mul(real_parts, inner_cos) + right_mul(imag_parts, inner_sin)
    back_imag = right_mul(imag_parts, inner_cos) - right_mul(real_parts, inner_sin)
    unturn_real = split_parts(back_real * twist_cos + back_imag * twist_sin)
    unturn_imag = split_parts(back_imag * twist_cos - back_real * twist_sin)
    rows_out = split_mul("ij,cin->cjn", outer_cos, unturn_real) + split_mul(
        "ij,cin->cjn", outer_sin, unturn_imag
    )
    return (rows_out * (1.0 / (2 * half_len * inner_len))).reshape(item_count, half_len * inner_len)


def filter_apply(signal, filter_spec, tables):
    sig_real, sig_imag = forward_dft(signal, tables)
    tap_real, tap_imag = filter_spec
    prod_real = sig_real * tap_real - sig_imag * tap_imag
    prod_imag = sig_real * tap_imag + sig_imag * tap_real
    return inverse_dft(prod_real, prod_imag, tables)


def body(queries, key_rows, values, doc_lengths, in_gate, out_gate, filter_taps):
    row_count, channels = queries.shape
    head_count = channels // HEAD_DIM
    group_count = lax.axis_size("ctx")
    per_group = channels // group_count
    seq_len = row_count * group_count
    tables = dft_tables(seq_len)
    taps_grouped = filter_taps.reshape(group_count, per_group, row_count)
    query_pos = lax.axis_index("ctx") * row_count + jnp.arange(row_count, dtype=jnp.int32)
    query_doc = doc_of(query_pos, doc_lengths)
    query_heads = queries.reshape(row_count, head_count, HEAD_DIM)
    carried = (
        jnp.full((head_count, row_count), masked_score, jnp.float32),
        jnp.zeros((head_count, row_count), jnp.float32),
        jnp.zeros((head_count, row_count, HEAD_DIM), jnp.float32),
    )

    def visit(state_now, pair, distance):
        key_pos = query_pos - distance * row_count
        key_doc = doc_of(key_pos, doc_lengths)
        allowed = (key_doc[None, :] == query_doc[:, None]) & (
            key_pos[None, :] <= query_pos[:, None]
        )
        return lax.cond(
            jnp.any(allowed),
            lambda state_in: attend_block(state_in, pair, query_heads, allowed),
            lambda state_in: state_in,
            state_now,
        )

    own_pair = jnp.stack((key_rows, values))
    carried = visit(carried, own_pair, 0)
    moving = own_pair
    for distance in range(1, KV_REACH + 1):
        moving = passed_along(moving, "ctx", 1)
        carried = visit(carried, moving, distance)
    running_max, running_sum, weighted = carried
    attended = (
        (weighted / running_sum[:, :, None])
        .transpose(1, 0, 2)
        .reshape(row_count, channels)
        .astype(jnp.bfloat16)
    )
    gated = (in_gate.astype(jnp.float32) * attended.astype(jnp.float32)).T
    gated_grouped = gated.reshape(group_count, per_group, row_count)
    pair = (
        lax.all_to_all(
            gated_grouped.astype(jnp.bfloat16), "ctx", split_axis=0, concat_axis=2, tiled=True
        ).astype(gated_grouped.dtype),
        lax.all_to_all(
            taps_grouped.astype(jnp.bfloat16), "ctx", split_axis=0, concat_axis=2, tiled=True
        ).astype(taps_grouped.dtype),
    )
    item_count = pair[0].shape[1]
    signal = pair[0].reshape(item_count, -1)
    taps = pair[1].reshape(item_count, -1)
    result = filter_apply(signal, forward_dft(taps, tables), tables)
    mixed = result.reshape(1, item_count, -1)
    returned = lax.all_to_all(
        mixed.astype(jnp.bfloat16), "ctx", split_axis=2, concat_axis=0, tiled=True
    ).astype(mixed.dtype)
    hyena_out = (out_gate.astype(jnp.float32) * returned.reshape(channels, row_count).T).astype(
        jnp.bfloat16
    )
    return (attended, hyena_out)


def block_tables(block):
    freq = np.arange(block)
    time = np.arange(block)
    angle = np.pi / (2 * block) * ((2 * freq[:, None] + 1) * time[None, :] % (4 * block))
    forward = np.concatenate((np.cos(angle), -np.sin(angle)), axis=0)
    inverse = forward.T / block
    return (jnp.asarray(forward, jnp.bfloat16), jnp.asarray(inverse, jnp.bfloat16))


def only_when(condition, action):
    @pl.when(condition)
    def _():
        action()


def fused_kernel(
    docs_ref,
    query_ref,
    key_ref,
    value_ref,
    gate_ref,
    last_ref,
    taps_ref,
    forward_ref,
    inverse_ref,
    attn_ref,
    hyena_ref,
    own_query,
    own_key,
    own_value,
    own_gate,
    final_gate,
    prev_key,
    prev_value,
    far_query,
    far_out,
    far_stat,
    low_out,
    low_stat,
    own_out,
    own_top,
    own_sum,
    row_starts,
    attn_buf,
    gated_buf,
    wide_taps,
    half_taps,
    forward_buf,
    inverse_buf,
    all_gate,
    all_taps,
    score_buf,
    sig_spec,
    tap_spec,
    prod_spec,
    mixed_buf,
    mixed_back,
    hyena_buf,
    send_sem,
    recv_sem,
    local_sem,
    result_sem,
    taps_sem,
):
    rows, channels = query_ref.shape
    length = all_gate.shape[0]
    groups = length // rows
    width = channels // groups
    heads = groups
    half = groups // 2
    block = inverse_ref.shape[0]
    blocks = length // block
    per_row = rows // block
    me = lax.axis_index("ctx")
    low = me < half
    high = me >= half
    second = half - 1
    odd = lax.rem(me, 2) == 1
    scale = math.log2(math.e) / math.sqrt(HEAD_DIM)

    def rows_of(group):
        return pl.ds(pl.multiple_of(group * rows, rows), rows)

    def cols_of(head):
        return pl.ds(pl.multiple_of(head * width, width), width)

    def home_of(head):
        return second + head // 2

    def part_of(at):
        return pl.ds(pl.multiple_of(at * block, block), block)

    barrier = pltpu.get_barrier_semaphore()
    for step in range(1, groups):
        peer = lax.rem(me + step, groups)
        pl.semaphore_signal(
            barrier, inc=1, device_id={"ctx": peer}, device_id_type=pl.DeviceIdType.MESH
        )
    pl.semaphore_wait(barrier, groups - 1)

    def remote(kind, head, place, source, target, device):
        return pltpu.make_async_remote_copy(
            src_ref=source,
            dst_ref=target,
            send_sem=send_sem.at[kind, head, place],
            recv_sem=recv_sem.at[kind, head, place],
            device_id={"ctx": device},
            device_id_type=pl.DeviceIdType.MESH,
        )

    following = lax.rem(me + 1, groups)

    def key_copy(head):
        cols = cols_of(head)
        return remote(0, head, 0, key_ref.at[:, cols], prev_key.at[:, cols], following)

    def value_copy(head):
        cols = cols_of(head)
        return remote(1, head, 0, value_ref.at[:, cols], prev_value.at[:, cols], following)

    def query_copy(head, which):
        cols = cols_of(head)
        return remote(
            2, head, half + which, query_ref.at[:, cols], far_query.at[which, :, cols], second
        )

    def taps_refs(head, group):
        return (
            half_taps.at[cols_of(head), :],
            all_taps.at[cols_of(head % 2), rows_of(group)],
        )

    def gated_refs(head, group):
        return (
            gated_buf.at[:, cols_of(head)],
            all_gate.at[rows_of(group), cols_of(head % 2)],
        )

    def mixed_refs(head, group):
        return (
            mixed_buf.at[rows_of(group), cols_of(head % 2)],
            mixed_back.at[:, cols_of(head)],
        )

    refs_of = {3: taps_refs, 4: gated_refs, 7: mixed_refs}

    def hop(kind, head, group, device):
        return remote(kind, head, group, *refs_of[kind](head, group), device)

    def stay(kind, head, group):
        return pltpu.make_async_copy(
            *refs_of[kind](head, group), recv_sem.at[kind, head, group]
        )

    def send_home(kind, head):
        home = home_of(head)
        only_when(me != home, lambda: hop(kind, head, me, home).start())
        only_when(me == home, lambda: stay(kind, head, me).start())

    def wait_home(kind, head):
        for group in range(groups):
            only_when(me != group, lambda: hop(kind, head, group, second).wait_recv())
            only_when(me == group, lambda: stay(kind, head, group).wait())

    def out_copy(head, which):
        cols = cols_of(head)
        return remote(
            5, head, half + which, far_out.at[which, :, cols], low_out.at[:, cols], half + which
        )

    def stat_copy(head, which):
        return remote(
            6, head, half + which, far_stat.at[which, head], low_stat.at[head], half + which
        )

    def pair_rows(pair):
        return pl.ds(pair * 2 * width, 2 * width)

    def taps_in(pair):
        return pltpu.make_async_copy(
            taps_ref.at[pair_rows(pair), :], wide_taps.at[pair_rows(pair), :], taps_sem.at[pair]
        )

    for pair in range(heads // 2 - 1, -1, -1):
        taps_in(pair).start()

    @pl.when(me == half)
    def _():
        for head in range(heads):
            query_copy(head, 0).start()

    @pl.when(me == groups - 1)
    def _():
        query_copy(0, 1).start()

    @pl.when(jnp.logical_not(odd))
    def _():
        key_copy(0).start()
        value_copy(0).start()

    loads = []
    for place, (source, target) in enumerate(
        (
            (query_ref, own_query),
            (key_ref, own_key),
            (value_ref, own_value),
            (gate_ref, own_gate),
        )
    ):
        loads.append(pltpu.make_async_copy(source, target, local_sem.at[place]))
    loads.append(pltpu.make_async_copy(last_ref, final_gate, local_sem.at[8]))
    loads.append(pltpu.make_async_copy(forward_ref, forward_buf, local_sem.at[5]))
    loads.append(pltpu.make_async_copy(inverse_ref, inverse_buf, local_sem.at[6]))
    for load in loads:
        load.start()

    def round_taps(pair):
        taps_in(pair).wait()

        def round_body(at, carry):
            part = pl.ds(pl.multiple_of(pair * 2 * width + at * 64, 64), 64)
            half_taps[part, :] = wide_taps[part, :].astype(jnp.bfloat16)
            return carry

        lax.fori_loop(0, 2 * width // 64, round_body, 0)

    round_taps(1)

    @pl.when(me == 0)
    def _():
        send_home(3, 2)
        key_copy(1).start()
        value_copy(1).start()
        send_home(3, 3)
        for head in range(2, heads):
            key_copy(head).start()
            value_copy(head).start()

    @pl.when(me == second)
    def _():
        for head in (2, 3):
            send_home(3, head)

    round_taps(0)

    @pl.when(me <= second)
    def _():
        for head in (0, 1):
            send_home(3, head)

    @pl.when(me == half)
    def _():
        for head in range(1, heads):
            key_copy(head).start()
            value_copy(head).start()
        for head in (0, 1, 2, 3):
            send_home(3, head)

    @pl.when(me == groups - 1)
    def _():
        for head in (2, 3):
            send_home(3, head)

    for load in loads:
        load.wait()

    starts = []
    total = 0
    wide_end = 0
    wide_start = 0
    for doc in range(docs_ref.shape[0]):
        starts.append(total)
        begun = total <= rows
        wide_start = jnp.where(begun, total, wide_start)
        total = total + docs_ref[doc]
        wide_end = jnp.where(begun, total, wide_end)

    def start_body(at, carry):
        row_pos = lax.broadcasted_iota(jnp.int32, (block, width), 0) + (me * rows + at * block)
        row_start = jnp.zeros((block, width), jnp.int32)
        for start in starts:
            row_start = jnp.where(row_pos >= start, start, row_start)
        row_starts[part_of(at), :] = row_start
        return carry

    lax.fori_loop(0, per_row, start_body, 0)
    lane_of = lax.broadcasted_iota(jnp.int32, (block, width), 1)
    row_of = lax.broadcasted_iota(jnp.int32, (block, width), 0)

    def attend(slot, query, chunks):
        top = jnp.full((block, width), masked_score, jnp.float32)
        for place, (key, _, mask) in enumerate(chunks):
            scores = lax.dot_general(
                query,
                key,
                (((1,), (1,)), ((), ())),
                preferred_element_type=jnp.float32,
            )
            for first in range(0, key.shape[0], width):
                piece = mask(scores[:, first : first + width], first)
                score_buf[slot, place, :, first : first + width] = piece
                top = jnp.maximum(top, piece)
        top = jnp.max(top, axis=1, keepdims=True)
        running = jnp.zeros((block, width), jnp.float32)
        weighted = jnp.zeros((block, width), jnp.float32)
        for place, (key, value, _) in enumerate(chunks):
            count = key.shape[0]
            weight = jnp.exp2((score_buf[slot, place, :, :count] - top) * scale)
            for first in range(0, count, width):
                running = running + weight[:, first : first + width]
            weighted = weighted + jnp.dot(
                weight.astype(jnp.bfloat16), value, preferred_element_type=jnp.float32
            )
        return (top * scale, jnp.sum(running, axis=1, keepdims=True), weighted)

    diagonal = lax.broadcasted_iota(jnp.int32, (width, width), 0) == lax.broadcasted_iota(
        jnp.int32, (width, width), 1
    )

    def as_rows(column):
        at_row = lax.broadcasted_iota(jnp.int32, (8, width), 0)
        packed = jnp.zeros((8, width), jnp.float32)
        for piece in range(block // width):
            spread = jnp.where(diagonal, column[piece * width : (piece + 1) * width, :], 0.0)
            packed = jnp.where(at_row == piece, jnp.sum(spread, axis=0, keepdims=True), packed)
        return packed

    def as_column(packed):
        pieces = []
        for piece in range(block // width):
            spread = jnp.where(diagonal, packed[piece : piece + 1, :], 0.0)
            pieces.append(jnp.sum(spread, axis=1, keepdims=True))
        return jnp.concatenate(pieces, axis=0)

    def far_tiles(head):
        cols = cols_of(head)
        first_lane = lax.broadcasted_iota(jnp.int32, (1, rows), 1)
        outside = jnp.where(first_lane >= wide_start, 0.0, masked_score)

        def first_mask(scores, first):
            return scores + outside[:, first : first + width]

        def no_mask(scores, first):
            return scores

        def which_body(turn, carry):
            which = 1 - turn
            query_copy(head, which).wait_recv()
            for at in range(per_row):
                part = pl.ds(at * block, block)
                top, total_weight, weighted = attend(
                    at,
                    far_query[which, part, cols],
                    (
                        (prev_key[:, cols], prev_value[:, cols], first_mask),
                        (own_key[:, cols], own_value[:, cols], no_mask),
                    ),
                )
                far_out[which, part, cols] = (weighted / total_weight).astype(jnp.bfloat16)
                level = top + jnp.log(total_weight) * math.log2(math.e)
                inside = row_of[:, :1] + ((half + which) * rows + at * block) < wide_end
                far_stat[which, head, at] = as_rows(jnp.where(inside, level, masked_score))
            out_copy(head, which).start()
            stat_copy(head, which).start()
            return carry

        lax.fori_loop(0, groups - half, which_body, 0)

    def own_tiles(head, with_prev):
        cols = cols_of(head)
        for at in range(per_row):
            part = pl.ds(at * block, block)
            row_start = row_starts[part, :]
            count = (at + 1) * block

            def own_mask(scores, first, at=at, row_start=row_start):
                allowed = lane_of >= row_start - (me * rows + first)
                if first >= at * block:
                    allowed = allowed & (lane_of <= row_of - (first - at * block))
                return jnp.where(allowed, scores, masked_score)

            def prev_mask(scores, first, row_start=row_start):
                allowed = lane_of >= row_start - ((me - 1) * rows + first)
                return jnp.where(allowed, scores, masked_score)

            chunks = ((own_key[:count, cols], own_value[:count, cols], own_mask),)
            if with_prev:
                chunks = ((prev_key[:, cols], prev_value[:, cols], prev_mask),) + chunks
            top, total_weight, weighted = attend(at, own_query[part, cols], chunks)
            own_out[part, cols] = weighted
            own_top[head, part, :] = jnp.broadcast_to(top, (block, width))
            own_sum[head, part, :] = jnp.broadcast_to(total_weight, (block, width))

    def finish(head, merged):
        cols = cols_of(head)
        for at in range(per_row):
            part = pl.ds(at * block, block)
            weighted = own_out[part, cols]
            total_weight = own_sum[head, part, :]
            if merged:
                own_level = own_top[head, part, :]
                low_level = jnp.broadcast_to(as_column(low_stat[head, at]), (block, width))
                level = jnp.maximum(own_level, low_level)
                own_share = jnp.exp2(own_level - level)
                low_share = jnp.exp2(low_level - level)
                total_weight = total_weight * own_share + low_share
                weighted = weighted * own_share + low_share * low_out[part, cols].astype(
                    jnp.float32
                )
            attended = (weighted / total_weight).astype(jnp.bfloat16)
            attn_buf[part, cols] = attended
            gated_buf[part, cols] = (
                own_gate[part, cols].astype(jnp.float32) * attended.astype(jnp.float32)
            ).astype(jnp.bfloat16)
        send_home(4, head)

    def head_body(head, carry):
        @pl.when(odd)
        def _():
            key_copy(head).wait_recv()
            value_copy(head).wait_recv()

        @pl.when((me == groups - 1) & (head < heads - 1))
        def _():
            query_copy(head + 1, 1).start()

        only_when(me == second, lambda: far_tiles(head))
        only_when(odd, lambda: own_tiles(head, True))
        only_when(jnp.logical_not(odd), lambda: own_tiles(head, False))
        only_when(low, lambda: finish(head, False))
        return carry

    lax.fori_loop(0, heads, head_body, 0)

    @pl.when(me == groups - 1)
    def _():
        for head in (0, 1):
            send_home(3, head)

    def merge_body(head, carry):
        out_copy(head, me - half).wait_recv()
        stat_copy(head, me - half).wait_recv()
        finish(head, True)
        return carry

    only_when(high, lambda: lax.fori_loop(0, heads, merge_body, 0))

    attn_done = pltpu.make_async_copy(attn_buf, attn_ref, local_sem.at[7])
    attn_done.start()

    lift = 8

    batch = 4

    def spectra(target, count, source_of):
        def body(turn, carry):
            for piece in range(batch):
                at = turn * batch + piece
                target[at] = source_of(at)
            return carry

        if count % batch:
            for at in range(count):
                target[at] = source_of(at)
        else:
            lax.fori_loop(0, count // batch, body, 0)

    def tap_blocks(count, source_of):
        spectra(
            tap_spec,
            count,
            lambda at: lax.dot_general(
                forward_buf[...],
                source_of(at),
                (((1,), (1,)), ((), ())),
                preferred_element_type=jnp.float32,
            ),
        )

    def signal_blocks(count, source_of):
        spectra(
            sig_spec,
            count,
            lambda at: jnp.dot(
                forward_buf[...], source_of(at), preferred_element_type=jnp.float32
            ),
        )

    def products(cols, first, count):
        def product_body(at, carry):
            real = pl.ds(pl.multiple_of(at * lift, lift), lift)
            imag = pl.ds(pl.multiple_of(block + at * lift, lift), lift)
            uneven = lax.rem(lax.broadcasted_iota(jnp.int32, (lift, width), 0), 2) == 1
            sign = jnp.where(uneven, -1.0, 1.0).astype(jnp.float32)
            tap_real = []
            tap_imag = []
            for k in range(count):
                now_real = tap_spec[k, real, cols]
                now_imag = tap_spec[k, imag, cols]
                if k > 0:
                    now_real = now_real - sign * tap_spec[k - 1, imag, cols]
                    now_imag = now_imag + sign * tap_spec[k - 1, real, cols]
                tap_real.append(now_real)
                tap_imag.append(now_imag)
            for out in range(first, count):
                sum_real = jnp.zeros((lift, width), jnp.float32)
                sum_imag = jnp.zeros((lift, width), jnp.float32)
                for j in range(out + 1):
                    sig_real = sig_spec[j, real, :]
                    sig_imag = sig_spec[j, imag, :]
                    sum_real = (
                        sum_real + sig_real * tap_real[out - j] - sig_imag * tap_imag[out - j]
                    )
                    sum_imag = (
                        sum_imag + sig_real * tap_imag[out - j] + sig_imag * tap_real[out - j]
                    )
                prod_spec[out, real, :] = sum_real
                prod_spec[out, imag, :] = sum_imag
            return carry

        lax.fori_loop(0, block // lift, product_body, 0)

    def mixed_block(index):
        return jnp.dot(
            inverse_buf[...],
            prod_spec[index].astype(jnp.bfloat16),
            preferred_element_type=jnp.float32,
        ).astype(jnp.bfloat16)

    def convolve(lane, carry):
        head = (me - second) * 2 + lane
        cols = cols_of(lane)
        wait_home(4, head)
        signal_blocks(blocks, lambda at: all_gate[part_of(at), cols])
        products(cols, per_row, blocks)

        def group_body(turn, carry):
            group = groups - 1 - turn
            for at in range(per_row):
                index = group * per_row + at
                mixed_buf[part_of(index), cols] = mixed_block(index)
            only_when(me != group, lambda: hop(7, head, group, group).start())
            only_when(me == group, lambda: stay(7, head, group).start())
            return carry

        lax.fori_loop(0, groups - 1, group_body, 0)
        return carry

    is_home = (me == second) | (me == half)

    @pl.when(is_home)
    def _():
        first = (me - second) * 2
        for lane in range(2):
            wait_home(3, first + lane)
        tap_blocks(blocks, lambda at: all_taps[:, part_of(at)])
        lax.fori_loop(0, 2, convolve, 0)

    @pl.when(me == 0)
    def _():
        def pair_body(pair, carry):
            channels_of = pl.ds(pl.multiple_of(pair * 2 * width, 2 * width), 2 * width)
            tap_blocks(per_row, lambda at: half_taps[channels_of, at * block : (at + 1) * block])

            def lane_body(lane, carry):
                cols = cols_of(pair * 2 + lane)
                signal_blocks(
                    per_row, lambda at: gated_buf[at * block : (at + 1) * block, cols]
                )
                products(cols_of(lane), 0, per_row)
                for at in range(per_row):
                    mixed_back[at * block : (at + 1) * block, cols] = mixed_block(at)
                return carry

            lax.fori_loop(0, 2, lane_body, 0)
            return carry

        lax.fori_loop(0, heads // 2, pair_body, 0)

    def result_copy(head):
        cols = cols_of(head)
        return pltpu.make_async_copy(
            hyena_buf.at[:, cols], hyena_ref.at[:, cols], result_sem.at[head]
        )

    for head in (0, 2, 1, 3):
        home = home_of(head)
        only_when((me != home) & (me != 0), lambda: hop(7, head, me, home).wait_recv())
        only_when(me == home, lambda: stay(7, head, me).wait())
        for at in range(per_row):
            part = pl.ds(at * block, block)
            hyena_buf[part, cols_of(head)] = (
                final_gate[part, cols_of(head)].astype(jnp.float32)
                * mixed_back[part, cols_of(head)].astype(jnp.float32)
            ).astype(jnp.bfloat16)
        result_copy(head).start()
    for head in range(heads):
        result_copy(head).wait()
    attn_done.wait()

    for head in range(heads):
        home = home_of(head)

        @pl.when(jnp.logical_not(odd))
        def _():
            key_copy(head).wait_send()
            value_copy(head).wait_send()

        only_when(high, lambda: query_copy(head, me - half).wait_send())

        @pl.when(me != home)
        def _():
            hop(3, head, me, home).wait_send()
            hop(4, head, me, home).wait_send()

        for which in range(groups - half):

            @pl.when(me == second)
            def _():
                out_copy(head, which).wait_send()
                stat_copy(head, which).wait_send()

        for group in range(1, groups):
            if group != home:
                only_when(me == home, lambda: hop(7, head, group, group).wait_send())


def fused_body(queries, key_rows, values, doc_lengths, in_gate, out_gate, filter_taps):
    rows, channels = queries.shape
    groups = lax.axis_size("ctx")
    width = channels // groups
    length = rows * groups
    block = BLOCK
    blocks = length // block
    per_row = rows // block
    heads = groups
    half_groups = groups // 2
    forward, inverse = block_tables(block)
    anywhere = pl.BlockSpec(memory_space=pl.ANY)
    half = jnp.bfloat16
    full = jnp.float32
    flat = (rows, channels)
    return pl.pallas_call(
        fused_kernel,
        out_shape=(
            jax.ShapeDtypeStruct(flat, half),
            jax.ShapeDtypeStruct(flat, half),
        ),
        in_specs=[pl.BlockSpec(memory_space=pltpu.SMEM)] + [anywhere] * 8,
        out_specs=(anywhere, anywhere),
        scratch_shapes=[
            pltpu.VMEM(flat, half),
            pltpu.VMEM(flat, half),
            pltpu.VMEM(flat, half),
            pltpu.VMEM(flat, half),
            pltpu.VMEM(flat, half),
            pltpu.VMEM(flat, half),
            pltpu.VMEM(flat, half),
            pltpu.VMEM((half_groups,) + flat, half),
            pltpu.VMEM((half_groups,) + flat, half),
            pltpu.VMEM((half_groups, heads, per_row, 8, width), full),
            pltpu.VMEM(flat, half),
            pltpu.VMEM((heads, per_row, 8, width), full),
            pltpu.VMEM(flat, full),
            pltpu.VMEM((heads, rows, width), full),
            pltpu.VMEM((heads, rows, width), full),
            pltpu.VMEM((rows, width), jnp.int32),
            pltpu.VMEM(flat, half),
            pltpu.VMEM(flat, half),
            pltpu.VMEM(filter_taps.shape, full),
            pltpu.VMEM(filter_taps.shape, half),
            pltpu.VMEM(forward.shape, half),
            pltpu.VMEM(inverse.shape, half),
            pltpu.VMEM((length, 2 * width), half),
            pltpu.VMEM((2 * width, length), half),
            pltpu.VMEM((per_row, 2, block, rows), full),
            pltpu.VMEM((blocks, 2 * block, width), full),
            pltpu.VMEM((blocks, 2 * block, 2 * width), full),
            pltpu.VMEM((blocks, 2 * block, width), full),
            pltpu.VMEM((length, 2 * width), half),
            pltpu.VMEM(flat, half),
            pltpu.VMEM(flat, half),
            pltpu.SemaphoreType.DMA((8, heads, groups)),
            pltpu.SemaphoreType.DMA((8, heads, groups)),
            pltpu.SemaphoreType.DMA((9,)),
            pltpu.SemaphoreType.DMA((heads,)),
            pltpu.SemaphoreType.DMA((heads // 2,)),
        ],
        compiler_params=pltpu.CompilerParams(
            collective_id=0, has_side_effects=True, vmem_limit_bytes=67043328
        ),
        name="fused_window",
    )(
        doc_lengths,
        queries,
        key_rows,
        values,
        in_gate,
        out_gate,
        filter_taps,
        forward,
        inverse,
    )


def fits_fused(queries):
    rows, channels = queries.shape
    groups = lax.axis_size("ctx")
    return groups == 4 and channels == groups * HEAD_DIM and rows % BLOCK == 0


def either_body(queries, *rest):
    if fits_fused(queries):
        return fused_body(queries, *rest)
    return body(queries, *rest)


def solution(mesh):
    return jax.shard_map(
        either_body,
        mesh=mesh,
        in_specs=(
            P(("dp", "ctx"), "tp"),
            P(("dp", "ctx"), "tp"),
            P(("dp", "ctx"), "tp"),
            P("dp"),
            P(("dp", "ctx"), "tp"),
            P(("dp", "ctx"), "tp"),
            P(("dp", "tp"), "ctx"),
        ),
        out_specs=(P(("dp", "ctx"), "tp"), P(("dp", "ctx"), "tp")),
        check_vma=False,
    )
```

```python
import math

import jax
import jax.numpy as jnp
import numpy as np
from jax import lax
from jax.experimental import pallas as pl
from jax.experimental.pallas import tpu as pltpu
from jax.sharding import PartitionSpec as P

HEAD_DIM = 128
KV_REACH = 3
BLOCK = 256


masked_score = -1e30


def passed_along(x, axis, by):
    length = lax.axis_size(axis)
    pairs = [(i, i + by) for i in range(length) if 0 <= i + by < length]
    return lax.ppermute(x, axis, pairs)


def doc_of(positions, doc_lengths):
    order = jnp.arange(doc_lengths.shape[0], dtype=jnp.int32)
    before = order[None, :] < order[:, None]
    starts = jnp.sum(jnp.where(before, doc_lengths[None, :], 0), axis=1)
    inside = (starts[None, :] <= positions[:, None]).astype(jnp.int32)
    return jnp.sum(inside, axis=1) - 1


def attend_block(carried, pair, query_heads, allowed):
    running_max, running_sum, weighted = carried
    row_count = query_heads.shape[0]
    key_heads = pair[0].reshape(row_count, -1, HEAD_DIM)
    value_heads = pair[1].reshape(row_count, -1, HEAD_DIM)
    scores = jnp.einsum(
        "qhd,khd->hqk", query_heads, key_heads, preferred_element_type=jnp.float32
    ) / math.sqrt(HEAD_DIM)
    scores = jnp.where(allowed[None], scores, masked_score)
    new_max = jnp.maximum(running_max, jnp.max(scores, axis=2))
    rescale = jnp.exp(running_max - new_max)
    exp_scores = jnp.exp(scores - new_max[:, :, None])
    running_sum = running_sum * rescale + jnp.sum(exp_scores, axis=2)
    weighted = weighted * rescale[:, :, None] + jnp.einsum(
        "hqk,khd->hqd",
        exp_scores.astype(jnp.bfloat16),
        value_heads,
        preferred_element_type=jnp.float32,
    )
    return (new_max, running_sum, weighted)


def split_parts(source):
    high_part = lax.optimization_barrier(source.astype(jnp.bfloat16))
    low_part = (source - high_part.astype(jnp.float32)).astype(jnp.bfloat16)
    return (high_part, low_part)


def split_mul(form, left_parts, right_parts):
    first = jnp.einsum(form, left_parts[0], right_parts[0], preferred_element_type=jnp.float32)
    second = jnp.einsum(form, left_parts[0], right_parts[1], preferred_element_type=jnp.float32)
    third = jnp.einsum(form, left_parts[1], right_parts[0], preferred_element_type=jnp.float32)
    return first + (second + third)


def dft_tables(length):
    inner_len = math.gcd(length, 256)
    outer_len = 2 * length // inner_len
    freq_rows = jnp.arange(outer_len, dtype=jnp.int32)
    time_rows = jnp.arange(outer_len // 2, dtype=jnp.int32)
    inner_index = jnp.arange(inner_len, dtype=jnp.int32)
    angle_outer = (
        2.0
        * math.pi
        / outer_len
        * (freq_rows[:, None] * time_rows[None, :] % outer_len).astype(jnp.float32)
    )
    angle_twist = (
        2.0
        * math.pi
        / (2 * length)
        * (freq_rows[:, None] * inner_index[None, :] % (2 * length)).astype(jnp.float32)
    )
    angle_inner = (
        2.0
        * math.pi
        / inner_len
        * (inner_index[:, None] * inner_index[None, :] % inner_len).astype(jnp.float32)
    )
    return (
        split_parts(jnp.cos(angle_outer)),
        split_parts(-jnp.sin(angle_outer)),
        jnp.cos(angle_twist),
        -jnp.sin(angle_twist),
        split_parts(jnp.cos(angle_inner)),
        split_parts(-jnp.sin(angle_inner)),
    )


def right_mul(left_parts, table_parts):
    return split_mul("cin,nm->cim", left_parts, table_parts)


def forward_dft(samples, tables):
    outer_cos, outer_sin, twist_cos, twist_sin, inner_cos, inner_sin = tables
    item_count = samples.shape[0]
    shaped = split_parts(samples.reshape(item_count, outer_cos[0].shape[1], inner_cos[0].shape[0]))
    section_real = split_mul("ij,cjn->cin", outer_cos, shaped)
    section_imag = split_mul("ij,cjn->cin", outer_sin, shaped)
    turned_real = split_parts(section_real * twist_cos - section_imag * twist_sin)
    turned_imag = split_parts(section_real * twist_sin + section_imag * twist_cos)
    spec_real = right_mul(turned_real, inner_cos) - right_mul(turned_imag, inner_sin)
    spec_imag = right_mul(turned_real, inner_sin) + right_mul(turned_imag, inner_cos)
    return (spec_real, spec_imag)


def inverse_dft(prod_real, prod_imag, tables):
    outer_cos, outer_sin, twist_cos, twist_sin, inner_cos, inner_sin = tables
    item_count = prod_real.shape[0]
    half_len = outer_cos[0].shape[1]
    inner_len = inner_cos[0].shape[0]
    real_parts = split_parts(prod_real)
    imag_parts = split_parts(prod_imag)
    back_real = right_mul(real_parts, inner_cos) + right_mul(imag_parts, inner_sin)
    back_imag = right_mul(imag_parts, inner_cos) - right_mul(real_parts, inner_sin)
    unturn_real = split_parts(back_real * twist_cos + back_imag * twist_sin)
    unturn_imag = split_parts(back_imag * twist_cos - back_real * twist_sin)
    rows_out = split_mul("ij,cin->cjn", outer_cos, unturn_real) + split_mul(
        "ij,cin->cjn", outer_sin, unturn_imag
    )
    return (rows_out * (1.0 / (2 * half_len * inner_len))).reshape(item_count, half_len * inner_len)


def filter_apply(signal, filter_spec, tables):
    sig_real, sig_imag = forward_dft(signal, tables)
    tap_real, tap_imag = filter_spec
    prod_real = sig_real * tap_real - sig_imag * tap_imag
    prod_imag = sig_real * tap_imag + sig_imag * tap_real
    return inverse_dft(prod_real, prod_imag, tables)


def body(queries, key_rows, values, doc_lengths, in_gate, out_gate, filter_taps):
    row_count, channels = queries.shape
    head_count = channels // HEAD_DIM
    group_count = lax.axis_size("ctx")
    per_group = channels // group_count
    seq_len = row_count * group_count
    tables = dft_tables(seq_len)
    taps_grouped = filter_taps.reshape(group_count, per_group, row_count)
    query_pos = lax.axis_index("ctx") * row_count + jnp.arange(row_count, dtype=jnp.int32)
    query_doc = doc_of(query_pos, doc_lengths)
    query_heads = queries.reshape(row_count, head_count, HEAD_DIM)
    carried = (
        jnp.full((head_count, row_count), masked_score, jnp.float32),
        jnp.zeros((head_count, row_count), jnp.float32),
        jnp.zeros((head_count, row_count, HEAD_DIM), jnp.float32),
    )

    def visit(state_now, pair, distance):
        key_pos = query_pos - distance * row_count
        key_doc = doc_of(key_pos, doc_lengths)
        allowed = (key_doc[None, :] == query_doc[:, None]) & (
            key_pos[None, :] <= query_pos[:, None]
        )
        return lax.cond(
            jnp.any(allowed),
            lambda state_in: attend_block(state_in, pair, query_heads, allowed),
            lambda state_in: state_in,
            state_now,
        )

    own_pair = jnp.stack((key_rows, values))
    carried = visit(carried, own_pair, 0)
    moving = own_pair
    for distance in range(1, KV_REACH + 1):
        moving = passed_along(moving, "ctx", 1)
        carried = visit(carried, moving, distance)
    running_max, running_sum, weighted = carried
    attended = (
        (weighted / running_sum[:, :, None])
        .transpose(1, 0, 2)
        .reshape(row_count, channels)
        .astype(jnp.bfloat16)
    )
    gated = (in_gate.astype(jnp.float32) * attended.astype(jnp.float32)).T
    gated_grouped = gated.reshape(group_count, per_group, row_count)
    pair = (
        lax.all_to_all(
            gated_grouped.astype(jnp.bfloat16), "ctx", split_axis=0, concat_axis=2, tiled=True
        ).astype(gated_grouped.dtype),
        lax.all_to_all(
            taps_grouped.astype(jnp.bfloat16), "ctx", split_axis=0, concat_axis=2, tiled=True
        ).astype(taps_grouped.dtype),
    )
    item_count = pair[0].shape[1]
    signal = pair[0].reshape(item_count, -1)
    taps = pair[1].reshape(item_count, -1)
    result = filter_apply(signal, forward_dft(taps, tables), tables)
    mixed = result.reshape(1, item_count, -1)
    returned = lax.all_to_all(
        mixed.astype(jnp.bfloat16), "ctx", split_axis=2, concat_axis=0, tiled=True
    ).astype(mixed.dtype)
    hyena_out = (out_gate.astype(jnp.float32) * returned.reshape(channels, row_count).T).astype(
        jnp.bfloat16
    )
    return (attended, hyena_out)


def block_tables(block):
    freq = np.arange(block)
    time = np.arange(block)
    angle = np.pi / (2 * block) * ((2 * freq[:, None] + 1) * time[None, :] % (4 * block))
    forward = np.concatenate((np.cos(angle), -np.sin(angle)), axis=0)
    inverse = forward.T / block
    return (jnp.asarray(forward, jnp.bfloat16), jnp.asarray(inverse, jnp.bfloat16))


def only_when(condition, action):
    @pl.when(condition)
    def _():
        action()


def fused_kernel(
    docs_ref,
    query_ref,
    key_ref,
    value_ref,
    gate_ref,
    taps_ref,
    forward_ref,
    inverse_ref,
    attn_ref,
    mixed_back,
    own_query,
    own_key,
    own_value,
    own_gate,
    prev_key,
    prev_value,
    far_query,
    far_out,
    far_stat,
    low_out,
    low_stat,
    own_out,
    own_top,
    own_sum,
    row_starts,
    attn_buf,
    gated_buf,
    wide_taps,
    half_taps,
    forward_buf,
    inverse_buf,
    all_gate,
    all_taps,
    score_buf,
    sig_spec,
    tap_spec,
    prod_spec,
    mixed_buf,
    first_mixed,
    send_sem,
    recv_sem,
    local_sem,
    taps_sem,
):
    rows, channels = query_ref.shape
    length = all_gate.shape[0]
    groups = length // rows
    width = channels // groups
    heads = groups
    half = groups // 2
    block = inverse_ref.shape[0]
    blocks = length // block
    per_row = rows // block
    me = lax.axis_index("ctx")
    low = me < half
    high = me >= half
    second = half - 1
    odd = lax.rem(me, 2) == 1
    scale = math.log2(math.e) / math.sqrt(HEAD_DIM)

    def rows_of(group):
        return pl.ds(pl.multiple_of(group * rows, rows), rows)

    def cols_of(head):
        return pl.ds(pl.multiple_of(head * width, width), width)

    def home_of(head):
        return second + head // 2

    def part_of(at):
        return pl.ds(pl.multiple_of(at * block, block), block)

    barrier = pltpu.get_barrier_semaphore()
    for step in range(1, groups):
        peer = lax.rem(me + step, groups)
        pl.semaphore_signal(
            barrier, inc=1, device_id={"ctx": peer}, device_id_type=pl.DeviceIdType.MESH
        )

    def remote(kind, head, place, source, target, device):
        return pltpu.make_async_remote_copy(
            src_ref=source,
            dst_ref=target,
            send_sem=send_sem.at[kind, head, place],
            recv_sem=recv_sem.at[kind, head, place],
            device_id={"ctx": device},
            device_id_type=pl.DeviceIdType.MESH,
        )

    following = lax.rem(me + 1, groups)

    def key_copy(head):
        cols = cols_of(head)
        return remote(0, head, 0, key_ref.at[:, cols], prev_key.at[:, cols], following)

    def value_copy(head):
        cols = cols_of(head)
        return remote(1, head, 0, value_ref.at[:, cols], prev_value.at[:, cols], following)

    def query_copy(head, which):
        cols = cols_of(head)
        return remote(
            2, head, half + which, query_ref.at[:, cols], far_query.at[which, :, cols], second
        )

    def taps_refs(head, group):
        return (
            half_taps.at[cols_of(head), :],
            all_taps.at[cols_of(head % 2), rows_of(group)],
        )

    def gated_refs(head, group):
        return (
            gated_buf.at[:, cols_of(head)],
            all_gate.at[rows_of(group), cols_of(head % 2)],
        )

    def mixed_refs(head, group):
        return (
            mixed_buf.at[rows_of(group), cols_of(head % 2)],
            mixed_back.at[:, cols_of(head)],
        )

    refs_of = {3: taps_refs, 4: gated_refs, 7: mixed_refs}

    def hop(kind, head, group, device):
        return remote(kind, head, group, *refs_of[kind](head, group), device)

    def stay(kind, head, group):
        return pltpu.make_async_copy(
            *refs_of[kind](head, group), recv_sem.at[kind, head, group]
        )

    def send_home(kind, head):
        home = home_of(head)
        only_when(me != home, lambda: hop(kind, head, me, home).start())
        only_when(me == home, lambda: stay(kind, head, me).start())

    def wait_home(kind, head):
        for group in range(groups):
            only_when(me != group, lambda: hop(kind, head, group, second).wait_recv())
            only_when(me == group, lambda: stay(kind, head, group).wait())

    def out_copy(head, which):
        cols = cols_of(head)
        return remote(
            5, head, half + which, far_out.at[which, :, cols], low_out.at[:, cols], half + which
        )

    def out_piece(head, which, at):
        cols = cols_of(head)
        part = pl.ds(at * block, block)
        return remote(
            5,
            head,
            half + which,
            far_out.at[which, part, cols],
            low_out.at[part, cols],
            half + which,
        )

    def stat_copy(head, which):
        return remote(
            6, head, half + which, far_stat.at[which, head], low_stat.at[head], half + which
        )

    def pair_rows(pair):
        return pl.ds(pair * 2 * width, 2 * width)

    def taps_in(pair):
        return pltpu.make_async_copy(
            taps_ref.at[pair_rows(pair), :], wide_taps.at[pair_rows(pair), :], taps_sem.at[pair]
        )

    for pair in range(heads // 2 - 1, -1, -1):
        taps_in(pair).start()

    loads = []
    for place, (source, target) in enumerate(
        (
            (query_ref, own_query),
            (key_ref, own_key),
            (value_ref, own_value),
            (gate_ref, own_gate),
        )
    ):
        loads.append(pltpu.make_async_copy(source, target, local_sem.at[place]))
    loads.append(pltpu.make_async_copy(forward_ref, forward_buf, local_sem.at[5]))
    loads.append(pltpu.make_async_copy(inverse_ref, inverse_buf, local_sem.at[6]))
    for load in loads:
        load.start()

    def round_taps(pair):
        taps_in(pair).wait()

        def round_body(at, carry):
            part = pl.ds(pl.multiple_of(pair * 2 * width + at * 64, 64), 64)
            half_taps[part, :] = wide_taps[part, :].astype(jnp.bfloat16)
            return carry

        lax.fori_loop(0, 2 * width // 64, round_body, 0)

    round_taps(1)
    pl.semaphore_wait(barrier, groups - 1)

    @pl.when(me == half)
    def _():
        for head in range(heads):
            query_copy(head, 0).start()

    @pl.when(me == groups - 1)
    def _():
        query_copy(0, 1).start()

    @pl.when(jnp.logical_not(odd))
    def _():
        key_copy(0).start()
        value_copy(0).start()

    @pl.when(me == 0)
    def _():
        send_home(3, 2)
        key_copy(1).start()
        value_copy(1).start()
        send_home(3, 3)
        for head in range(2, heads):
            key_copy(head).start()
            value_copy(head).start()

    @pl.when(me == second)
    def _():
        for head in (2, 3):
            send_home(3, head)

    round_taps(0)

    @pl.when(me <= second)
    def _():
        for head in (0, 1):
            send_home(3, head)

    @pl.when(me == half)
    def _():
        for head in range(1, heads):
            key_copy(head).start()
            value_copy(head).start()
        for head in (0, 1, 2, 3):
            send_home(3, head)

    @pl.when(me == groups - 1)
    def _():
        for head in (2, 3):
            send_home(3, head)

    for load in loads:
        load.wait()

    starts = []
    total = 0
    wide_end = 0
    wide_start = 0
    for doc in range(docs_ref.shape[0]):
        starts.append(total)
        begun = total <= rows
        wide_start = jnp.where(begun, total, wide_start)
        total = total + docs_ref[doc]
        wide_end = jnp.where(begun, total, wide_end)

    def start_body(at, carry):
        row_pos = lax.broadcasted_iota(jnp.int32, (block, width), 0) + (me * rows + at * block)
        row_start = jnp.zeros((block, width), jnp.int32)
        for start in starts:
            row_start = jnp.where(row_pos >= start, start, row_start)
        row_starts[part_of(at), :] = row_start
        return carry

    lax.fori_loop(0, per_row, start_body, 0)
    lane_of = lax.broadcasted_iota(jnp.int32, (block, width), 1)
    row_of = lax.broadcasted_iota(jnp.int32, (block, width), 0)

    def attend(slot, query, chunks):
        top = jnp.full((block, width), masked_score, jnp.float32)
        for place, (key, _, mask) in enumerate(chunks):
            scores = lax.dot_general(
                query,
                key,
                (((1,), (1,)), ((), ())),
                preferred_element_type=jnp.float32,
            )
            for first in range(0, key.shape[0], width):
                piece = mask(scores[:, first : first + width], first)
                score_buf[slot, place, :, first : first + width] = piece
                top = jnp.maximum(top, piece)
        top = jnp.max(top, axis=1, keepdims=True)
        running = jnp.zeros((block, width), jnp.float32)
        weighted = jnp.zeros((block, width), jnp.float32)
        for place, (key, value, _) in enumerate(chunks):
            count = key.shape[0]
            weight = jnp.exp2((score_buf[slot, place, :, :count] - top) * scale)
            for first in range(0, count, width):
                running = running + weight[:, first : first + width]
            weighted = weighted + jnp.dot(
                weight.astype(jnp.bfloat16), value, preferred_element_type=jnp.float32
            )
        return (top * scale, jnp.sum(running, axis=1, keepdims=True), weighted)

    diagonal = lax.broadcasted_iota(jnp.int32, (width, width), 0) == lax.broadcasted_iota(
        jnp.int32, (width, width), 1
    )

    pieces_of = block // width

    def as_rows(packed, at, column):
        at_row = lax.broadcasted_iota(jnp.int32, (8, width), 0)
        for piece in range(pieces_of):
            spread = jnp.where(diagonal, column[piece * width : (piece + 1) * width, :], 0.0)
            line = jnp.sum(spread, axis=0, keepdims=True)
            packed = jnp.where(at_row == at * pieces_of + piece, line, packed)
        return packed

    def as_column(packed, at):
        pieces = []
        for piece in range(at * pieces_of, (at + 1) * pieces_of):
            spread = jnp.where(diagonal, packed[piece : piece + 1, :], 0.0)
            pieces.append(jnp.sum(spread, axis=1, keepdims=True))
        return jnp.concatenate(pieces, axis=0)

    def far_tiles(head):
        cols = cols_of(head)
        first_lane = lax.broadcasted_iota(jnp.int32, (1, rows), 1)
        outside = jnp.where(first_lane >= wide_start, 0.0, masked_score)

        def first_mask(scores, first):
            return scores + outside[:, first : first + width]

        def no_mask(scores, first):
            return scores

        def which_body(turn, carry):
            which = 1 - turn
            query_copy(head, which).wait_recv()
            packed = jnp.zeros((8, width), jnp.float32)
            for at in range(per_row):
                part = pl.ds(at * block, block)
                top, total_weight, weighted = attend(
                    at,
                    far_query[which, part, cols],
                    (
                        (prev_key[:, cols], prev_value[:, cols], first_mask),
                        (own_key[:, cols], own_value[:, cols], no_mask),
                    ),
                )
                far_out[which, part, cols] = (weighted / total_weight).astype(jnp.bfloat16)
                out_piece(head, which, at).start()
                level = top + jnp.log(total_weight) * math.log2(math.e)
                inside = row_of[:, :1] + ((half + which) * rows + at * block) < wide_end
                packed = as_rows(packed, at, jnp.where(inside, level, masked_score))
            far_stat[which, head] = packed
            stat_copy(head, which).start()
            return carry

        lax.fori_loop(0, groups - half, which_body, 0)

    def own_tiles(head, with_prev):
        cols = cols_of(head)
        for at in range(per_row):
            part = pl.ds(at * block, block)
            row_start = row_starts[part, :]
            count = (at + 1) * block

            def own_mask(scores, first, at=at, row_start=row_start):
                allowed = lane_of >= row_start - (me * rows + first)
                if first >= at * block:
                    allowed = allowed & (lane_of <= row_of - (first - at * block))
                return jnp.where(allowed, scores, masked_score)

            def prev_mask(scores, first, row_start=row_start):
                allowed = lane_of >= row_start - ((me - 1) * rows + first)
                return jnp.where(allowed, scores, masked_score)

            chunks = ((own_key[:count, cols], own_value[:count, cols], own_mask),)
            if with_prev:
                chunks = ((prev_key[:, cols], prev_value[:, cols], prev_mask),) + chunks
            top, total_weight, weighted = attend(at, own_query[part, cols], chunks)
            own_out[part, cols] = weighted
            own_top[head, part, :] = jnp.broadcast_to(top, (block, width))
            own_sum[head, part, :] = jnp.broadcast_to(total_weight, (block, width))

    def finish(head, merged):
        cols = cols_of(head)
        for at in range(per_row):
            part = pl.ds(at * block, block)
            weighted = own_out[part, cols]
            total_weight = own_sum[head, part, :]
            if merged:
                own_level = own_top[head, part, :]
                low_level = jnp.broadcast_to(as_column(low_stat[head], at), (block, width))
                level = jnp.maximum(own_level, low_level)
                own_share = jnp.exp2(own_level - level)
                low_share = jnp.exp2(low_level - level)
                total_weight = total_weight * own_share + low_share
                weighted = weighted * own_share + low_share * low_out[part, cols].astype(
                    jnp.float32
                )
            attended = (weighted / total_weight).astype(jnp.bfloat16)
            attn_buf[part, cols] = attended
            gated_buf[part, cols] = (
                own_gate[part, cols].astype(jnp.float32) * attended.astype(jnp.float32)
            ).astype(jnp.bfloat16)
        send_home(4, head)

    def head_body(head, carry):
        @pl.when(odd)
        def _():
            key_copy(head).wait_recv()
            value_copy(head).wait_recv()

        @pl.when((me == groups - 1) & (head < heads - 1))
        def _():
            query_copy(head + 1, 1).start()

        only_when(me == second, lambda: far_tiles(head))
        only_when(odd, lambda: own_tiles(head, True))
        only_when(jnp.logical_not(odd), lambda: own_tiles(head, False))
        only_when(low, lambda: finish(head, False))
        return carry

    lax.fori_loop(0, heads, head_body, 0)

    @pl.when(me == groups - 1)
    def _():
        for head in (0, 1):
            send_home(3, head)

    def merge_body(head, carry):
        out_copy(head, me - half).wait_recv()
        stat_copy(head, me - half).wait_recv()
        finish(head, True)
        return carry

    only_when(high, lambda: lax.fori_loop(0, heads, merge_body, 0))

    attn_done = pltpu.make_async_copy(attn_buf, attn_ref, local_sem.at[7])
    attn_done.start()

    lift = 8

    batch = 4

    def spectra(target, count, source_of):
        def body(turn, carry):
            for piece in range(batch):
                at = turn * batch + piece
                target[at] = source_of(at)
            return carry

        if count % batch:
            for at in range(count):
                target[at] = source_of(at)
        else:
            lax.fori_loop(0, count // batch, body, 0)

    def tap_blocks(count, source_of):
        spectra(
            tap_spec,
            count,
            lambda at: lax.dot_general(
                forward_buf[...],
                source_of(at),
                (((1,), (1,)), ((), ())),
                preferred_element_type=jnp.float32,
            ),
        )

    def signal_blocks(count, source_of):
        spectra(
            sig_spec,
            count,
            lambda at: jnp.dot(
                forward_buf[...], source_of(at), preferred_element_type=jnp.float32
            ),
        )

    def products(cols, first, count):
        def product_body(at, carry):
            real = pl.ds(pl.multiple_of(at * lift, lift), lift)
            imag = pl.ds(pl.multiple_of(block + at * lift, lift), lift)
            uneven = lax.rem(lax.broadcasted_iota(jnp.int32, (lift, width), 0), 2) == 1
            sign = jnp.where(uneven, -1.0, 1.0).astype(jnp.float32)
            tap_real = []
            tap_imag = []
            for k in range(count):
                now_real = tap_spec[k, real, cols]
                now_imag = tap_spec[k, imag, cols]
                if k > 0:
                    now_real = now_real - sign * tap_spec[k - 1, imag, cols]
                    now_imag = now_imag + sign * tap_spec[k - 1, real, cols]
                tap_real.append(now_real)
                tap_imag.append(now_imag)
            for out in range(first, count):
                sum_real = jnp.zeros((lift, width), jnp.float32)
                sum_imag = jnp.zeros((lift, width), jnp.float32)
                for j in range(out + 1):
                    sig_real = sig_spec[j, real, :]
                    sig_imag = sig_spec[j, imag, :]
                    sum_real = (
                        sum_real + sig_real * tap_real[out - j] - sig_imag * tap_imag[out - j]
                    )
                    sum_imag = (
                        sum_imag + sig_real * tap_imag[out - j] + sig_imag * tap_real[out - j]
                    )
                prod_spec[out, real, :] = sum_real
                prod_spec[out, imag, :] = sum_imag
            return carry

        lax.fori_loop(0, block // lift, product_body, 0)

    def mixed_block(index):
        return jnp.dot(
            inverse_buf[...],
            prod_spec[index].astype(jnp.bfloat16),
            preferred_element_type=jnp.float32,
        ).astype(jnp.bfloat16)

    def convolve(lane, carry):
        head = (me - second) * 2 + lane
        cols = cols_of(lane)
        wait_home(4, head)
        signal_blocks(blocks, lambda at: all_gate[part_of(at), cols])
        products(cols, per_row, blocks)

        def group_body(turn, carry):
            group = groups - 1 - turn
            for at in range(per_row):
                index = group * per_row + at
                mixed_buf[part_of(index), cols] = mixed_block(index)
            only_when(me != group, lambda: hop(7, head, group, group).start())
            only_when(me == group, lambda: stay(7, head, group).start())
            return carry

        lax.fori_loop(0, groups - 1, group_body, 0)
        return carry

    is_home = (me == second) | (me == half)

    @pl.when(is_home)
    def _():
        first = (me - second) * 2
        for lane in range(2):
            wait_home(3, first + lane)
        tap_blocks(blocks, lambda at: all_taps[:, part_of(at)])
        lax.fori_loop(0, 2, convolve, 0)

    @pl.when(me == 0)
    def _():
        def pair_body(pair, carry):
            channels_of = pl.ds(pl.multiple_of(pair * 2 * width, 2 * width), 2 * width)
            tap_blocks(per_row, lambda at: half_taps[channels_of, at * block : (at + 1) * block])

            def lane_body(lane, carry):
                cols = cols_of(pair * 2 + lane)
                signal_blocks(
                    per_row, lambda at: gated_buf[at * block : (at + 1) * block, cols]
                )
                products(cols_of(lane), 0, per_row)
                for at in range(per_row):
                    first_mixed[at * block : (at + 1) * block, cols] = mixed_block(at)
                return carry

            lax.fori_loop(0, 2, lane_body, 0)
            return carry

        lax.fori_loop(0, heads // 2, pair_body, 0)
        first_done = pltpu.make_async_copy(first_mixed, mixed_back, local_sem.at[8])
        first_done.start()
        first_done.wait()

    for head in range(heads):
        home = home_of(head)
        only_when((me != home) & (me != 0), lambda: hop(7, head, me, home).wait_recv())
        only_when(me == home, lambda: stay(7, head, me).wait())
    attn_done.wait()

    for head in range(heads):
        home = home_of(head)

        @pl.when(jnp.logical_not(odd))
        def _():
            key_copy(head).wait_send()
            value_copy(head).wait_send()

        only_when(high, lambda: query_copy(head, me - half).wait_send())

        @pl.when(me != home)
        def _():
            hop(3, head, me, home).wait_send()
            hop(4, head, me, home).wait_send()

        for which in range(groups - half):

            @pl.when(me == second)
            def _():
                out_copy(head, which).wait_send()
                stat_copy(head, which).wait_send()

        for group in range(1, groups):
            if group != home:
                only_when(me == home, lambda: hop(7, head, group, group).wait_send())


PIECES = 4


def finish_kernel(
    attn_in,
    mixed_in,
    gate_in,
    attn_out,
    hyena_out,
    attn_buf,
    mixed_buf,
    gate_buf,
    hyena_buf,
    sem,
):
    count = mixed_buf.shape[0] // PIECES

    def move(kind, piece):
        part = pl.ds(piece * count, count)
        source, target = (
            (mixed_in, mixed_buf),
            (gate_in, gate_buf),
            (attn_in, attn_buf),
            (hyena_buf, hyena_out),
            (attn_buf, attn_out),
        )[kind]
        return pltpu.make_async_copy(source.at[part, :], target.at[part, :], sem.at[kind, piece])

    for piece in range(PIECES):
        move(0, piece).start()
        move(1, piece).start()
    for piece in range(PIECES):
        move(2, piece).start()
    for piece in range(PIECES):
        part = pl.ds(piece * count, count)
        move(0, piece).wait()
        move(1, piece).wait()
        hyena_buf[part, :] = (
            gate_buf[part, :].astype(jnp.float32) * mixed_buf[part, :].astype(jnp.float32)
        ).astype(jnp.bfloat16)
        move(3, piece).start()
    for piece in range(PIECES):
        move(2, piece).wait()
        move(4, piece).start()
    for piece in range(PIECES):
        move(3, piece).wait()
        move(4, piece).wait()


def fused_body(queries, key_rows, values, doc_lengths, in_gate, out_gate, filter_taps):
    rows, channels = queries.shape
    groups = lax.axis_size("ctx")
    width = channels // groups
    length = rows * groups
    block = BLOCK
    blocks = length // block
    per_row = rows // block
    heads = groups
    half_groups = groups // 2
    forward, inverse = block_tables(block)
    anywhere = pl.BlockSpec(memory_space=pl.ANY)
    half = jnp.bfloat16
    full = jnp.float32
    flat = (rows, channels)
    attended, mixed = pl.pallas_call(
        fused_kernel,
        out_shape=(
            jax.ShapeDtypeStruct(flat, half),
            jax.ShapeDtypeStruct(flat, half),
        ),
        in_specs=[pl.BlockSpec(memory_space=pltpu.SMEM)] + [anywhere] * 7,
        out_specs=(anywhere, anywhere),
        scratch_shapes=[
            pltpu.VMEM(flat, half),
            pltpu.VMEM(flat, half),
            pltpu.VMEM(flat, half),
            pltpu.VMEM(flat, half),
            pltpu.VMEM(flat, half),
            pltpu.VMEM(flat, half),
            pltpu.VMEM((half_groups,) + flat, half),
            pltpu.VMEM((half_groups,) + flat, half),
            pltpu.VMEM((half_groups, heads, 8, width), full),
            pltpu.VMEM(flat, half),
            pltpu.VMEM((heads, 8, width), full),
            pltpu.VMEM(flat, full),
            pltpu.VMEM((heads, rows, width), full),
            pltpu.VMEM((heads, rows, width), full),
            pltpu.VMEM((rows, width), jnp.int32),
            pltpu.VMEM(flat, half),
            pltpu.VMEM(flat, half),
            pltpu.VMEM(filter_taps.shape, full),
            pltpu.VMEM(filter_taps.shape, half),
            pltpu.VMEM(forward.shape, half),
            pltpu.VMEM(inverse.shape, half),
            pltpu.VMEM((length, 2 * width), half),
            pltpu.VMEM((2 * width, length), half),
            pltpu.VMEM((per_row, 2, block, rows), full),
            pltpu.VMEM((blocks, 2 * block, width), full),
            pltpu.VMEM((blocks, 2 * block, 2 * width), full),
            pltpu.VMEM((blocks, 2 * block, width), full),
            pltpu.VMEM((length, 2 * width), half),
            pltpu.VMEM(flat, half),
            pltpu.SemaphoreType.DMA((8, heads, groups)),
            pltpu.SemaphoreType.DMA((8, heads, groups)),
            pltpu.SemaphoreType.DMA((9,)),
            pltpu.SemaphoreType.DMA((heads // 2,)),
        ],
        compiler_params=pltpu.CompilerParams(
            collective_id=0, has_side_effects=True, vmem_limit_bytes=67043328
        ),
        name="fused_window",
    )(
        doc_lengths,
        queries,
        key_rows,
        values,
        in_gate,
        filter_taps,
        forward,
        inverse,
    )
    return pl.pallas_call(
        finish_kernel,
        out_shape=(
            jax.ShapeDtypeStruct(flat, half),
            jax.ShapeDtypeStruct(flat, half),
        ),
        in_specs=[anywhere] * 3,
        out_specs=(anywhere, anywhere),
        scratch_shapes=[
            pltpu.VMEM(flat, half),
            pltpu.VMEM(flat, half),
            pltpu.VMEM(flat, half),
            pltpu.VMEM(flat, half),
            pltpu.SemaphoreType.DMA((5, PIECES)),
        ],
        compiler_params=pltpu.CompilerParams(vmem_limit_bytes=67043328),
        name="finish_window",
    )(attended, mixed, out_gate)


def fits_fused(queries):
    rows, channels = queries.shape
    groups = lax.axis_size("ctx")
    return (
        groups == 4
        and channels == groups * HEAD_DIM
        and rows % BLOCK == 0
        and rows <= 8 * HEAD_DIM
    )


def either_body(queries, *rest):
    if fits_fused(queries):
        return fused_body(queries, *rest)
    return body(queries, *rest)


def solution(mesh):
    return jax.shard_map(
        either_body,
        mesh=mesh,
        in_specs=(
            P(("dp", "ctx"), "tp"),
            P(("dp", "ctx"), "tp"),
            P(("dp", "ctx"), "tp"),
            P("dp"),
            P(("dp", "ctx"), "tp"),
            P(("dp", "ctx"), "tp"),
            P(("dp", "tp"), "ctx"),
        ),
        out_specs=(P(("dp", "ctx"), "tp"), P(("dp", "ctx"), "tp")),
        check_vma=False,
    )
```

```python
import math

import jax
import jax.numpy as jnp
import numpy as np
from jax import lax
from jax.experimental import pallas as pl
from jax.experimental.pallas import tpu as pltpu
from jax.sharding import PartitionSpec as P

HEAD_DIM = 128
KV_REACH = 3
BLOCK = 256


masked_score = -1e30


def passed_along(x, axis, by):
    length = lax.axis_size(axis)
    pairs = [(i, i + by) for i in range(length) if 0 <= i + by < length]
    return lax.ppermute(x, axis, pairs)


def doc_of(positions, doc_lengths):
    order = jnp.arange(doc_lengths.shape[0], dtype=jnp.int32)
    before = order[None, :] < order[:, None]
    starts = jnp.sum(jnp.where(before, doc_lengths[None, :], 0), axis=1)
    inside = (starts[None, :] <= positions[:, None]).astype(jnp.int32)
    return jnp.sum(inside, axis=1) - 1


def attend_block(carried, pair, query_heads, allowed):
    running_max, running_sum, weighted = carried
    row_count = query_heads.shape[0]
    key_heads = pair[0].reshape(row_count, -1, HEAD_DIM)
    value_heads = pair[1].reshape(row_count, -1, HEAD_DIM)
    scores = jnp.einsum(
        "qhd,khd->hqk", query_heads, key_heads, preferred_element_type=jnp.float32
    ) / math.sqrt(HEAD_DIM)
    scores = jnp.where(allowed[None], scores, masked_score)
    new_max = jnp.maximum(running_max, jnp.max(scores, axis=2))
    rescale = jnp.exp(running_max - new_max)
    exp_scores = jnp.exp(scores - new_max[:, :, None])
    running_sum = running_sum * rescale + jnp.sum(exp_scores, axis=2)
    weighted = weighted * rescale[:, :, None] + jnp.einsum(
        "hqk,khd->hqd",
        exp_scores.astype(jnp.bfloat16),
        value_heads,
        preferred_element_type=jnp.float32,
    )
    return (new_max, running_sum, weighted)


def split_parts(source):
    high_part = lax.optimization_barrier(source.astype(jnp.bfloat16))
    low_part = (source - high_part.astype(jnp.float32)).astype(jnp.bfloat16)
    return (high_part, low_part)


def split_mul(form, left_parts, right_parts):
    first = jnp.einsum(form, left_parts[0], right_parts[0], preferred_element_type=jnp.float32)
    second = jnp.einsum(form, left_parts[0], right_parts[1], preferred_element_type=jnp.float32)
    third = jnp.einsum(form, left_parts[1], right_parts[0], preferred_element_type=jnp.float32)
    return first + (second + third)


def dft_tables(length):
    inner_len = math.gcd(length, 256)
    outer_len = 2 * length // inner_len
    freq_rows = jnp.arange(outer_len, dtype=jnp.int32)
    time_rows = jnp.arange(outer_len // 2, dtype=jnp.int32)
    inner_index = jnp.arange(inner_len, dtype=jnp.int32)
    angle_outer = (
        2.0
        * math.pi
        / outer_len
        * (freq_rows[:, None] * time_rows[None, :] % outer_len).astype(jnp.float32)
    )
    angle_twist = (
        2.0
        * math.pi
        / (2 * length)
        * (freq_rows[:, None] * inner_index[None, :] % (2 * length)).astype(jnp.float32)
    )
    angle_inner = (
        2.0
        * math.pi
        / inner_len
        * (inner_index[:, None] * inner_index[None, :] % inner_len).astype(jnp.float32)
    )
    return (
        split_parts(jnp.cos(angle_outer)),
        split_parts(-jnp.sin(angle_outer)),
        jnp.cos(angle_twist),
        -jnp.sin(angle_twist),
        split_parts(jnp.cos(angle_inner)),
        split_parts(-jnp.sin(angle_inner)),
    )


def right_mul(left_parts, table_parts):
    return split_mul("cin,nm->cim", left_parts, table_parts)


def forward_dft(samples, tables):
    outer_cos, outer_sin, twist_cos, twist_sin, inner_cos, inner_sin = tables
    item_count = samples.shape[0]
    shaped = split_parts(samples.reshape(item_count, outer_cos[0].shape[1], inner_cos[0].shape[0]))
    section_real = split_mul("ij,cjn->cin", outer_cos, shaped)
    section_imag = split_mul("ij,cjn->cin", outer_sin, shaped)
    turned_real = split_parts(section_real * twist_cos - section_imag * twist_sin)
    turned_imag = split_parts(section_real * twist_sin + section_imag * twist_cos)
    spec_real = right_mul(turned_real, inner_cos) - right_mul(turned_imag, inner_sin)
    spec_imag = right_mul(turned_real, inner_sin) + right_mul(turned_imag, inner_cos)
    return (spec_real, spec_imag)


def inverse_dft(prod_real, prod_imag, tables):
    outer_cos, outer_sin, twist_cos, twist_sin, inner_cos, inner_sin = tables
    item_count = prod_real.shape[0]
    half_len = outer_cos[0].shape[1]
    inner_len = inner_cos[0].shape[0]
    real_parts = split_parts(prod_real)
    imag_parts = split_parts(prod_imag)
    back_real = right_mul(real_parts, inner_cos) + right_mul(imag_parts, inner_sin)
    back_imag = right_mul(imag_parts, inner_cos) - right_mul(real_parts, inner_sin)
    unturn_real = split_parts(back_real * twist_cos + back_imag * twist_sin)
    unturn_imag = split_parts(back_imag * twist_cos - back_real * twist_sin)
    rows_out = split_mul("ij,cin->cjn", outer_cos, unturn_real) + split_mul(
        "ij,cin->cjn", outer_sin, unturn_imag
    )
    return (rows_out * (1.0 / (2 * half_len * inner_len))).reshape(item_count, half_len * inner_len)


def filter_apply(signal, filter_spec, tables):
    sig_real, sig_imag = forward_dft(signal, tables)
    tap_real, tap_imag = filter_spec
    prod_real = sig_real * tap_real - sig_imag * tap_imag
    prod_imag = sig_real * tap_imag + sig_imag * tap_real
    return inverse_dft(prod_real, prod_imag, tables)


def body(queries, key_rows, values, doc_lengths, in_gate, out_gate, filter_taps):
    row_count, channels = queries.shape
    head_count = channels // HEAD_DIM
    group_count = lax.axis_size("ctx")
    per_group = channels // group_count
    seq_len = row_count * group_count
    tables = dft_tables(seq_len)
    taps_grouped = filter_taps.reshape(group_count, per_group, row_count)
    query_pos = lax.axis_index("ctx") * row_count + jnp.arange(row_count, dtype=jnp.int32)
    query_doc = doc_of(query_pos, doc_lengths)
    query_heads = queries.reshape(row_count, head_count, HEAD_DIM)
    carried = (
        jnp.full((head_count, row_count), masked_score, jnp.float32),
        jnp.zeros((head_count, row_count), jnp.float32),
        jnp.zeros((head_count, row_count, HEAD_DIM), jnp.float32),
    )

    def visit(state_now, pair, distance):
        key_pos = query_pos - distance * row_count
        key_doc = doc_of(key_pos, doc_lengths)
        allowed = (key_doc[None, :] == query_doc[:, None]) & (
            key_pos[None, :] <= query_pos[:, None]
        )
        return lax.cond(
            jnp.any(allowed),
            lambda state_in: attend_block(state_in, pair, query_heads, allowed),
            lambda state_in: state_in,
            state_now,
        )

    own_pair = jnp.stack((key_rows, values))
    carried = visit(carried, own_pair, 0)
    moving = own_pair
    for distance in range(1, KV_REACH + 1):
        moving = passed_along(moving, "ctx", 1)
        carried = visit(carried, moving, distance)
    running_max, running_sum, weighted = carried
    attended = (
        (weighted / running_sum[:, :, None])
        .transpose(1, 0, 2)
        .reshape(row_count, channels)
        .astype(jnp.bfloat16)
    )
    gated = (in_gate.astype(jnp.float32) * attended.astype(jnp.float32)).T
    gated_grouped = gated.reshape(group_count, per_group, row_count)
    pair = (
        lax.all_to_all(
            gated_grouped.astype(jnp.bfloat16), "ctx", split_axis=0, concat_axis=2, tiled=True
        ).astype(gated_grouped.dtype),
        lax.all_to_all(
            taps_grouped.astype(jnp.bfloat16), "ctx", split_axis=0, concat_axis=2, tiled=True
        ).astype(taps_grouped.dtype),
    )
    item_count = pair[0].shape[1]
    signal = pair[0].reshape(item_count, -1)
    taps = pair[1].reshape(item_count, -1)
    result = filter_apply(signal, forward_dft(taps, tables), tables)
    mixed = result.reshape(1, item_count, -1)
    returned = lax.all_to_all(
        mixed.astype(jnp.bfloat16), "ctx", split_axis=2, concat_axis=0, tiled=True
    ).astype(mixed.dtype)
    hyena_out = (out_gate.astype(jnp.float32) * returned.reshape(channels, row_count).T).astype(
        jnp.bfloat16
    )
    return (attended, hyena_out)


def block_tables(block):
    freq = np.arange(block)
    time = np.arange(block)
    angle = np.pi / (2 * block) * ((2 * freq[:, None] + 1) * time[None, :] % (4 * block))
    forward = np.concatenate((np.cos(angle), -np.sin(angle)), axis=0)
    inverse = forward.T / block
    return (jnp.asarray(forward, jnp.bfloat16), jnp.asarray(inverse, jnp.bfloat16))


def only_when(condition, action):
    @pl.when(condition)
    def _():
        action()


def fused_kernel(
    docs_ref,
    query_ref,
    key_ref,
    value_ref,
    gate_ref,
    taps_ref,
    forward_ref,
    inverse_ref,
    attn_ref,
    mixed_back,
    own_query,
    own_key,
    own_value,
    own_gate,
    prev_key,
    prev_value,
    far_query,
    far_out,
    far_stat,
    low_out,
    low_stat,
    own_out,
    own_top,
    own_sum,
    row_starts,
    attn_buf,
    gated_buf,
    wide_taps,
    half_taps,
    forward_buf,
    inverse_buf,
    all_gate,
    all_taps,
    score_buf,
    sig_spec,
    tap_spec,
    prod_spec,
    mixed_buf,
    first_mixed,
    send_sem,
    recv_sem,
    local_sem,
    taps_sem,
):
    rows, channels = query_ref.shape
    length = all_gate.shape[0]
    groups = length // rows
    width = channels // groups
    heads = groups
    half = groups // 2
    block = inverse_ref.shape[0]
    blocks = length // block
    per_row = rows // block
    me = lax.axis_index("ctx")
    low = me < half
    high = me >= half
    second = half - 1
    odd = lax.rem(me, 2) == 1
    scale = math.log2(math.e) / math.sqrt(HEAD_DIM)

    def rows_of(group):
        return pl.ds(pl.multiple_of(group * rows, rows), rows)

    def cols_of(head):
        return pl.ds(pl.multiple_of(head * width, width), width)

    def home_of(head):
        return second + head // 2

    def part_of(at):
        return pl.ds(pl.multiple_of(at * block, block), block)

    barrier = pltpu.get_barrier_semaphore()
    for step in range(1, groups):
        peer = lax.rem(me + step, groups)
        pl.semaphore_signal(
            barrier, inc=1, device_id={"ctx": peer}, device_id_type=pl.DeviceIdType.MESH
        )

    def remote(kind, head, place, source, target, device):
        return pltpu.make_async_remote_copy(
            src_ref=source,
            dst_ref=target,
            send_sem=send_sem.at[kind, head, place],
            recv_sem=recv_sem.at[kind, head, place],
            device_id={"ctx": device},
            device_id_type=pl.DeviceIdType.MESH,
        )

    following = lax.rem(me + 1, groups)

    def key_copy(head):
        cols = cols_of(head)
        return remote(0, head, 0, key_ref.at[:, cols], prev_key.at[:, cols], following)

    def value_copy(head):
        cols = cols_of(head)
        return remote(1, head, 0, value_ref.at[:, cols], prev_value.at[:, cols], following)

    def query_copy(head, which):
        cols = cols_of(head)
        return remote(
            2, head, half + which, query_ref.at[:, cols], far_query.at[which, :, cols], second
        )

    def taps_refs(head, group):
        return (
            half_taps.at[cols_of(head), :],
            all_taps.at[cols_of(head % 2), rows_of(group)],
        )

    def gated_refs(head, group):
        return (
            gated_buf.at[:, cols_of(head)],
            all_gate.at[rows_of(group), cols_of(head % 2)],
        )

    def mixed_refs(head, group):
        return (
            mixed_buf.at[rows_of(group), cols_of(head % 2)],
            mixed_back.at[:, cols_of(head)],
        )

    refs_of = {3: taps_refs, 4: gated_refs, 7: mixed_refs}

    def hop(kind, head, group, device):
        return remote(kind, head, group, *refs_of[kind](head, group), device)

    def stay(kind, head, group):
        return pltpu.make_async_copy(
            *refs_of[kind](head, group), recv_sem.at[kind, head, group]
        )

    def send_home(kind, head):
        home = home_of(head)
        only_when(me != home, lambda: hop(kind, head, me, home).start())
        only_when(me == home, lambda: stay(kind, head, me).start())

    def wait_home(kind, head):
        for group in range(groups):
            only_when(me != group, lambda: hop(kind, head, group, second).wait_recv())
            only_when(me == group, lambda: stay(kind, head, group).wait())

    def out_copy(head, which):
        cols = cols_of(head)
        return remote(
            5, head, half + which, far_out.at[which, :, cols], low_out.at[:, cols], half + which
        )

    def out_piece(head, which, at):
        cols = cols_of(head)
        part = pl.ds(at * block, block)
        return remote(
            5,
            head,
            half + which,
            far_out.at[which, part, cols],
            low_out.at[part, cols],
            half + which,
        )

    def stat_copy(head, which):
        return remote(
            6, head, half + which, far_stat.at[which, head], low_stat.at[head], half + which
        )

    def pair_rows(pair):
        return pl.ds(pair * 2 * width, 2 * width)

    def taps_in(pair):
        return pltpu.make_async_copy(
            taps_ref.at[pair_rows(pair), :], wide_taps.at[pair_rows(pair), :], taps_sem.at[pair]
        )

    for pair in range(heads // 2 - 1, -1, -1):
        taps_in(pair).start()

    loads = []
    for place, (source, target) in enumerate(
        (
            (query_ref, own_query),
            (key_ref, own_key),
            (value_ref, own_value),
            (gate_ref, own_gate),
        )
    ):
        loads.append(pltpu.make_async_copy(source, target, local_sem.at[place]))
    loads.append(pltpu.make_async_copy(forward_ref, forward_buf, local_sem.at[5]))
    loads.append(pltpu.make_async_copy(inverse_ref, inverse_buf, local_sem.at[6]))
    for load in loads:
        load.start()

    def round_taps(pair):
        taps_in(pair).wait()

        def round_body(at, carry):
            part = pl.ds(pl.multiple_of(pair * 2 * width + at * 64, 64), 64)
            half_taps[part, :] = wide_taps[part, :].astype(jnp.bfloat16)
            return carry

        lax.fori_loop(0, 2 * width // 64, round_body, 0)

    round_taps(1)
    pl.semaphore_wait(barrier, groups - 1)

    @pl.when(me == half)
    def _():
        for head in range(heads):
            query_copy(head, 0).start()

    @pl.when(me == groups - 1)
    def _():
        query_copy(0, 1).start()

    @pl.when(jnp.logical_not(odd))
    def _():
        key_copy(0).start()
        value_copy(0).start()

    @pl.when(me == 0)
    def _():
        send_home(3, 2)
        key_copy(1).start()
        value_copy(1).start()
        send_home(3, 3)
        for head in range(2, heads):
            key_copy(head).start()
            value_copy(head).start()

    @pl.when(me == second)
    def _():
        for head in (2, 3):
            send_home(3, head)

    round_taps(0)

    @pl.when(me <= second)
    def _():
        for head in (0, 1):
            send_home(3, head)

    @pl.when(me == half)
    def _():
        for head in range(1, heads):
            key_copy(head).start()
            value_copy(head).start()
        for head in (0, 1, 2, 3):
            send_home(3, head)

    @pl.when(me == groups - 1)
    def _():
        for head in (2, 3):
            send_home(3, head)

    for load in loads:
        load.wait()

    starts = []
    total = 0
    wide_end = 0
    wide_start = 0
    for doc in range(docs_ref.shape[0]):
        starts.append(total)
        begun = total <= rows
        wide_start = jnp.where(begun, total, wide_start)
        total = total + docs_ref[doc]
        wide_end = jnp.where(begun, total, wide_end)

    def start_body(at, carry):
        row_pos = lax.broadcasted_iota(jnp.int32, (block, width), 0) + (me * rows + at * block)
        row_start = jnp.zeros((block, width), jnp.int32)
        for start in starts:
            row_start = jnp.where(row_pos >= start, start, row_start)
        row_starts[part_of(at), :] = row_start
        return carry

    lax.fori_loop(0, per_row, start_body, 0)
    lane_of = lax.broadcasted_iota(jnp.int32, (block, width), 1)
    row_of = lax.broadcasted_iota(jnp.int32, (block, width), 0)

    def attend(slot, query, chunks):
        top = jnp.full((block, width), masked_score, jnp.float32)
        for place, (key, _, mask) in enumerate(chunks):
            scores = lax.dot_general(
                query,
                key,
                (((1,), (1,)), ((), ())),
                preferred_element_type=jnp.float32,
            )
            for first in range(0, key.shape[0], width):
                piece = mask(scores[:, first : first + width], first)
                score_buf[slot, place, :, first : first + width] = piece
                top = jnp.maximum(top, piece)
        top = jnp.max(top, axis=1, keepdims=True)
        running = jnp.zeros((block, width), jnp.float32)
        weighted = jnp.zeros((block, width), jnp.float32)
        for place, (key, value, _) in enumerate(chunks):
            count = key.shape[0]
            weight = jnp.exp2((score_buf[slot, place, :, :count] - top) * scale)
            for first in range(0, count, width):
                running = running + weight[:, first : first + width]
            weighted = weighted + jnp.dot(
                weight.astype(jnp.bfloat16), value, preferred_element_type=jnp.float32
            )
        return (top * scale, jnp.sum(running, axis=1, keepdims=True), weighted)

    diagonal = lax.broadcasted_iota(jnp.int32, (width, width), 0) == lax.broadcasted_iota(
        jnp.int32, (width, width), 1
    )

    pieces_of = block // width

    def as_rows(packed, at, column):
        at_row = lax.broadcasted_iota(jnp.int32, (8, width), 0)
        for piece in range(pieces_of):
            spread = jnp.where(diagonal, column[piece * width : (piece + 1) * width, :], 0.0)
            line = jnp.sum(spread, axis=0, keepdims=True)
            packed = jnp.where(at_row == at * pieces_of + piece, line, packed)
        return packed

    def as_column(packed, at):
        pieces = []
        for piece in range(at * pieces_of, (at + 1) * pieces_of):
            spread = jnp.where(diagonal, packed[piece : piece + 1, :], 0.0)
            pieces.append(jnp.sum(spread, axis=1, keepdims=True))
        return jnp.concatenate(pieces, axis=0)

    def far_tiles(head):
        cols = cols_of(head)
        first_lane = lax.broadcasted_iota(jnp.int32, (1, rows), 1)
        outside = jnp.where(first_lane >= wide_start, 0.0, masked_score)

        def first_mask(scores, first):
            return scores + outside[:, first : first + width]

        def no_mask(scores, first):
            return scores

        def which_body(turn, carry):
            which = 1 - turn
            query_copy(head, which).wait_recv()
            packed = jnp.zeros((8, width), jnp.float32)
            for at in range(per_row):
                part = pl.ds(at * block, block)
                top, total_weight, weighted = attend(
                    at,
                    far_query[which, part, cols],
                    (
                        (prev_key[:, cols], prev_value[:, cols], first_mask),
                        (own_key[:, cols], own_value[:, cols], no_mask),
                    ),
                )
                far_out[which, part, cols] = (weighted / total_weight).astype(jnp.bfloat16)
                out_piece(head, which, at).start()
                level = top + jnp.log(total_weight) * math.log2(math.e)
                inside = row_of[:, :1] + ((half + which) * rows + at * block) < wide_end
                packed = as_rows(packed, at, jnp.where(inside, level, masked_score))
            far_stat[which, head] = packed
            stat_copy(head, which).start()
            return carry

        lax.fori_loop(0, groups - half, which_body, 0)

    def own_tiles(head, with_prev):
        cols = cols_of(head)
        for at in range(per_row):
            part = pl.ds(at * block, block)
            row_start = row_starts[part, :]
            count = (at + 1) * block

            def own_mask(scores, first, at=at, row_start=row_start):
                allowed = lane_of >= row_start - (me * rows + first)
                if first >= at * block:
                    allowed = allowed & (lane_of <= row_of - (first - at * block))
                return jnp.where(allowed, scores, masked_score)

            def prev_mask(scores, first, row_start=row_start):
                allowed = lane_of >= row_start - ((me - 1) * rows + first)
                return jnp.where(allowed, scores, masked_score)

            chunks = ((own_key[:count, cols], own_value[:count, cols], own_mask),)
            if with_prev:
                chunks = ((prev_key[:, cols], prev_value[:, cols], prev_mask),) + chunks
            top, total_weight, weighted = attend(at, own_query[part, cols], chunks)
            own_out[part, cols] = weighted
            own_top[head, part, :] = jnp.broadcast_to(top, (block, width))
            own_sum[head, part, :] = jnp.broadcast_to(total_weight, (block, width))

    def finish(head, merged):
        cols = cols_of(head)
        for at in range(per_row):
            part = pl.ds(at * block, block)
            weighted = own_out[part, cols]
            total_weight = own_sum[head, part, :]
            if merged:
                own_level = own_top[head, part, :]
                low_level = jnp.broadcast_to(as_column(low_stat[head], at), (block, width))
                level = jnp.maximum(own_level, low_level)
                own_share = jnp.exp2(own_level - level)
                low_share = jnp.exp2(low_level - level)
                total_weight = total_weight * own_share + low_share
                weighted = weighted * own_share + low_share * low_out[part, cols].astype(
                    jnp.float32
                )
            attended = (weighted / total_weight).astype(jnp.bfloat16)
            attn_buf[part, cols] = attended
            gated_buf[part, cols] = (
                own_gate[part, cols].astype(jnp.float32) * attended.astype(jnp.float32)
            ).astype(jnp.bfloat16)
        send_home(4, head)

    def head_body(head, carry):
        @pl.when(odd)
        def _():
            key_copy(head).wait_recv()
            value_copy(head).wait_recv()

        @pl.when((me == groups - 1) & (head < heads - 1))
        def _():
            query_copy(head + 1, 1).start()

        only_when(me == second, lambda: far_tiles(head))
        only_when(odd, lambda: own_tiles(head, True))
        only_when(jnp.logical_not(odd), lambda: own_tiles(head, False))
        only_when(low, lambda: finish(head, False))
        return carry

    lax.fori_loop(0, heads, head_body, 0)

    @pl.when(me == groups - 1)
    def _():
        for head in (0, 1):
            send_home(3, head)

    def merge_body(head, carry):
        out_copy(head, me - half).wait_recv()
        stat_copy(head, me - half).wait_recv()
        finish(head, True)
        return carry

    only_when(high, lambda: lax.fori_loop(0, heads, merge_body, 0))

    attn_done = pltpu.make_async_copy(attn_buf, attn_ref, local_sem.at[7])
    attn_done.start()

    lift = 8

    batch = 4

    def tap_blocks(count, source_of):
        def transform(at):
            tap_spec[at] = lax.dot_general(
                forward_buf[...],
                source_of(at),
                (((1,), (1,)), ((), ())),
                preferred_element_type=jnp.float32,
            )

        if count % batch:
            for at in range(count):
                transform(at)
        else:

            def body(turn, carry):
                for piece in range(batch):
                    transform(turn * batch + piece)
                return carry

            lax.fori_loop(0, count // batch, body, 0)

        uneven = lax.rem(lax.broadcasted_iota(jnp.int32, (lift, width), 0), 2) == 1
        sign = jnp.where(uneven, -1.0, 1.0).astype(jnp.float32)

        def combine_body(at, carry):
            real, imag = planes_of(at)
            for lane in range(2):
                cols = pl.ds(lane * width, width)
                reals = [tap_spec[k, real, cols] for k in range(count)]
                imags = [tap_spec[k, imag, cols] for k in range(count)]
                for k in range(count):
                    now_real = reals[k]
                    now_imag = imags[k]
                    if k > 0:
                        now_real = now_real - sign * imags[k - 1]
                        now_imag = now_imag + sign * reals[k - 1]
                    tap_spec[k, real, cols] = now_real
                    tap_spec[k, imag, cols] = now_imag
            return carry

        lax.fori_loop(0, block // lift, combine_body, 0)

    def planes_of(at):
        return tuple(
            pl.ds(pl.multiple_of(plane * block + at * lift, lift), lift) for plane in range(2)
        )

    def signal_block(at, source):
        sig_spec[at] = jnp.dot(forward_buf[...], source, preferred_element_type=jnp.float32)

    def products(cols, group):
        outs = range(group * per_row, (group + 1) * per_row)

        def product_rows(at):
            real, imag = planes_of(at)
            sums = {out: [jnp.zeros((lift, width), jnp.float32)] * 3 for out in outs}
            taps = {}
            for j in range(outs[-1] + 1):
                sig_real = sig_spec[j, real, :]
                sig_imag = sig_spec[j, imag, :]
                sig_both = sig_real + sig_imag
                for out in outs:
                    k = out - j
                    if k < 0:
                        continue
                    if k not in taps:
                        tap_real = tap_spec[k, real, cols]
                        tap_imag = tap_spec[k, imag, cols]
                        taps[k] = (tap_real, tap_imag - tap_real, tap_imag + tap_real)
                    tap_real, tap_less, tap_more = taps[k]
                    first, second_sum, third = sums[out]
                    sums[out] = [
                        first + sig_both * tap_real,
                        second_sum + sig_real * tap_less,
                        third + sig_imag * tap_more,
                    ]
            for out in outs:
                first, second_sum, third = sums[out]
                prod_spec[out, real, :] = first - third
                prod_spec[out, imag, :] = first + second_sum

        def product_body(turn, carry):
            for piece in range(batch):
                product_rows(turn * batch + piece)
            return carry

        lax.fori_loop(0, block // (lift * batch), product_body, 0)

    def mixed_block(index):
        return jnp.dot(
            inverse_buf[...],
            prod_spec[index].astype(jnp.bfloat16),
            preferred_element_type=jnp.float32,
        ).astype(jnp.bfloat16)

    def convolve(lane, carry):
        head = (me - second) * 2 + lane
        cols = cols_of(lane)
        for turn in range(groups):
            if turn < half:
                group = jnp.where(me == second, second - turn, half + turn)
            else:
                group = jnp.where(me == second, groups + second - turn, turn - half)
            if turn == 0:
                stay(4, head, group).wait()
            else:
                hop(4, head, group, second).wait_recv()
            for piece in range(per_row):
                at = group * per_row + piece
                signal_block(at, all_gate[part_of(at), cols])
        for group in [groups - 1] + list(range(1, groups - 1)):
            products(cols, group)
            for at in range(group * per_row, (group + 1) * per_row):
                mixed_buf[at * block : (at + 1) * block, cols] = mixed_block(at)
            only_when(me != group, lambda: hop(7, head, group, group).start())
            only_when(me == group, lambda: stay(7, head, group).start())
        return carry

    is_home = (me == second) | (me == half)

    @pl.when(is_home)
    def _():
        first = (me - second) * 2
        for lane in range(2):
            wait_home(3, first + lane)
        tap_blocks(blocks, lambda at: all_taps[:, part_of(at)])
        lax.fori_loop(0, 2, convolve, 0)

    @pl.when(me == 0)
    def _():
        def pair_body(pair, carry):
            channels_of = pl.ds(pl.multiple_of(pair * 2 * width, 2 * width), 2 * width)
            tap_blocks(per_row, lambda at: half_taps[channels_of, at * block : (at + 1) * block])

            def lane_body(lane, carry):
                cols = cols_of(pair * 2 + lane)
                for at in range(per_row):
                    signal_block(at, gated_buf[at * block : (at + 1) * block, cols])
                products(cols_of(lane), 0)
                for at in range(per_row):
                    first_mixed[at * block : (at + 1) * block, cols] = mixed_block(at)
                return carry

            lax.fori_loop(0, 2, lane_body, 0)
            return carry

        lax.fori_loop(0, heads // 2, pair_body, 0)
        first_done = pltpu.make_async_copy(first_mixed, mixed_back, local_sem.at[8])
        first_done.start()
        first_done.wait()

    for head in range(heads):
        home = home_of(head)
        only_when((me != home) & (me != 0), lambda: hop(7, head, me, home).wait_recv())
        only_when(me == home, lambda: stay(7, head, me).wait())
    attn_done.wait()

    for head in range(heads):
        home = home_of(head)

        @pl.when(jnp.logical_not(odd))
        def _():
            key_copy(head).wait_send()
            value_copy(head).wait_send()

        only_when(high, lambda: query_copy(head, me - half).wait_send())

        @pl.when(me != home)
        def _():
            hop(3, head, me, home).wait_send()
            hop(4, head, me, home).wait_send()

        for which in range(groups - half):

            @pl.when(me == second)
            def _():
                out_copy(head, which).wait_send()
                stat_copy(head, which).wait_send()

        for group in range(1, groups):
            if group != home:
                only_when(me == home, lambda: hop(7, head, group, group).wait_send())


PIECES = 4


def finish_kernel(
    attn_in,
    mixed_in,
    gate_in,
    attn_out,
    hyena_out,
    attn_buf,
    mixed_buf,
    gate_buf,
    hyena_buf,
    sem,
):
    count = mixed_buf.shape[0] // PIECES

    def move(kind, piece):
        part = pl.ds(piece * count, count)
        source, target = (
            (mixed_in, mixed_buf),
            (gate_in, gate_buf),
            (attn_in, attn_buf),
            (hyena_buf, hyena_out),
            (attn_buf, attn_out),
        )[kind]
        return pltpu.make_async_copy(source.at[part, :], target.at[part, :], sem.at[kind, piece])

    for piece in range(PIECES):
        move(0, piece).start()
        move(1, piece).start()
    for piece in range(PIECES):
        move(2, piece).start()
    for piece in range(PIECES):
        part = pl.ds(piece * count, count)
        move(0, piece).wait()
        move(1, piece).wait()
        hyena_buf[part, :] = (
            gate_buf[part, :].astype(jnp.float32) * mixed_buf[part, :].astype(jnp.float32)
        ).astype(jnp.bfloat16)
        move(3, piece).start()
    for piece in range(PIECES):
        move(2, piece).wait()
        move(4, piece).start()
    for piece in range(PIECES):
        move(3, piece).wait()
        move(4, piece).wait()


def fused_body(queries, key_rows, values, doc_lengths, in_gate, out_gate, filter_taps):
    rows, channels = queries.shape
    groups = lax.axis_size("ctx")
    width = channels // groups
    length = rows * groups
    block = BLOCK
    blocks = length // block
    per_row = rows // block
    heads = groups
    half_groups = groups // 2
    forward, inverse = block_tables(block)
    anywhere = pl.BlockSpec(memory_space=pl.ANY)
    half = jnp.bfloat16
    full = jnp.float32
    flat = (rows, channels)
    attended, mixed = pl.pallas_call(
        fused_kernel,
        out_shape=(
            jax.ShapeDtypeStruct(flat, half),
            jax.ShapeDtypeStruct(flat, half),
        ),
        in_specs=[pl.BlockSpec(memory_space=pltpu.SMEM)] + [anywhere] * 7,
        out_specs=(anywhere, anywhere),
        scratch_shapes=[
            pltpu.VMEM(flat, half),
            pltpu.VMEM(flat, half),
            pltpu.VMEM(flat, half),
            pltpu.VMEM(flat, half),
            pltpu.VMEM(flat, half),
            pltpu.VMEM(flat, half),
            pltpu.VMEM((half_groups,) + flat, half),
            pltpu.VMEM((half_groups,) + flat, half),
            pltpu.VMEM((half_groups, heads, 8, width), full),
            pltpu.VMEM(flat, half),
            pltpu.VMEM((heads, 8, width), full),
            pltpu.VMEM(flat, full),
            pltpu.VMEM((heads, rows, width), full),
            pltpu.VMEM((heads, rows, width), full),
            pltpu.VMEM((rows, width), jnp.int32),
            pltpu.VMEM(flat, half),
            pltpu.VMEM(flat, half),
            pltpu.VMEM(filter_taps.shape, full),
            pltpu.VMEM(filter_taps.shape, half),
            pltpu.VMEM(forward.shape, half),
            pltpu.VMEM(inverse.shape, half),
            pltpu.VMEM((length, 2 * width), half),
            pltpu.VMEM((2 * width, length), half),
            pltpu.VMEM((per_row, 2, block, rows), full),
            pltpu.VMEM((blocks, 2 * block, width), full),
            pltpu.VMEM((blocks, 2 * block, 2 * width), full),
            pltpu.VMEM((blocks, 2 * block, width), full),
            pltpu.VMEM((length, 2 * width), half),
            pltpu.VMEM(flat, half),
            pltpu.SemaphoreType.DMA((8, heads, groups)),
            pltpu.SemaphoreType.DMA((8, heads, groups)),
            pltpu.SemaphoreType.DMA((9,)),
            pltpu.SemaphoreType.DMA((heads // 2,)),
        ],
        compiler_params=pltpu.CompilerParams(
            collective_id=0, has_side_effects=True, vmem_limit_bytes=67043328
        ),
        name="fused_window",
    )(
        doc_lengths,
        queries,
        key_rows,
        values,
        in_gate,
        filter_taps,
        forward,
        inverse,
    )
    return pl.pallas_call(
        finish_kernel,
        out_shape=(
            jax.ShapeDtypeStruct(flat, half),
            jax.ShapeDtypeStruct(flat, half),
        ),
        in_specs=[anywhere] * 3,
        out_specs=(anywhere, anywhere),
        scratch_shapes=[
            pltpu.VMEM(flat, half),
            pltpu.VMEM(flat, half),
            pltpu.VMEM(flat, half),
            pltpu.VMEM(flat, half),
            pltpu.SemaphoreType.DMA((5, PIECES)),
        ],
        compiler_params=pltpu.CompilerParams(vmem_limit_bytes=67043328),
        name="finish_window",
    )(attended, mixed, out_gate)


def fits_fused(queries):
    rows, channels = queries.shape
    groups = lax.axis_size("ctx")
    return (
        groups == 4
        and channels == groups * HEAD_DIM
        and rows % BLOCK == 0
        and rows <= 8 * HEAD_DIM
    )


def either_body(queries, *rest):
    if fits_fused(queries):
        return fused_body(queries, *rest)
    return body(queries, *rest)


def solution(mesh):
    return jax.shard_map(
        either_body,
        mesh=mesh,
        in_specs=(
            P(("dp", "ctx"), "tp"),
            P(("dp", "ctx"), "tp"),
            P(("dp", "ctx"), "tp"),
            P("dp"),
            P(("dp", "ctx"), "tp"),
            P(("dp", "ctx"), "tp"),
            P(("dp", "tp"), "ctx"),
        ),
        out_specs=(P(("dp", "ctx"), "tp"), P(("dp", "ctx"), "tp")),
        check_vma=False,
    )
```

```python
import math

import jax
import jax.numpy as jnp
import numpy as np
from jax import lax
from jax.experimental import pallas as pl
from jax.experimental.pallas import tpu as pltpu
from jax.sharding import PartitionSpec as P

HEAD_DIM = 128
KV_REACH = 3
BLOCK = 256


masked_score = -1e30


def passed_along(x, axis, by):
    length = lax.axis_size(axis)
    pairs = [(i, i + by) for i in range(length) if 0 <= i + by < length]
    return lax.ppermute(x, axis, pairs)


def doc_of(positions, doc_lengths):
    order = jnp.arange(doc_lengths.shape[0], dtype=jnp.int32)
    before = order[None, :] < order[:, None]
    starts = jnp.sum(jnp.where(before, doc_lengths[None, :], 0), axis=1)
    inside = (starts[None, :] <= positions[:, None]).astype(jnp.int32)
    return jnp.sum(inside, axis=1) - 1


def attend_block(carried, pair, query_heads, allowed):
    running_max, running_sum, weighted = carried
    row_count = query_heads.shape[0]
    key_heads = pair[0].reshape(row_count, -1, HEAD_DIM)
    value_heads = pair[1].reshape(row_count, -1, HEAD_DIM)
    scores = jnp.einsum(
        "qhd,khd->hqk", query_heads, key_heads, preferred_element_type=jnp.float32
    ) / math.sqrt(HEAD_DIM)
    scores = jnp.where(allowed[None], scores, masked_score)
    new_max = jnp.maximum(running_max, jnp.max(scores, axis=2))
    rescale = jnp.exp(running_max - new_max)
    exp_scores = jnp.exp(scores - new_max[:, :, None])
    running_sum = running_sum * rescale + jnp.sum(exp_scores, axis=2)
    weighted = weighted * rescale[:, :, None] + jnp.einsum(
        "hqk,khd->hqd",
        exp_scores.astype(jnp.bfloat16),
        value_heads,
        preferred_element_type=jnp.float32,
    )
    return (new_max, running_sum, weighted)


def split_parts(source):
    high_part = lax.optimization_barrier(source.astype(jnp.bfloat16))
    low_part = (source - high_part.astype(jnp.float32)).astype(jnp.bfloat16)
    return (high_part, low_part)


def split_mul(form, left_parts, right_parts):
    first = jnp.einsum(form, left_parts[0], right_parts[0], preferred_element_type=jnp.float32)
    second = jnp.einsum(form, left_parts[0], right_parts[1], preferred_element_type=jnp.float32)
    third = jnp.einsum(form, left_parts[1], right_parts[0], preferred_element_type=jnp.float32)
    return first + (second + third)


def dft_tables(length):
    inner_len = math.gcd(length, 256)
    outer_len = 2 * length // inner_len
    freq_rows = jnp.arange(outer_len, dtype=jnp.int32)
    time_rows = jnp.arange(outer_len // 2, dtype=jnp.int32)
    inner_index = jnp.arange(inner_len, dtype=jnp.int32)
    angle_outer = (
        2.0
        * math.pi
        / outer_len
        * (freq_rows[:, None] * time_rows[None, :] % outer_len).astype(jnp.float32)
    )
    angle_twist = (
        2.0
        * math.pi
        / (2 * length)
        * (freq_rows[:, None] * inner_index[None, :] % (2 * length)).astype(jnp.float32)
    )
    angle_inner = (
        2.0
        * math.pi
        / inner_len
        * (inner_index[:, None] * inner_index[None, :] % inner_len).astype(jnp.float32)
    )
    return (
        split_parts(jnp.cos(angle_outer)),
        split_parts(-jnp.sin(angle_outer)),
        jnp.cos(angle_twist),
        -jnp.sin(angle_twist),
        split_parts(jnp.cos(angle_inner)),
        split_parts(-jnp.sin(angle_inner)),
    )


def right_mul(left_parts, table_parts):
    return split_mul("cin,nm->cim", left_parts, table_parts)


def forward_dft(samples, tables):
    outer_cos, outer_sin, twist_cos, twist_sin, inner_cos, inner_sin = tables
    item_count = samples.shape[0]
    shaped = split_parts(samples.reshape(item_count, outer_cos[0].shape[1], inner_cos[0].shape[0]))
    section_real = split_mul("ij,cjn->cin", outer_cos, shaped)
    section_imag = split_mul("ij,cjn->cin", outer_sin, shaped)
    turned_real = split_parts(section_real * twist_cos - section_imag * twist_sin)
    turned_imag = split_parts(section_real * twist_sin + section_imag * twist_cos)
    spec_real = right_mul(turned_real, inner_cos) - right_mul(turned_imag, inner_sin)
    spec_imag = right_mul(turned_real, inner_sin) + right_mul(turned_imag, inner_cos)
    return (spec_real, spec_imag)


def inverse_dft(prod_real, prod_imag, tables):
    outer_cos, outer_sin, twist_cos, twist_sin, inner_cos, inner_sin = tables
    item_count = prod_real.shape[0]
    half_len = outer_cos[0].shape[1]
    inner_len = inner_cos[0].shape[0]
    real_parts = split_parts(prod_real)
    imag_parts = split_parts(prod_imag)
    back_real = right_mul(real_parts, inner_cos) + right_mul(imag_parts, inner_sin)
    back_imag = right_mul(imag_parts, inner_cos) - right_mul(real_parts, inner_sin)
    unturn_real = split_parts(back_real * twist_cos + back_imag * twist_sin)
    unturn_imag = split_parts(back_imag * twist_cos - back_real * twist_sin)
    rows_out = split_mul("ij,cin->cjn", outer_cos, unturn_real) + split_mul(
        "ij,cin->cjn", outer_sin, unturn_imag
    )
    return (rows_out * (1.0 / (2 * half_len * inner_len))).reshape(item_count, half_len * inner_len)


def filter_apply(signal, filter_spec, tables):
    sig_real, sig_imag = forward_dft(signal, tables)
    tap_real, tap_imag = filter_spec
    prod_real = sig_real * tap_real - sig_imag * tap_imag
    prod_imag = sig_real * tap_imag + sig_imag * tap_real
    return inverse_dft(prod_real, prod_imag, tables)


def body(queries, key_rows, values, doc_lengths, in_gate, out_gate, filter_taps):
    row_count, channels = queries.shape
    head_count = channels // HEAD_DIM
    group_count = lax.axis_size("ctx")
    per_group = channels // group_count
    seq_len = row_count * group_count
    tables = dft_tables(seq_len)
    taps_grouped = filter_taps.reshape(group_count, per_group, row_count)
    query_pos = lax.axis_index("ctx") * row_count + jnp.arange(row_count, dtype=jnp.int32)
    query_doc = doc_of(query_pos, doc_lengths)
    query_heads = queries.reshape(row_count, head_count, HEAD_DIM)
    carried = (
        jnp.full((head_count, row_count), masked_score, jnp.float32),
        jnp.zeros((head_count, row_count), jnp.float32),
        jnp.zeros((head_count, row_count, HEAD_DIM), jnp.float32),
    )

    def visit(state_now, pair, distance):
        key_pos = query_pos - distance * row_count
        key_doc = doc_of(key_pos, doc_lengths)
        allowed = (key_doc[None, :] == query_doc[:, None]) & (
            key_pos[None, :] <= query_pos[:, None]
        )
        return lax.cond(
            jnp.any(allowed),
            lambda state_in: attend_block(state_in, pair, query_heads, allowed),
            lambda state_in: state_in,
            state_now,
        )

    own_pair = jnp.stack((key_rows, values))
    carried = visit(carried, own_pair, 0)
    moving = own_pair
    for distance in range(1, KV_REACH + 1):
        moving = passed_along(moving, "ctx", 1)
        carried = visit(carried, moving, distance)
    running_max, running_sum, weighted = carried
    attended = (
        (weighted / running_sum[:, :, None])
        .transpose(1, 0, 2)
        .reshape(row_count, channels)
        .astype(jnp.bfloat16)
    )
    gated = (in_gate.astype(jnp.float32) * attended.astype(jnp.float32)).T
    gated_grouped = gated.reshape(group_count, per_group, row_count)
    pair = (
        lax.all_to_all(
            gated_grouped.astype(jnp.bfloat16), "ctx", split_axis=0, concat_axis=2, tiled=True
        ).astype(gated_grouped.dtype),
        lax.all_to_all(
            taps_grouped.astype(jnp.bfloat16), "ctx", split_axis=0, concat_axis=2, tiled=True
        ).astype(taps_grouped.dtype),
    )
    item_count = pair[0].shape[1]
    signal = pair[0].reshape(item_count, -1)
    taps = pair[1].reshape(item_count, -1)
    result = filter_apply(signal, forward_dft(taps, tables), tables)
    mixed = result.reshape(1, item_count, -1)
    returned = lax.all_to_all(
        mixed.astype(jnp.bfloat16), "ctx", split_axis=2, concat_axis=0, tiled=True
    ).astype(mixed.dtype)
    hyena_out = (out_gate.astype(jnp.float32) * returned.reshape(channels, row_count).T).astype(
        jnp.bfloat16
    )
    return (attended, hyena_out)


def block_tables(block):
    freq = np.arange(block)
    time = np.arange(block)
    angle = np.pi / (2 * block) * ((2 * freq[:, None] + 1) * time[None, :] % (4 * block))
    forward = np.concatenate((np.cos(angle), -np.sin(angle)), axis=0)
    inverse = forward.T / block
    return (jnp.asarray(forward, jnp.bfloat16), jnp.asarray(inverse, jnp.bfloat16))


def only_when(condition, action):
    @pl.when(condition)
    def _():
        action()


def fused_kernel(
    docs_ref,
    query_ref,
    key_ref,
    value_ref,
    gate_ref,
    taps_ref,
    forward_ref,
    inverse_ref,
    attn_ref,
    mixed_back,
    own_query,
    own_key,
    own_value,
    own_gate,
    prev_key,
    prev_value,
    far_query,
    far_out,
    far_stat,
    low_out,
    low_stat,
    own_out,
    own_top,
    own_sum,
    row_starts,
    attn_buf,
    gated_buf,
    wide_taps,
    half_taps,
    forward_buf,
    inverse_buf,
    all_gate,
    all_taps,
    score_buf,
    sig_spec,
    tap_spec,
    prod_spec,
    mixed_buf,
    first_mixed,
    send_sem,
    recv_sem,
    local_sem,
    taps_sem,
):
    rows, channels = query_ref.shape
    length = all_gate.shape[0]
    groups = length // rows
    width = channels // groups
    heads = groups
    half = groups // 2
    block = inverse_ref.shape[0]
    blocks = length // block
    per_row = rows // block
    me = lax.axis_index("ctx")
    low = me < half
    high = me >= half
    second = half - 1
    odd = lax.rem(me, 2) == 1
    scale = math.log2(math.e) / math.sqrt(HEAD_DIM)

    def rows_of(group):
        return pl.ds(pl.multiple_of(group * rows, rows), rows)

    def cols_of(head):
        return pl.ds(pl.multiple_of(head * width, width), width)

    def home_of(head):
        return second + head // 2

    def part_of(at):
        return pl.ds(pl.multiple_of(at * block, block), block)

    barrier = pltpu.get_barrier_semaphore()
    for step in range(1, groups):
        peer = lax.rem(me + step, groups)

        @pl.when((me != 0) & ((me != groups - 1) | (peer != 0)))
        def _(peer=peer):
            pl.semaphore_signal(
                barrier, inc=1, device_id={"ctx": peer}, device_id_type=pl.DeviceIdType.MESH
            )


    def remote(kind, head, place, source, target, device):
        return pltpu.make_async_remote_copy(
            src_ref=source,
            dst_ref=target,
            send_sem=send_sem.at[kind, head, place],
            recv_sem=recv_sem.at[kind, head, place],
            device_id={"ctx": device},
            device_id_type=pl.DeviceIdType.MESH,
        )

    following = lax.rem(me + 1, groups)

    def key_copy(head):
        cols = cols_of(head)
        return remote(0, head, 0, key_ref.at[:, cols], prev_key.at[:, cols], following)

    def value_copy(head):
        cols = cols_of(head)
        return remote(1, head, 0, value_ref.at[:, cols], prev_value.at[:, cols], following)

    def query_copy(head, which):
        cols = cols_of(head)
        return remote(
            2, head, half + which, query_ref.at[:, cols], far_query.at[which, :, cols], second
        )

    def taps_refs(head, group):
        return (
            half_taps.at[cols_of(head), :],
            all_taps.at[cols_of(head % 2), rows_of(group)],
        )

    def gated_refs(head, group):
        return (
            gated_buf.at[:, cols_of(head)],
            all_gate.at[rows_of(group), cols_of(head % 2)],
        )

    def mixed_refs(head, group):
        return (
            mixed_buf.at[rows_of(group), cols_of(head % 2)],
            mixed_back.at[:, cols_of(head)],
        )

    refs_of = {3: taps_refs, 4: gated_refs, 7: mixed_refs}

    def hop(kind, head, group, device):
        return remote(kind, head, group, *refs_of[kind](head, group), device)

    def stay(kind, head, group):
        return pltpu.make_async_copy(
            *refs_of[kind](head, group), recv_sem.at[kind, head, group]
        )

    def send_home(kind, head):
        home = home_of(head)
        only_when(me != home, lambda: hop(kind, head, me, home).start())
        only_when(me == home, lambda: stay(kind, head, me).start())

    def wait_home(kind, head):
        for group in range(groups):
            only_when(me != group, lambda: hop(kind, head, group, second).wait_recv())
            only_when(me == group, lambda: stay(kind, head, group).wait())

    def out_copy(head, which):
        cols = cols_of(head)
        return remote(
            5, head, half + which, far_out.at[which, :, cols], low_out.at[:, cols], half + which
        )

    def out_piece(head, which, at):
        cols = cols_of(head)
        part = pl.ds(at * block, block)
        return remote(
            5,
            head,
            half + which,
            far_out.at[which, part, cols],
            low_out.at[part, cols],
            half + which,
        )

    def stat_copy(head, which):
        return remote(
            6, head, half + which, far_stat.at[which, head], low_stat.at[head], half + which
        )

    def pair_rows(pair):
        return pl.ds(pair * 2 * width, 2 * width)

    def taps_in(pair):
        return pltpu.make_async_copy(
            taps_ref.at[pair_rows(pair), :], wide_taps.at[pair_rows(pair), :], taps_sem.at[pair]
        )

    for pair in range(heads // 2 - 1, -1, -1):
        taps_in(pair).start()

    loads = []
    for place, (source, target) in enumerate(
        (
            (query_ref, own_query),
            (key_ref, own_key),
            (value_ref, own_value),
            (gate_ref, own_gate),
        )
    ):
        loads.append(pltpu.make_async_copy(source, target, local_sem.at[place]))
    loads.append(pltpu.make_async_copy(forward_ref, forward_buf, local_sem.at[5]))
    loads.append(pltpu.make_async_copy(inverse_ref, inverse_buf, local_sem.at[6]))
    for load in loads:
        load.start()

    def round_taps(pair):
        taps_in(pair).wait()

        def round_body(at, carry):
            part = pl.ds(pl.multiple_of(pair * 2 * width + at * 64, 64), 64)
            half_taps[part, :] = wide_taps[part, :].astype(jnp.bfloat16)
            return carry

        lax.fori_loop(0, 2 * width // 64, round_body, 0)

    round_taps(1)
    pl.semaphore_wait(barrier, groups - 2)

    @pl.when(me == half)
    def _():
        for head in range(heads):
            query_copy(head, 0).start()

    @pl.when(me == groups - 1)
    def _():
        query_copy(0, 1).start()

    @pl.when(jnp.logical_not(odd))
    def _():
        key_copy(0).start()
        value_copy(0).start()

    @pl.when(me == 0)
    def _():
        send_home(3, 2)
        key_copy(1).start()
        value_copy(1).start()
        send_home(3, 3)
        for head in range(2, heads):
            key_copy(head).start()
            value_copy(head).start()

    @pl.when(me == second)
    def _():
        for head in (2, 3):
            send_home(3, head)

    round_taps(0)

    @pl.when(me <= second)
    def _():
        for head in (0, 1):
            send_home(3, head)

    @pl.when(me == half)
    def _():
        for head in range(1, heads):
            key_copy(head).start()
            value_copy(head).start()
        for head in (0, 1, 2, 3):
            send_home(3, head)

    @pl.when(me == groups - 1)
    def _():
        for head in (2, 3):
            send_home(3, head)

    for load in loads:
        load.wait()

    starts = []
    total = 0
    wide_end = 0
    wide_start = 0
    for doc in range(docs_ref.shape[0]):
        starts.append(total)
        begun = total <= rows
        wide_start = jnp.where(begun, total, wide_start)
        total = total + docs_ref[doc]
        wide_end = jnp.where(begun, total, wide_end)

    def start_body(at, carry):
        row_pos = lax.broadcasted_iota(jnp.int32, (block, width), 0) + (me * rows + at * block)
        row_start = jnp.zeros((block, width), jnp.int32)
        for start in starts:
            row_start = jnp.where(row_pos >= start, start, row_start)
        row_starts[part_of(at), :] = row_start
        return carry

    lax.fori_loop(0, per_row, start_body, 0)
    lane_of = lax.broadcasted_iota(jnp.int32, (block, width), 1)
    row_of = lax.broadcasted_iota(jnp.int32, (block, width), 0)

    def attend(slot, query, chunks):
        top = jnp.full((block, width), masked_score, jnp.float32)
        for place, (key, _, mask) in enumerate(chunks):
            scores = lax.dot_general(
                query,
                key,
                (((1,), (1,)), ((), ())),
                preferred_element_type=jnp.float32,
            )
            for first in range(0, key.shape[0], width):
                piece = mask(scores[:, first : first + width], first)
                score_buf[slot, place, :, first : first + width] = piece
                top = jnp.maximum(top, piece)
        top = jnp.max(top, axis=1, keepdims=True)
        running = jnp.zeros((block, width), jnp.float32)
        weighted = jnp.zeros((block, width), jnp.float32)
        for place, (key, value, _) in enumerate(chunks):
            count = key.shape[0]
            weight = jnp.exp2((score_buf[slot, place, :, :count] - top) * scale)
            for first in range(0, count, width):
                running = running + weight[:, first : first + width]
            weighted = weighted + jnp.dot(
                weight.astype(jnp.bfloat16), value, preferred_element_type=jnp.float32
            )
        return (top * scale, jnp.sum(running, axis=1, keepdims=True), weighted)

    diagonal = lax.broadcasted_iota(jnp.int32, (width, width), 0) == lax.broadcasted_iota(
        jnp.int32, (width, width), 1
    )

    pieces_of = block // width

    def as_rows(packed, at, column):
        at_row = lax.broadcasted_iota(jnp.int32, (8, width), 0)
        for piece in range(pieces_of):
            spread = jnp.where(diagonal, column[piece * width : (piece + 1) * width, :], 0.0)
            line = jnp.sum(spread, axis=0, keepdims=True)
            packed = jnp.where(at_row == at * pieces_of + piece, line, packed)
        return packed

    def as_column(packed, at):
        pieces = []
        for piece in range(at * pieces_of, (at + 1) * pieces_of):
            spread = jnp.where(diagonal, packed[piece : piece + 1, :], 0.0)
            pieces.append(jnp.sum(spread, axis=1, keepdims=True))
        return jnp.concatenate(pieces, axis=0)

    def far_tiles(head):
        cols = cols_of(head)
        first_lane = lax.broadcasted_iota(jnp.int32, (1, rows), 1)
        outside = jnp.where(first_lane >= wide_start, 0.0, masked_score)

        def first_mask(scores, first):
            return scores + outside[:, first : first + width]

        def no_mask(scores, first):
            return scores

        def which_body(turn, carry):
            which = 1 - turn
            query_copy(head, which).wait_recv()
            packed = jnp.zeros((8, width), jnp.float32)
            for at in range(per_row):
                part = pl.ds(at * block, block)
                top, total_weight, weighted = attend(
                    at,
                    far_query[which, part, cols],
                    (
                        (prev_key[:, cols], prev_value[:, cols], first_mask),
                        (own_key[:, cols], own_value[:, cols], no_mask),
                    ),
                )
                far_out[which, part, cols] = (weighted / total_weight).astype(jnp.bfloat16)
                out_piece(head, which, at).start()
                level = top + jnp.log(total_weight) * math.log2(math.e)
                inside = row_of[:, :1] + ((half + which) * rows + at * block) < wide_end
                packed = as_rows(packed, at, jnp.where(inside, level, masked_score))
            far_stat[which, head] = packed
            stat_copy(head, which).start()
            return carry

        lax.fori_loop(0, groups - half, which_body, 0)

    def own_tiles(head, with_prev):
        cols = cols_of(head)
        for at in range(per_row):
            part = pl.ds(at * block, block)
            row_start = row_starts[part, :]
            count = (at + 1) * block

            def own_mask(scores, first, at=at, row_start=row_start):
                allowed = lane_of >= row_start - (me * rows + first)
                if first >= at * block:
                    allowed = allowed & (lane_of <= row_of - (first - at * block))
                return jnp.where(allowed, scores, masked_score)

            def prev_mask(scores, first, row_start=row_start):
                allowed = lane_of >= row_start - ((me - 1) * rows + first)
                return jnp.where(allowed, scores, masked_score)

            chunks = ((own_key[:count, cols], own_value[:count, cols], own_mask),)
            if with_prev:
                chunks = ((prev_key[:, cols], prev_value[:, cols], prev_mask),) + chunks
            top, total_weight, weighted = attend(at, own_query[part, cols], chunks)
            own_out[part, cols] = weighted
            own_top[head, part, :] = jnp.broadcast_to(top, (block, width))
            own_sum[head, part, :] = jnp.broadcast_to(total_weight, (block, width))

    def finish(head, merged):
        cols = cols_of(head)
        for at in range(per_row):
            part = pl.ds(at * block, block)
            weighted = own_out[part, cols]
            total_weight = own_sum[head, part, :]
            if merged:
                own_level = own_top[head, part, :]
                low_level = jnp.broadcast_to(as_column(low_stat[head], at), (block, width))
                level = jnp.maximum(own_level, low_level)
                own_share = jnp.exp2(own_level - level)
                low_share = jnp.exp2(low_level - level)
                total_weight = total_weight * own_share + low_share
                weighted = weighted * own_share + low_share * low_out[part, cols].astype(
                    jnp.float32
                )
            attended = (weighted / total_weight).astype(jnp.bfloat16)
            attn_buf[part, cols] = attended
            gated_buf[part, cols] = (
                own_gate[part, cols].astype(jnp.float32) * attended.astype(jnp.float32)
            ).astype(jnp.bfloat16)
        send_home(4, head)

    def merge(head):
        out_copy(head, me - half).wait_recv()
        stat_copy(head, me - half).wait_recv()
        finish(head, True)

    def head_body(head, carry):
        @pl.when(odd)
        def _():
            key_copy(head).wait_recv()
            value_copy(head).wait_recv()

        @pl.when((me == groups - 1) & (head < heads - 1))
        def _():
            query_copy(head + 1, 1).start()

        @pl.when((me == groups - 1) & (head == heads - 1))
        def _():
            send_home(3, 0)
            send_home(3, 1)

        only_when(me == second, lambda: far_tiles(head))
        only_when(odd, lambda: own_tiles(head, True))
        only_when(jnp.logical_not(odd), lambda: own_tiles(head, False))
        only_when(low, lambda: finish(head, False))
        only_when(high & (head > 0), lambda: merge(head - 1))
        return carry

    lax.fori_loop(0, heads, head_body, 0)
    only_when(high, lambda: merge(heads - 1))

    attn_done = pltpu.make_async_copy(attn_buf, attn_ref, local_sem.at[7])
    attn_done.start()

    lift = 8

    batch = 4

    def tap_blocks(count, source_of):
        def transform(at):
            tap_spec[at] = lax.dot_general(
                forward_buf[...],
                source_of(at),
                (((1,), (1,)), ((), ())),
                preferred_element_type=jnp.float32,
            )

        if count % batch:
            for at in range(count):
                transform(at)
        else:

            def body(turn, carry):
                for piece in range(batch):
                    transform(turn * batch + piece)
                return carry

            lax.fori_loop(0, count // batch, body, 0)

        uneven = lax.rem(lax.broadcasted_iota(jnp.int32, (lift, width), 0), 2) == 1
        sign = jnp.where(uneven, -1.0, 1.0).astype(jnp.float32)

        def combine_body(at, carry):
            real, imag = planes_of(at)
            for lane in range(2):
                cols = pl.ds(lane * width, width)
                reals = [tap_spec[k, real, cols] for k in range(count)]
                imags = [tap_spec[k, imag, cols] for k in range(count)]
                for k in range(count):
                    now_real = reals[k]
                    now_imag = imags[k]
                    if k > 0:
                        now_real = now_real - sign * imags[k - 1]
                        now_imag = now_imag + sign * reals[k - 1]
                    tap_spec[k, real, cols] = now_real
                    tap_spec[k, imag, cols] = now_imag
            return carry

        lax.fori_loop(0, block // lift, combine_body, 0)

    def planes_of(at):
        return tuple(
            pl.ds(pl.multiple_of(plane * block + at * lift, lift), lift) for plane in range(2)
        )

    def signal_block(at, source):
        sig_spec[at] = jnp.dot(forward_buf[...], source, preferred_element_type=jnp.float32)

    def products(cols, group):
        outs = range(group * per_row, (group + 1) * per_row)

        def product_rows(at):
            real, imag = planes_of(at)
            sums = {out: [jnp.zeros((lift, width), jnp.float32)] * 3 for out in outs}
            taps = {}
            for j in range(outs[-1] + 1):
                sig_real = sig_spec[j, real, :]
                sig_imag = sig_spec[j, imag, :]
                sig_both = sig_real + sig_imag
                for out in outs:
                    k = out - j
                    if k < 0:
                        continue
                    if k not in taps:
                        tap_real = tap_spec[k, real, cols]
                        tap_imag = tap_spec[k, imag, cols]
                        taps[k] = (tap_real, tap_imag - tap_real, tap_imag + tap_real)
                    tap_real, tap_less, tap_more = taps[k]
                    first, second_sum, third = sums[out]
                    sums[out] = [
                        first + sig_both * tap_real,
                        second_sum + sig_real * tap_less,
                        third + sig_imag * tap_more,
                    ]
            for out in outs:
                first, second_sum, third = sums[out]
                prod_spec[out, real, :] = first - third
                prod_spec[out, imag, :] = first + second_sum

        def product_body(turn, carry):
            for piece in range(batch):
                product_rows(turn * batch + piece)
            return carry

        lax.fori_loop(0, block // (lift * batch), product_body, 0)

    def mixed_block(index):
        return jnp.dot(
            inverse_buf[...],
            prod_spec[index].astype(jnp.bfloat16),
            preferred_element_type=jnp.float32,
        ).astype(jnp.bfloat16)

    def convolve(lane, carry):
        head = (me - second) * 2 + lane
        cols = cols_of(lane)
        for turn in range(groups):
            if turn < half:
                group = jnp.where(me == second, second - turn, half + turn)
            else:
                group = jnp.where(me == second, groups + second - turn, turn - half)
            if turn == 0:
                stay(4, head, group).wait()
            else:
                hop(4, head, group, second).wait_recv()
            for piece in range(per_row):
                at = group * per_row + piece
                signal_block(at, all_gate[part_of(at), cols])
        for group in [groups - 1] + list(range(1, groups - 1)):
            products(cols, group)
            for at in range(group * per_row, (group + 1) * per_row):
                mixed_buf[at * block : (at + 1) * block, cols] = mixed_block(at)
            only_when(me != group, lambda: hop(7, head, group, group).start())
            only_when(me == group, lambda: stay(7, head, group).start())
        return carry

    is_home = (me == second) | (me == half)

    @pl.when(is_home)
    def _():
        first = (me - second) * 2
        for lane in range(2):
            wait_home(3, first + lane)
        tap_blocks(blocks, lambda at: all_taps[:, part_of(at)])
        lax.fori_loop(0, 2, convolve, 0)

    @pl.when(me == 0)
    def _():
        def pair_body(pair, carry):
            channels_of = pl.ds(pl.multiple_of(pair * 2 * width, 2 * width), 2 * width)
            tap_blocks(per_row, lambda at: half_taps[channels_of, at * block : (at + 1) * block])

            def lane_body(lane, carry):
                cols = cols_of(pair * 2 + lane)
                for at in range(per_row):
                    signal_block(at, gated_buf[at * block : (at + 1) * block, cols])
                products(cols_of(lane), 0)
                for at in range(per_row):
                    first_mixed[at * block : (at + 1) * block, cols] = mixed_block(at)
                return carry

            lax.fori_loop(0, 2, lane_body, 0)
            return carry

        lax.fori_loop(0, heads // 2, pair_body, 0)
        first_done = pltpu.make_async_copy(first_mixed, mixed_back, local_sem.at[8])
        first_done.start()
        first_done.wait()

    for head in range(heads):
        home = home_of(head)
        only_when((me != home) & (me != 0), lambda: hop(7, head, me, home).wait_recv())
        only_when(me == home, lambda: stay(7, head, me).wait())
    attn_done.wait()

    for head in range(heads):
        home = home_of(head)

        @pl.when(jnp.logical_not(odd))
        def _():
            key_copy(head).wait_send()
            value_copy(head).wait_send()

        only_when(high, lambda: query_copy(head, me - half).wait_send())

        @pl.when(me != home)
        def _():
            hop(3, head, me, home).wait_send()
            hop(4, head, me, home).wait_send()

        for which in range(groups - half):

            @pl.when(me == second)
            def _():
                out_copy(head, which).wait_send()
                stat_copy(head, which).wait_send()

        for group in range(1, groups):
            if group != home:
                only_when(me == home, lambda: hop(7, head, group, group).wait_send())


PIECES = 2


def finish_kernel(
    attn_in,
    mixed_in,
    gate_in,
    attn_out,
    hyena_out,
    attn_buf,
    mixed_buf,
    gate_buf,
    hyena_buf,
    sem,
):
    count = mixed_buf.shape[0] // PIECES

    def move(kind, piece):
        part = pl.ds(piece * count, count)
        source, target = (
            (mixed_in, mixed_buf),
            (gate_in, gate_buf),
            (attn_in, attn_buf),
            (hyena_buf, hyena_out),
            (attn_buf, attn_out),
        )[kind]
        return pltpu.make_async_copy(source.at[part, :], target.at[part, :], sem.at[kind, piece])

    for piece in range(PIECES):
        move(2, piece).start()
    for piece in range(PIECES):
        move(0, piece).start()
        move(1, piece).start()
    for piece in range(PIECES):
        move(2, piece).wait()
        move(4, piece).start()
    for piece in range(PIECES):
        part = pl.ds(piece * count, count)
        move(0, piece).wait()
        move(1, piece).wait()
        hyena_buf[part, :] = (
            gate_buf[part, :].astype(jnp.float32) * mixed_buf[part, :].astype(jnp.float32)
        ).astype(jnp.bfloat16)
        move(3, piece).start()
    for piece in range(PIECES):
        move(3, piece).wait()
        move(4, piece).wait()


def fused_body(queries, key_rows, values, doc_lengths, in_gate, out_gate, filter_taps):
    rows, channels = queries.shape
    groups = lax.axis_size("ctx")
    width = channels // groups
    length = rows * groups
    block = BLOCK
    blocks = length // block
    per_row = rows // block
    heads = groups
    half_groups = groups // 2
    forward, inverse = block_tables(block)
    anywhere = pl.BlockSpec(memory_space=pl.ANY)
    half = jnp.bfloat16
    full = jnp.float32
    flat = (rows, channels)
    attended, mixed = pl.pallas_call(
        fused_kernel,
        out_shape=(
            jax.ShapeDtypeStruct(flat, half),
            jax.ShapeDtypeStruct(flat, half),
        ),
        in_specs=[pl.BlockSpec(memory_space=pltpu.SMEM)] + [anywhere] * 7,
        out_specs=(anywhere, anywhere),
        scratch_shapes=[
            pltpu.VMEM(flat, half),
            pltpu.VMEM(flat, half),
            pltpu.VMEM(flat, half),
            pltpu.VMEM(flat, half),
            pltpu.VMEM(flat, half),
            pltpu.VMEM(flat, half),
            pltpu.VMEM((half_groups,) + flat, half),
            pltpu.VMEM((half_groups,) + flat, half),
            pltpu.VMEM((half_groups, heads, 8, width), full),
            pltpu.VMEM(flat, half),
            pltpu.VMEM((heads, 8, width), full),
            pltpu.VMEM(flat, full),
            pltpu.VMEM((heads, rows, width), full),
            pltpu.VMEM((heads, rows, width), full),
            pltpu.VMEM((rows, width), jnp.int32),
            pltpu.VMEM(flat, half),
            pltpu.VMEM(flat, half),
            pltpu.VMEM(filter_taps.shape, full),
            pltpu.VMEM(filter_taps.shape, half),
            pltpu.VMEM(forward.shape, half),
            pltpu.VMEM(inverse.shape, half),
            pltpu.VMEM((length, 2 * width), half),
            pltpu.VMEM((2 * width, length), half),
            pltpu.VMEM((per_row, 2, block, rows), full),
            pltpu.VMEM((blocks, 2 * block, width), full),
            pltpu.VMEM((blocks, 2 * block, 2 * width), full),
            pltpu.VMEM((blocks, 2 * block, width), full),
            pltpu.VMEM((length, 2 * width), half),
            pltpu.VMEM(flat, half),
            pltpu.SemaphoreType.DMA((8, heads, groups)),
            pltpu.SemaphoreType.DMA((8, heads, groups)),
            pltpu.SemaphoreType.DMA((9,)),
            pltpu.SemaphoreType.DMA((heads // 2,)),
        ],
        compiler_params=pltpu.CompilerParams(
            collective_id=0, has_side_effects=True, vmem_limit_bytes=67043328
        ),
        name="fused_window",
    )(
        doc_lengths,
        queries,
        key_rows,
        values,
        in_gate,
        filter_taps,
        forward,
        inverse,
    )
    return pl.pallas_call(
        finish_kernel,
        out_shape=(
            jax.ShapeDtypeStruct(flat, half),
            jax.ShapeDtypeStruct(flat, half),
        ),
        in_specs=[anywhere] * 3,
        out_specs=(anywhere, anywhere),
        scratch_shapes=[
            pltpu.VMEM(flat, half),
            pltpu.VMEM(flat, half),
            pltpu.VMEM(flat, half),
            pltpu.VMEM(flat, half),
            pltpu.SemaphoreType.DMA((5, PIECES)),
        ],
        compiler_params=pltpu.CompilerParams(vmem_limit_bytes=67043328),
        name="finish_window",
    )(attended, mixed, out_gate)


def fits_fused(queries):
    rows, channels = queries.shape
    groups = lax.axis_size("ctx")
    return (
        groups == 4
        and channels == groups * HEAD_DIM
        and rows % BLOCK == 0
        and rows <= 8 * HEAD_DIM
    )


def either_body(queries, *rest):
    if fits_fused(queries):
        return fused_body(queries, *rest)
    return body(queries, *rest)


def solution(mesh):
    return jax.shard_map(
        either_body,
        mesh=mesh,
        in_specs=(
            P(("dp", "ctx"), "tp"),
            P(("dp", "ctx"), "tp"),
            P(("dp", "ctx"), "tp"),
            P("dp"),
            P(("dp", "ctx"), "tp"),
            P(("dp", "ctx"), "tp"),
            P(("dp", "tp"), "ctx"),
        ),
        out_specs=(P(("dp", "ctx"), "tp"), P(("dp", "ctx"), "tp")),
        check_vma=False,
    )
```

```python
import math

import jax
import jax.numpy as jnp
import numpy as np
from jax import lax
from jax.experimental import pallas as pl
from jax.experimental.pallas import tpu as pltpu
from jax.sharding import PartitionSpec as P

HEAD_DIM = 128
KV_REACH = 3
BLOCK = 256


masked_score = -1e30


def passed_along(x, axis, by):
    length = lax.axis_size(axis)
    pairs = [(i, i + by) for i in range(length) if 0 <= i + by < length]
    return lax.ppermute(x, axis, pairs)


def doc_of(positions, doc_lengths):
    order = jnp.arange(doc_lengths.shape[0], dtype=jnp.int32)
    before = order[None, :] < order[:, None]
    starts = jnp.sum(jnp.where(before, doc_lengths[None, :], 0), axis=1)
    inside = (starts[None, :] <= positions[:, None]).astype(jnp.int32)
    return jnp.sum(inside, axis=1) - 1


def attend_block(carried, pair, query_heads, allowed):
    running_max, running_sum, weighted = carried
    row_count = query_heads.shape[0]
    key_heads = pair[0].reshape(row_count, -1, HEAD_DIM)
    value_heads = pair[1].reshape(row_count, -1, HEAD_DIM)
    scores = jnp.einsum(
        "qhd,khd->hqk", query_heads, key_heads, preferred_element_type=jnp.float32
    ) / math.sqrt(HEAD_DIM)
    scores = jnp.where(allowed[None], scores, masked_score)
    new_max = jnp.maximum(running_max, jnp.max(scores, axis=2))
    rescale = jnp.exp(running_max - new_max)
    exp_scores = jnp.exp(scores - new_max[:, :, None])
    running_sum = running_sum * rescale + jnp.sum(exp_scores, axis=2)
    weighted = weighted * rescale[:, :, None] + jnp.einsum(
        "hqk,khd->hqd",
        exp_scores.astype(jnp.bfloat16),
        value_heads,
        preferred_element_type=jnp.float32,
    )
    return (new_max, running_sum, weighted)


def split_parts(source):
    high_part = lax.optimization_barrier(source.astype(jnp.bfloat16))
    low_part = (source - high_part.astype(jnp.float32)).astype(jnp.bfloat16)
    return (high_part, low_part)


def split_mul(form, left_parts, right_parts):
    first = jnp.einsum(form, left_parts[0], right_parts[0], preferred_element_type=jnp.float32)
    second = jnp.einsum(form, left_parts[0], right_parts[1], preferred_element_type=jnp.float32)
    third = jnp.einsum(form, left_parts[1], right_parts[0], preferred_element_type=jnp.float32)
    return first + (second + third)


def dft_tables(length):
    inner_len = math.gcd(length, 256)
    outer_len = 2 * length // inner_len
    freq_rows = jnp.arange(outer_len, dtype=jnp.int32)
    time_rows = jnp.arange(outer_len // 2, dtype=jnp.int32)
    inner_index = jnp.arange(inner_len, dtype=jnp.int32)
    angle_outer = (
        2.0
        * math.pi
        / outer_len
        * (freq_rows[:, None] * time_rows[None, :] % outer_len).astype(jnp.float32)
    )
    angle_twist = (
        2.0
        * math.pi
        / (2 * length)
        * (freq_rows[:, None] * inner_index[None, :] % (2 * length)).astype(jnp.float32)
    )
    angle_inner = (
        2.0
        * math.pi
        / inner_len
        * (inner_index[:, None] * inner_index[None, :] % inner_len).astype(jnp.float32)
    )
    return (
        split_parts(jnp.cos(angle_outer)),
        split_parts(-jnp.sin(angle_outer)),
        jnp.cos(angle_twist),
        -jnp.sin(angle_twist),
        split_parts(jnp.cos(angle_inner)),
        split_parts(-jnp.sin(angle_inner)),
    )


def right_mul(left_parts, table_parts):
    return split_mul("cin,nm->cim", left_parts, table_parts)


def forward_dft(samples, tables):
    outer_cos, outer_sin, twist_cos, twist_sin, inner_cos, inner_sin = tables
    item_count = samples.shape[0]
    shaped = split_parts(samples.reshape(item_count, outer_cos[0].shape[1], inner_cos[0].shape[0]))
    section_real = split_mul("ij,cjn->cin", outer_cos, shaped)
    section_imag = split_mul("ij,cjn->cin", outer_sin, shaped)
    turned_real = split_parts(section_real * twist_cos - section_imag * twist_sin)
    turned_imag = split_parts(section_real * twist_sin + section_imag * twist_cos)
    spec_real = right_mul(turned_real, inner_cos) - right_mul(turned_imag, inner_sin)
    spec_imag = right_mul(turned_real, inner_sin) + right_mul(turned_imag, inner_cos)
    return (spec_real, spec_imag)


def inverse_dft(prod_real, prod_imag, tables):
    outer_cos, outer_sin, twist_cos, twist_sin, inner_cos, inner_sin = tables
    item_count = prod_real.shape[0]
    half_len = outer_cos[0].shape[1]
    inner_len = inner_cos[0].shape[0]
    real_parts = split_parts(prod_real)
    imag_parts = split_parts(prod_imag)
    back_real = right_mul(real_parts, inner_cos) + right_mul(imag_parts, inner_sin)
    back_imag = right_mul(imag_parts, inner_cos) - right_mul(real_parts, inner_sin)
    unturn_real = split_parts(back_real * twist_cos + back_imag * twist_sin)
    unturn_imag = split_parts(back_imag * twist_cos - back_real * twist_sin)
    rows_out = split_mul("ij,cin->cjn", outer_cos, unturn_real) + split_mul(
        "ij,cin->cjn", outer_sin, unturn_imag
    )
    return (rows_out * (1.0 / (2 * half_len * inner_len))).reshape(item_count, half_len * inner_len)


def filter_apply(signal, filter_spec, tables):
    sig_real, sig_imag = forward_dft(signal, tables)
    tap_real, tap_imag = filter_spec
    prod_real = sig_real * tap_real - sig_imag * tap_imag
    prod_imag = sig_real * tap_imag + sig_imag * tap_real
    return inverse_dft(prod_real, prod_imag, tables)


def body(queries, key_rows, values, doc_lengths, in_gate, out_gate, filter_taps):
    row_count, channels = queries.shape
    head_count = channels // HEAD_DIM
    group_count = lax.axis_size("ctx")
    per_group = channels // group_count
    seq_len = row_count * group_count
    tables = dft_tables(seq_len)
    taps_grouped = filter_taps.reshape(group_count, per_group, row_count)
    query_pos = lax.axis_index("ctx") * row_count + jnp.arange(row_count, dtype=jnp.int32)
    query_doc = doc_of(query_pos, doc_lengths)
    query_heads = queries.reshape(row_count, head_count, HEAD_DIM)
    carried = (
        jnp.full((head_count, row_count), masked_score, jnp.float32),
        jnp.zeros((head_count, row_count), jnp.float32),
        jnp.zeros((head_count, row_count, HEAD_DIM), jnp.float32),
    )

    def visit(state_now, pair, distance):
        key_pos = query_pos - distance * row_count
        key_doc = doc_of(key_pos, doc_lengths)
        allowed = (key_doc[None, :] == query_doc[:, None]) & (
            key_pos[None, :] <= query_pos[:, None]
        )
        return lax.cond(
            jnp.any(allowed),
            lambda state_in: attend_block(state_in, pair, query_heads, allowed),
            lambda state_in: state_in,
            state_now,
        )

    own_pair = jnp.stack((key_rows, values))
    carried = visit(carried, own_pair, 0)
    moving = own_pair
    for distance in range(1, KV_REACH + 1):
        moving = passed_along(moving, "ctx", 1)
        carried = visit(carried, moving, distance)
    running_max, running_sum, weighted = carried
    attended = (
        (weighted / running_sum[:, :, None])
        .transpose(1, 0, 2)
        .reshape(row_count, channels)
        .astype(jnp.bfloat16)
    )
    gated = (in_gate.astype(jnp.float32) * attended.astype(jnp.float32)).T
    gated_grouped = gated.reshape(group_count, per_group, row_count)
    pair = (
        lax.all_to_all(
            gated_grouped.astype(jnp.bfloat16), "ctx", split_axis=0, concat_axis=2, tiled=True
        ).astype(gated_grouped.dtype),
        lax.all_to_all(
            taps_grouped.astype(jnp.bfloat16), "ctx", split_axis=0, concat_axis=2, tiled=True
        ).astype(taps_grouped.dtype),
    )
    item_count = pair[0].shape[1]
    signal = pair[0].reshape(item_count, -1)
    taps = pair[1].reshape(item_count, -1)
    result = filter_apply(signal, forward_dft(taps, tables), tables)
    mixed = result.reshape(1, item_count, -1)
    returned = lax.all_to_all(
        mixed.astype(jnp.bfloat16), "ctx", split_axis=2, concat_axis=0, tiled=True
    ).astype(mixed.dtype)
    hyena_out = (out_gate.astype(jnp.float32) * returned.reshape(channels, row_count).T).astype(
        jnp.bfloat16
    )
    return (attended, hyena_out)


def block_tables(block):
    freq = np.arange(block)
    time = np.arange(block)
    angle = np.pi / (2 * block) * ((2 * freq[:, None] + 1) * time[None, :] % (4 * block))
    forward = np.concatenate((np.cos(angle), -np.sin(angle)), axis=0)
    inverse = forward.T / block
    return (jnp.asarray(forward, jnp.bfloat16), jnp.asarray(inverse, jnp.bfloat16))


def only_when(condition, action):
    @pl.when(condition)
    def _():
        action()


def fused_kernel(
    docs_ref,
    query_ref,
    key_ref,
    value_ref,
    gate_ref,
    taps_ref,
    forward_ref,
    inverse_ref,
    attn_ref,
    mixed_back,
    own_query,
    own_key,
    own_value,
    own_gate,
    prev_key,
    prev_value,
    far_query,
    far_out,
    far_stat,
    low_out,
    low_stat,
    own_out,
    own_top,
    own_sum,
    row_starts,
    attn_buf,
    gated_buf,
    wide_taps,
    half_taps,
    forward_buf,
    inverse_buf,
    all_gate,
    all_taps,
    score_buf,
    sig_spec,
    tap_spec,
    prod_spec,
    mixed_buf,
    first_mixed,
    send_sem,
    recv_sem,
    local_sem,
    taps_sem,
):
    rows, channels = query_ref.shape
    length = all_gate.shape[0]
    groups = length // rows
    width = channels // groups
    heads = groups
    half = groups // 2
    block = inverse_ref.shape[0]
    blocks = length // block
    per_row = rows // block
    me = lax.axis_index("ctx")
    low = me < half
    high = me >= half
    second = half - 1
    odd = lax.rem(me, 2) == 1
    scale = math.log2(math.e) / math.sqrt(HEAD_DIM)

    def rows_of(group):
        return pl.ds(pl.multiple_of(group * rows, rows), rows)

    def cols_of(head):
        return pl.ds(pl.multiple_of(head * width, width), width)

    def home_of(head):
        return second + head // 2

    def part_of(at):
        return pl.ds(pl.multiple_of(at * block, block), block)

    barrier = pltpu.get_barrier_semaphore()
    for step in range(1, groups):
        peer = lax.rem(me + step, groups)

        @pl.when((me != 0) & ((me != groups - 1) | (peer != 0)))
        def _(peer=peer):
            pl.semaphore_signal(
                barrier, inc=1, device_id={"ctx": peer}, device_id_type=pl.DeviceIdType.MESH
            )


    def remote(kind, head, place, source, target, device):
        return pltpu.make_async_remote_copy(
            src_ref=source,
            dst_ref=target,
            send_sem=send_sem.at[kind, head, place],
            recv_sem=recv_sem.at[kind, head, place],
            device_id={"ctx": device},
            device_id_type=pl.DeviceIdType.MESH,
        )

    following = lax.rem(me + 1, groups)

    def key_copy(head):
        cols = cols_of(head)
        return remote(0, head, 0, key_ref.at[:, cols], prev_key.at[:, cols], following)

    def value_copy(head):
        cols = cols_of(head)
        return remote(1, head, 0, value_ref.at[:, cols], prev_value.at[:, cols], following)

    def query_copy(head, which):
        cols = cols_of(head)
        return remote(
            2, head, half + which, query_ref.at[:, cols], far_query.at[which, :, cols], second
        )

    def taps_refs(head, group):
        return (
            half_taps.at[cols_of(head), :],
            all_taps.at[cols_of(head % 2), rows_of(group)],
        )

    def gated_refs(head, group):
        return (
            gated_buf.at[:, cols_of(head)],
            all_gate.at[rows_of(group), cols_of(head % 2)],
        )

    def mixed_refs(head, group):
        return (
            mixed_buf.at[rows_of(group), cols_of(head % 2)],
            mixed_back.at[:, cols_of(head)],
        )

    refs_of = {3: taps_refs, 4: gated_refs, 7: mixed_refs}

    def hop(kind, head, group, device):
        return remote(kind, head, group, *refs_of[kind](head, group), device)

    def stay(kind, head, group):
        return pltpu.make_async_copy(
            *refs_of[kind](head, group), recv_sem.at[kind, head, group]
        )

    def send_home(kind, head):
        home = home_of(head)
        only_when(me != home, lambda: hop(kind, head, me, home).start())
        only_when(me == home, lambda: stay(kind, head, me).start())

    def wait_home(kind, head):
        for group in range(groups):
            only_when(me != group, lambda: hop(kind, head, group, second).wait_recv())
            only_when(me == group, lambda: stay(kind, head, group).wait())

    def out_copy(head, which):
        cols = cols_of(head)
        return remote(
            5, head, half + which, far_out.at[which, :, cols], low_out.at[:, cols], half + which
        )

    def out_piece(head, which, at):
        cols = cols_of(head)
        part = pl.ds(at * block, block)
        return remote(
            5,
            head,
            half + which,
            far_out.at[which, part, cols],
            low_out.at[part, cols],
            half + which,
        )

    def stat_copy(head, which):
        return remote(
            6, head, half + which, far_stat.at[which, head], low_stat.at[head], half + which
        )

    def pair_rows(pair):
        return pl.ds(pair * 2 * width, 2 * width)

    def taps_in(pair):
        return pltpu.make_async_copy(
            taps_ref.at[pair_rows(pair), :], wide_taps.at[pair_rows(pair), :], taps_sem.at[pair]
        )

    for pair in range(heads // 2 - 1, -1, -1):
        taps_in(pair).start()

    loads = []
    for place, (source, target) in enumerate(
        (
            (query_ref, own_query),
            (key_ref, own_key),
            (value_ref, own_value),
            (gate_ref, own_gate),
        )
    ):
        loads.append(pltpu.make_async_copy(source, target, local_sem.at[place]))
    loads.append(pltpu.make_async_copy(forward_ref, forward_buf, local_sem.at[5]))
    loads.append(pltpu.make_async_copy(inverse_ref, inverse_buf, local_sem.at[6]))
    for load in loads:
        load.start()

    def round_taps(pair):
        taps_in(pair).wait()

        def round_body(at, carry):
            part = pl.ds(pl.multiple_of(pair * 2 * width + at * 64, 64), 64)
            half_taps[part, :] = wide_taps[part, :].astype(jnp.bfloat16)
            return carry

        lax.fori_loop(0, 2 * width // 64, round_body, 0)

    round_taps(1)
    pl.semaphore_wait(barrier, groups - 2)

    @pl.when(me == half)
    def _():
        for head in range(heads):
            query_copy(head, 0).start()

    @pl.when(me == groups - 1)
    def _():
        query_copy(0, 1).start()

    @pl.when(jnp.logical_not(odd))
    def _():
        key_copy(0).start()
        value_copy(0).start()

    @pl.when(me == 0)
    def _():
        send_home(3, 2)
        key_copy(1).start()
        value_copy(1).start()
        send_home(3, 3)
        for head in range(2, heads):
            key_copy(head).start()
            value_copy(head).start()

    @pl.when(me == second)
    def _():
        for head in (2, 3):
            send_home(3, head)

    round_taps(0)

    @pl.when(me <= second)
    def _():
        for head in (0, 1):
            send_home(3, head)

    @pl.when(me == half)
    def _():
        for head in range(1, heads):
            key_copy(head).start()
            value_copy(head).start()
        for head in (0, 1, 2, 3):
            send_home(3, head)

    @pl.when(me == groups - 1)
    def _():
        for head in (2, 3):
            send_home(3, head)

    for load in loads:
        load.wait()

    starts = []
    total = 0
    wide_end = 0
    wide_start = 0
    for doc in range(docs_ref.shape[0]):
        starts.append(total)
        begun = total <= rows
        wide_start = jnp.where(begun, total, wide_start)
        total = total + docs_ref[doc]
        wide_end = jnp.where(begun, total, wide_end)

    def start_body(at, carry):
        row_pos = lax.broadcasted_iota(jnp.int32, (block, width), 0) + (me * rows + at * block)
        row_start = jnp.zeros((block, width), jnp.int32)
        for start in starts:
            row_start = jnp.where(row_pos >= start, start, row_start)
        row_starts[part_of(at), :] = row_start
        return carry

    lax.fori_loop(0, per_row, start_body, 0)
    lane_of = lax.broadcasted_iota(jnp.int32, (block, width), 1)
    row_of = lax.broadcasted_iota(jnp.int32, (block, width), 0)

    def attend(slot, query, chunks, between=None):
        top = jnp.full((block, width), masked_score, jnp.float32)
        for place, (key, _, mask) in enumerate(chunks):
            scores = lax.dot_general(
                query,
                key,
                (((1,), (1,)), ((), ())),
                preferred_element_type=jnp.float32,
            )
            for first in range(0, key.shape[0], width):
                piece = mask(scores[:, first : first + width], first)
                score_buf[slot, place, :, first : first + width] = piece
                top = jnp.maximum(top, piece)
        top = jnp.max(top, axis=1, keepdims=True)
        if between is not None:
            between()
        running = jnp.zeros((block, width), jnp.float32)
        weighted = jnp.zeros((block, width), jnp.float32)
        for place, (key, value, _) in enumerate(chunks):
            count = key.shape[0]
            weight = jnp.exp2((score_buf[slot, place, :, :count] - top) * scale)
            for first in range(0, count, width):
                running = running + weight[:, first : first + width]
            weighted = weighted + jnp.dot(
                weight.astype(jnp.bfloat16), value(), preferred_element_type=jnp.float32
            )
        return (top * scale, jnp.sum(running, axis=1, keepdims=True), weighted)

    diagonal = lax.broadcasted_iota(jnp.int32, (width, width), 0) == lax.broadcasted_iota(
        jnp.int32, (width, width), 1
    )

    pieces_of = block // width

    def as_rows(packed, at, column):
        at_row = lax.broadcasted_iota(jnp.int32, (8, width), 0)
        for piece in range(pieces_of):
            spread = jnp.where(diagonal, column[piece * width : (piece + 1) * width, :], 0.0)
            line = jnp.sum(spread, axis=0, keepdims=True)
            packed = jnp.where(at_row == at * pieces_of + piece, line, packed)
        return packed

    def as_column(packed, at):
        pieces = []
        for piece in range(at * pieces_of, (at + 1) * pieces_of):
            spread = jnp.where(diagonal, packed[piece : piece + 1, :], 0.0)
            pieces.append(jnp.sum(spread, axis=1, keepdims=True))
        return jnp.concatenate(pieces, axis=0)

    def far_tiles(head):
        cols = cols_of(head)
        first_lane = lax.broadcasted_iota(jnp.int32, (1, rows), 1)
        outside = jnp.where(first_lane >= wide_start, 0.0, masked_score)

        def first_mask(scores, first):
            return scores + outside[:, first : first + width]

        def no_mask(scores, first):
            return scores

        def which_body(turn, carry):
            which = 1 - turn

            def values_in():
                only_when(turn == 0, lambda: value_copy(head).wait_recv())

            query_copy(head, which).wait_recv()
            packed = jnp.zeros((8, width), jnp.float32)
            for at in range(per_row):
                part = pl.ds(at * block, block)
                top, total_weight, weighted = attend(
                    at,
                    far_query[which, part, cols],
                    (
                        (prev_key[:, cols], lambda: prev_value[:, cols], first_mask),
                        (own_key[:, cols], lambda: own_value[:, cols], no_mask),
                    ),
                    values_in if at == 0 else None,
                )
                far_out[which, part, cols] = (weighted / total_weight).astype(jnp.bfloat16)
                out_piece(head, which, at).start()
                level = top + jnp.log(total_weight) * math.log2(math.e)
                inside = row_of[:, :1] + ((half + which) * rows + at * block) < wide_end
                packed = as_rows(packed, at, jnp.where(inside, level, masked_score))
            far_stat[which, head] = packed
            stat_copy(head, which).start()
            return carry

        lax.fori_loop(0, groups - half, which_body, 0)

    def own_tiles(head, with_prev):
        cols = cols_of(head)
        for at in range(per_row):
            part = pl.ds(at * block, block)
            row_start = row_starts[part, :]
            count = (at + 1) * block

            def own_mask(scores, first, at=at, row_start=row_start):
                allowed = lane_of >= row_start - (me * rows + first)
                if first >= at * block:
                    allowed = allowed & (lane_of <= row_of - (first - at * block))
                return jnp.where(allowed, scores, masked_score)

            def prev_mask(scores, first, row_start=row_start):
                allowed = lane_of >= row_start - ((me - 1) * rows + first)
                return jnp.where(allowed, scores, masked_score)

            chunks = (
                (own_key[:count, cols], lambda count=count: own_value[:count, cols], own_mask),
            )
            if with_prev:
                chunks = ((prev_key[:, cols], lambda: prev_value[:, cols], prev_mask),) + chunks
            top, total_weight, weighted = attend(at, own_query[part, cols], chunks)
            own_out[part, cols] = weighted
            own_top[head, part, :] = jnp.broadcast_to(top, (block, width))
            own_sum[head, part, :] = jnp.broadcast_to(total_weight, (block, width))

    def finish(head, merged):
        cols = cols_of(head)
        for at in range(per_row):
            part = pl.ds(at * block, block)
            weighted = own_out[part, cols]
            total_weight = own_sum[head, part, :]
            if merged:
                own_level = own_top[head, part, :]
                low_level = jnp.broadcast_to(as_column(low_stat[head], at), (block, width))
                level = jnp.maximum(own_level, low_level)
                own_share = jnp.exp2(own_level - level)
                low_share = jnp.exp2(low_level - level)
                total_weight = total_weight * own_share + low_share
                weighted = weighted * own_share + low_share * low_out[part, cols].astype(
                    jnp.float32
                )
            attended = (weighted / total_weight).astype(jnp.bfloat16)
            attn_buf[part, cols] = attended
            gated_buf[part, cols] = (
                own_gate[part, cols].astype(jnp.float32) * attended.astype(jnp.float32)
            ).astype(jnp.bfloat16)
        send_home(4, head)

    def merge(head):
        out_copy(head, me - half).wait_recv()
        stat_copy(head, me - half).wait_recv()
        finish(head, True)

    def head_body(head, carry):
        @pl.when(odd)
        def _():
            key_copy(head).wait_recv()

        only_when(me == groups - 1, lambda: value_copy(head).wait_recv())

        @pl.when((me == groups - 1) & (head < heads - 1))
        def _():
            query_copy(head + 1, 1).start()

        @pl.when((me == groups - 1) & (head == heads - 1))
        def _():
            send_home(3, 0)
            send_home(3, 1)

        only_when(me == second, lambda: far_tiles(head))
        only_when(odd, lambda: own_tiles(head, True))
        only_when(jnp.logical_not(odd), lambda: own_tiles(head, False))
        only_when(low, lambda: finish(head, False))
        only_when(high & (head > 0), lambda: merge(head - 1))
        return carry

    lax.fori_loop(0, heads, head_body, 0)
    only_when(high, lambda: merge(heads - 1))

    attn_done = pltpu.make_async_copy(attn_buf, attn_ref, local_sem.at[7])
    attn_done.start()

    lift = 8

    batch = 4

    def tap_blocks(count, source_of):
        def transform(at):
            tap_spec[at] = lax.dot_general(
                forward_buf[...],
                source_of(at),
                (((1,), (1,)), ((), ())),
                preferred_element_type=jnp.float32,
            )

        if count % batch:
            for at in range(count):
                transform(at)
        else:

            def body(turn, carry):
                for piece in range(batch):
                    transform(turn * batch + piece)
                return carry

            lax.fori_loop(0, count // batch, body, 0)

        uneven = lax.rem(lax.broadcasted_iota(jnp.int32, (lift, width), 0), 2) == 1
        sign = jnp.where(uneven, -1.0, 1.0).astype(jnp.float32)

        def combine_body(at, carry):
            real, imag = planes_of(at)
            for lane in range(2):
                cols = pl.ds(lane * width, width)
                reals = [tap_spec[k, real, cols] for k in range(count)]
                imags = [tap_spec[k, imag, cols] for k in range(count)]
                for k in range(count):
                    now_real = reals[k]
                    now_imag = imags[k]
                    if k > 0:
                        now_real = now_real - sign * imags[k - 1]
                        now_imag = now_imag + sign * reals[k - 1]
                    tap_spec[k, real, cols] = now_real
                    tap_spec[k, imag, cols] = now_imag
            return carry

        lax.fori_loop(0, block // lift, combine_body, 0)

    def planes_of(at):
        return tuple(
            pl.ds(pl.multiple_of(plane * block + at * lift, lift), lift) for plane in range(2)
        )

    def signal_block(at, source):
        sig_spec[at] = jnp.dot(forward_buf[...], source, preferred_element_type=jnp.float32)

    def products(cols, group):
        outs = range(group * per_row, (group + 1) * per_row)

        def product_rows(at):
            real, imag = planes_of(at)
            sums = {out: [jnp.zeros((lift, width), jnp.float32)] * 3 for out in outs}
            taps = {}
            for j in range(outs[-1] + 1):
                sig_real = sig_spec[j, real, :]
                sig_imag = sig_spec[j, imag, :]
                sig_both = sig_real + sig_imag
                for out in outs:
                    k = out - j
                    if k < 0:
                        continue
                    if k not in taps:
                        tap_real = tap_spec[k, real, cols]
                        tap_imag = tap_spec[k, imag, cols]
                        taps[k] = (tap_real, tap_imag - tap_real, tap_imag + tap_real)
                    tap_real, tap_less, tap_more = taps[k]
                    first, second_sum, third = sums[out]
                    sums[out] = [
                        first + sig_both * tap_real,
                        second_sum + sig_real * tap_less,
                        third + sig_imag * tap_more,
                    ]
            for out in outs:
                first, second_sum, third = sums[out]
                prod_spec[out, real, :] = first - third
                prod_spec[out, imag, :] = first + second_sum

        def product_body(turn, carry):
            for piece in range(batch):
                product_rows(turn * batch + piece)
            return carry

        lax.fori_loop(0, block // (lift * batch), product_body, 0)

    def mixed_block(index):
        return jnp.dot(
            inverse_buf[...],
            prod_spec[index].astype(jnp.bfloat16),
            preferred_element_type=jnp.float32,
        ).astype(jnp.bfloat16)

    def convolve(lane, carry):
        head = (me - second) * 2 + lane
        cols = cols_of(lane)
        for turn in range(groups):
            if turn < half:
                group = jnp.where(me == second, second - turn, half + turn)
            else:
                group = jnp.where(me == second, groups + second - turn, turn - half)
            if turn == 0:
                stay(4, head, group).wait()
            else:
                hop(4, head, group, second).wait_recv()
            for piece in range(per_row):
                at = group * per_row + piece
                signal_block(at, all_gate[part_of(at), cols])
        for group in [groups - 1] + list(range(1, groups - 1)):
            products(cols, group)
            for at in range(group * per_row, (group + 1) * per_row):
                mixed_buf[at * block : (at + 1) * block, cols] = mixed_block(at)
            only_when(me != group, lambda: hop(7, head, group, group).start())
            only_when(me == group, lambda: stay(7, head, group).start())
        return carry

    is_home = (me == second) | (me == half)

    @pl.when(is_home)
    def _():
        first = (me - second) * 2
        for lane in range(2):
            wait_home(3, first + lane)
        tap_blocks(blocks, lambda at: all_taps[:, part_of(at)])
        lax.fori_loop(0, 2, convolve, 0)

    @pl.when(me == 0)
    def _():
        def pair_body(pair, carry):
            channels_of = pl.ds(pl.multiple_of(pair * 2 * width, 2 * width), 2 * width)
            tap_blocks(per_row, lambda at: half_taps[channels_of, at * block : (at + 1) * block])

            def lane_body(lane, carry):
                cols = cols_of(pair * 2 + lane)
                for at in range(per_row):
                    signal_block(at, gated_buf[at * block : (at + 1) * block, cols])
                products(cols_of(lane), 0)
                for at in range(per_row):
                    first_mixed[at * block : (at + 1) * block, cols] = mixed_block(at)
                return carry

            lax.fori_loop(0, 2, lane_body, 0)
            return carry

        lax.fori_loop(0, heads // 2, pair_body, 0)
        first_done = pltpu.make_async_copy(first_mixed, mixed_back, local_sem.at[8])
        first_done.start()
        first_done.wait()

    for head in range(heads):
        home = home_of(head)
        only_when((me != home) & (me != 0), lambda: hop(7, head, me, home).wait_recv())
        only_when(me == home, lambda: stay(7, head, me).wait())
    attn_done.wait()

    for head in range(heads):
        home = home_of(head)

        @pl.when(jnp.logical_not(odd))
        def _():
            key_copy(head).wait_send()
            value_copy(head).wait_send()

        only_when(high, lambda: query_copy(head, me - half).wait_send())

        @pl.when(me != home)
        def _():
            hop(3, head, me, home).wait_send()
            hop(4, head, me, home).wait_send()

        for which in range(groups - half):

            @pl.when(me == second)
            def _():
                out_copy(head, which).wait_send()
                stat_copy(head, which).wait_send()

        for group in range(1, groups):
            if group != home:
                only_when(me == home, lambda: hop(7, head, group, group).wait_send())


PIECES = 2


def finish_kernel(
    attn_in,
    mixed_in,
    gate_in,
    attn_out,
    hyena_out,
    attn_buf,
    mixed_buf,
    gate_buf,
    hyena_buf,
    sem,
):
    count = mixed_buf.shape[0] // PIECES

    def move(kind, piece):
        part = pl.ds(piece * count, count)
        source, target = (
            (mixed_in, mixed_buf),
            (gate_in, gate_buf),
            (attn_in, attn_buf),
            (hyena_buf, hyena_out),
            (attn_buf, attn_out),
        )[kind]
        return pltpu.make_async_copy(source.at[part, :], target.at[part, :], sem.at[kind, piece])

    for piece in range(PIECES):
        move(2, piece).start()
    for piece in range(PIECES):
        move(0, piece).start()
        move(1, piece).start()
    for piece in range(PIECES):
        move(2, piece).wait()
        move(4, piece).start()
    for piece in range(PIECES):
        part = pl.ds(piece * count, count)
        move(0, piece).wait()
        move(1, piece).wait()
        hyena_buf[part, :] = (
            gate_buf[part, :].astype(jnp.float32) * mixed_buf[part, :].astype(jnp.float32)
        ).astype(jnp.bfloat16)
        move(3, piece).start()
    for piece in range(PIECES):
        move(3, piece).wait()
        move(4, piece).wait()


def fused_body(queries, key_rows, values, doc_lengths, in_gate, out_gate, filter_taps):
    rows, channels = queries.shape
    groups = lax.axis_size("ctx")
    width = channels // groups
    length = rows * groups
    block = BLOCK
    blocks = length // block
    per_row = rows // block
    heads = groups
    half_groups = groups // 2
    forward, inverse = block_tables(block)
    anywhere = pl.BlockSpec(memory_space=pl.ANY)
    half = jnp.bfloat16
    full = jnp.float32
    flat = (rows, channels)
    attended, mixed = pl.pallas_call(
        fused_kernel,
        out_shape=(
            jax.ShapeDtypeStruct(flat, half),
            jax.ShapeDtypeStruct(flat, half),
        ),
        in_specs=[pl.BlockSpec(memory_space=pltpu.SMEM)] + [anywhere] * 7,
        out_specs=(anywhere, anywhere),
        scratch_shapes=[
            pltpu.VMEM(flat, half),
            pltpu.VMEM(flat, half),
            pltpu.VMEM(flat, half),
            pltpu.VMEM(flat, half),
            pltpu.VMEM(flat, half),
            pltpu.VMEM(flat, half),
            pltpu.VMEM((half_groups,) + flat, half),
            pltpu.VMEM((half_groups,) + flat, half),
            pltpu.VMEM((half_groups, heads, 8, width), full),
            pltpu.VMEM(flat, half),
            pltpu.VMEM((heads, 8, width), full),
            pltpu.VMEM(flat, full),
            pltpu.VMEM((heads, rows, width), full),
            pltpu.VMEM((heads, rows, width), full),
            pltpu.VMEM((rows, width), jnp.int32),
            pltpu.VMEM(flat, half),
            pltpu.VMEM(flat, half),
            pltpu.VMEM(filter_taps.shape, full),
            pltpu.VMEM(filter_taps.shape, half),
            pltpu.VMEM(forward.shape, half),
            pltpu.VMEM(inverse.shape, half),
            pltpu.VMEM((length, 2 * width), half),
            pltpu.VMEM((2 * width, length), half),
            pltpu.VMEM((per_row, 2, block, rows), full),
            pltpu.VMEM((blocks, 2 * block, width), full),
            pltpu.VMEM((blocks, 2 * block, 2 * width), full),
            pltpu.VMEM((blocks, 2 * block, width), full),
            pltpu.VMEM((length, 2 * width), half),
            pltpu.VMEM(flat, half),
            pltpu.SemaphoreType.DMA((8, heads, groups)),
            pltpu.SemaphoreType.DMA((8, heads, groups)),
            pltpu.SemaphoreType.DMA((9,)),
            pltpu.SemaphoreType.DMA((heads // 2,)),
        ],
        compiler_params=pltpu.CompilerParams(
            collective_id=0, has_side_effects=True, vmem_limit_bytes=67043328
        ),
        name="fused_window",
    )(
        doc_lengths,
        queries,
        key_rows,
        values,
        in_gate,
        filter_taps,
        forward,
        inverse,
    )
    return pl.pallas_call(
        finish_kernel,
        out_shape=(
            jax.ShapeDtypeStruct(flat, half),
            jax.ShapeDtypeStruct(flat, half),
        ),
        in_specs=[anywhere] * 3,
        out_specs=(anywhere, anywhere),
        scratch_shapes=[
            pltpu.VMEM(flat, half),
            pltpu.VMEM(flat, half),
            pltpu.VMEM(flat, half),
            pltpu.VMEM(flat, half),
            pltpu.SemaphoreType.DMA((5, PIECES)),
        ],
        compiler_params=pltpu.CompilerParams(vmem_limit_bytes=67043328),
        name="finish_window",
    )(attended, mixed, out_gate)


def fits_fused(queries):
    rows, channels = queries.shape
    groups = lax.axis_size("ctx")
    return (
        groups == 4
        and channels == groups * HEAD_DIM
        and rows % BLOCK == 0
        and rows <= 8 * HEAD_DIM
    )


def either_body(queries, *rest):
    if fits_fused(queries):
        return fused_body(queries, *rest)
    return body(queries, *rest)


def solution(mesh):
    return jax.shard_map(
        either_body,
        mesh=mesh,
        in_specs=(
            P(("dp", "ctx"), "tp"),
            P(("dp", "ctx"), "tp"),
            P(("dp", "ctx"), "tp"),
            P("dp"),
            P(("dp", "ctx"), "tp"),
            P(("dp", "ctx"), "tp"),
            P(("dp", "tp"), "ctx"),
        ),
        out_specs=(P(("dp", "ctx"), "tp"), P(("dp", "ctx"), "tp")),
        check_vma=False,
    )
```

```python
import math

import jax
import jax.numpy as jnp
import numpy as np
from jax import lax
from jax.experimental import pallas as pl
from jax.experimental.pallas import tpu as pltpu
from jax.sharding import PartitionSpec as P

HEAD_DIM = 128
KV_REACH = 3
BLOCK = 256


masked_score = -1e30


def passed_along(x, axis, by):
    length = lax.axis_size(axis)
    pairs = [(i, i + by) for i in range(length) if 0 <= i + by < length]
    return lax.ppermute(x, axis, pairs)


def doc_of(positions, doc_lengths):
    order = jnp.arange(doc_lengths.shape[0], dtype=jnp.int32)
    before = order[None, :] < order[:, None]
    starts = jnp.sum(jnp.where(before, doc_lengths[None, :], 0), axis=1)
    inside = (starts[None, :] <= positions[:, None]).astype(jnp.int32)
    return jnp.sum(inside, axis=1) - 1


def attend_block(carried, pair, query_heads, allowed):
    running_max, running_sum, weighted = carried
    row_count = query_heads.shape[0]
    key_heads = pair[0].reshape(row_count, -1, HEAD_DIM)
    value_heads = pair[1].reshape(row_count, -1, HEAD_DIM)
    scores = jnp.einsum(
        "qhd,khd->hqk", query_heads, key_heads, preferred_element_type=jnp.float32
    ) / math.sqrt(HEAD_DIM)
    scores = jnp.where(allowed[None], scores, masked_score)
    new_max = jnp.maximum(running_max, jnp.max(scores, axis=2))
    rescale = jnp.exp(running_max - new_max)
    exp_scores = jnp.exp(scores - new_max[:, :, None])
    running_sum = running_sum * rescale + jnp.sum(exp_scores, axis=2)
    weighted = weighted * rescale[:, :, None] + jnp.einsum(
        "hqk,khd->hqd",
        exp_scores.astype(jnp.bfloat16),
        value_heads,
        preferred_element_type=jnp.float32,
    )
    return (new_max, running_sum, weighted)


def split_parts(source):
    high_part = lax.optimization_barrier(source.astype(jnp.bfloat16))
    low_part = (source - high_part.astype(jnp.float32)).astype(jnp.bfloat16)
    return (high_part, low_part)


def split_mul(form, left_parts, right_parts):
    first = jnp.einsum(form, left_parts[0], right_parts[0], preferred_element_type=jnp.float32)
    second = jnp.einsum(form, left_parts[0], right_parts[1], preferred_element_type=jnp.float32)
    third = jnp.einsum(form, left_parts[1], right_parts[0], preferred_element_type=jnp.float32)
    return first + (second + third)


def dft_tables(length):
    inner_len = math.gcd(length, 256)
    outer_len = 2 * length // inner_len
    freq_rows = jnp.arange(outer_len, dtype=jnp.int32)
    time_rows = jnp.arange(outer_len // 2, dtype=jnp.int32)
    inner_index = jnp.arange(inner_len, dtype=jnp.int32)
    angle_outer = (
        2.0
        * math.pi
        / outer_len
        * (freq_rows[:, None] * time_rows[None, :] % outer_len).astype(jnp.float32)
    )
    angle_twist = (
        2.0
        * math.pi
        / (2 * length)
        * (freq_rows[:, None] * inner_index[None, :] % (2 * length)).astype(jnp.float32)
    )
    angle_inner = (
        2.0
        * math.pi
        / inner_len
        * (inner_index[:, None] * inner_index[None, :] % inner_len).astype(jnp.float32)
    )
    return (
        split_parts(jnp.cos(angle_outer)),
        split_parts(-jnp.sin(angle_outer)),
        jnp.cos(angle_twist),
        -jnp.sin(angle_twist),
        split_parts(jnp.cos(angle_inner)),
        split_parts(-jnp.sin(angle_inner)),
    )


def right_mul(left_parts, table_parts):
    return split_mul("cin,nm->cim", left_parts, table_parts)


def forward_dft(samples, tables):
    outer_cos, outer_sin, twist_cos, twist_sin, inner_cos, inner_sin = tables
    item_count = samples.shape[0]
    shaped = split_parts(samples.reshape(item_count, outer_cos[0].shape[1], inner_cos[0].shape[0]))
    section_real = split_mul("ij,cjn->cin", outer_cos, shaped)
    section_imag = split_mul("ij,cjn->cin", outer_sin, shaped)
    turned_real = split_parts(section_real * twist_cos - section_imag * twist_sin)
    turned_imag = split_parts(section_real * twist_sin + section_imag * twist_cos)
    spec_real = right_mul(turned_real, inner_cos) - right_mul(turned_imag, inner_sin)
    spec_imag = right_mul(turned_real, inner_sin) + right_mul(turned_imag, inner_cos)
    return (spec_real, spec_imag)


def inverse_dft(prod_real, prod_imag, tables):
    outer_cos, outer_sin, twist_cos, twist_sin, inner_cos, inner_sin = tables
    item_count = prod_real.shape[0]
    half_len = outer_cos[0].shape[1]
    inner_len = inner_cos[0].shape[0]
    real_parts = split_parts(prod_real)
    imag_parts = split_parts(prod_imag)
    back_real = right_mul(real_parts, inner_cos) + right_mul(imag_parts, inner_sin)
    back_imag = right_mul(imag_parts, inner_cos) - right_mul(real_parts, inner_sin)
    unturn_real = split_parts(back_real * twist_cos + back_imag * twist_sin)
    unturn_imag = split_parts(back_imag * twist_cos - back_real * twist_sin)
    rows_out = split_mul("ij,cin->cjn", outer_cos, unturn_real) + split_mul(
        "ij,cin->cjn", outer_sin, unturn_imag
    )
    return (rows_out * (1.0 / (2 * half_len * inner_len))).reshape(item_count, half_len * inner_len)


def filter_apply(signal, filter_spec, tables):
    sig_real, sig_imag = forward_dft(signal, tables)
    tap_real, tap_imag = filter_spec
    prod_real = sig_real * tap_real - sig_imag * tap_imag
    prod_imag = sig_real * tap_imag + sig_imag * tap_real
    return inverse_dft(prod_real, prod_imag, tables)


def body(queries, key_rows, values, doc_lengths, in_gate, out_gate, filter_taps):
    row_count, channels = queries.shape
    head_count = channels // HEAD_DIM
    group_count = lax.axis_size("ctx")
    per_group = channels // group_count
    seq_len = row_count * group_count
    tables = dft_tables(seq_len)
    taps_grouped = filter_taps.reshape(group_count, per_group, row_count)
    query_pos = lax.axis_index("ctx") * row_count + jnp.arange(row_count, dtype=jnp.int32)
    query_doc = doc_of(query_pos, doc_lengths)
    query_heads = queries.reshape(row_count, head_count, HEAD_DIM)
    carried = (
        jnp.full((head_count, row_count), masked_score, jnp.float32),
        jnp.zeros((head_count, row_count), jnp.float32),
        jnp.zeros((head_count, row_count, HEAD_DIM), jnp.float32),
    )

    def visit(state_now, pair, distance):
        key_pos = query_pos - distance * row_count
        key_doc = doc_of(key_pos, doc_lengths)
        allowed = (key_doc[None, :] == query_doc[:, None]) & (
            key_pos[None, :] <= query_pos[:, None]
        )
        return lax.cond(
            jnp.any(allowed),
            lambda state_in: attend_block(state_in, pair, query_heads, allowed),
            lambda state_in: state_in,
            state_now,
        )

    own_pair = jnp.stack((key_rows, values))
    carried = visit(carried, own_pair, 0)
    moving = own_pair
    for distance in range(1, KV_REACH + 1):
        moving = passed_along(moving, "ctx", 1)
        carried = visit(carried, moving, distance)
    running_max, running_sum, weighted = carried
    attended = (
        (weighted / running_sum[:, :, None])
        .transpose(1, 0, 2)
        .reshape(row_count, channels)
        .astype(jnp.bfloat16)
    )
    gated = (in_gate.astype(jnp.float32) * attended.astype(jnp.float32)).T
    gated_grouped = gated.reshape(group_count, per_group, row_count)
    pair = (
        lax.all_to_all(
            gated_grouped.astype(jnp.bfloat16), "ctx", split_axis=0, concat_axis=2, tiled=True
        ).astype(gated_grouped.dtype),
        lax.all_to_all(
            taps_grouped.astype(jnp.bfloat16), "ctx", split_axis=0, concat_axis=2, tiled=True
        ).astype(taps_grouped.dtype),
    )
    item_count = pair[0].shape[1]
    signal = pair[0].reshape(item_count, -1)
    taps = pair[1].reshape(item_count, -1)
    result = filter_apply(signal, forward_dft(taps, tables), tables)
    mixed = result.reshape(1, item_count, -1)
    returned = lax.all_to_all(
        mixed.astype(jnp.bfloat16), "ctx", split_axis=2, concat_axis=0, tiled=True
    ).astype(mixed.dtype)
    hyena_out = (out_gate.astype(jnp.float32) * returned.reshape(channels, row_count).T).astype(
        jnp.bfloat16
    )
    return (attended, hyena_out)


def block_tables(block):
    freq = np.arange(block)
    time = np.arange(block)
    angle = np.pi / (2 * block) * ((2 * freq[:, None] + 1) * time[None, :] % (4 * block))
    forward = np.concatenate((np.cos(angle), -np.sin(angle)), axis=0)
    inverse = forward.T / block
    return (jnp.asarray(forward, jnp.bfloat16), jnp.asarray(inverse, jnp.bfloat16))


def only_when(condition, action):
    @pl.when(condition)
    def _():
        action()


def fused_kernel(
    docs_ref,
    query_ref,
    key_ref,
    value_ref,
    gate_ref,
    taps_ref,
    forward_ref,
    inverse_ref,
    attn_ref,
    mixed_back,
    own_query,
    own_key,
    own_value,
    own_gate,
    prev_key,
    prev_value,
    far_query,
    far_out,
    far_stat,
    low_out,
    low_stat,
    own_out,
    own_top,
    own_sum,
    row_starts,
    attn_buf,
    gated_buf,
    wide_taps,
    half_taps,
    forward_buf,
    inverse_buf,
    all_gate,
    all_taps,
    score_buf,
    sig_spec,
    tap_spec,
    prod_spec,
    mixed_buf,
    first_mixed,
    send_sem,
    recv_sem,
    local_sem,
    taps_sem,
):
    rows, channels = query_ref.shape
    length = all_gate.shape[0]
    groups = length // rows
    width = channels // groups
    heads = groups
    half = groups // 2
    block = inverse_ref.shape[0]
    blocks = length // block
    per_row = rows // block
    me = lax.axis_index("ctx")
    low = me < half
    high = me >= half
    second = half - 1
    odd = lax.rem(me, 2) == 1
    scale = math.log2(math.e) / math.sqrt(HEAD_DIM)

    def rows_of(group):
        return pl.ds(pl.multiple_of(group * rows, rows), rows)

    def cols_of(head):
        return pl.ds(pl.multiple_of(head * width, width), width)

    def home_of(head):
        return second + head // 2

    def part_of(at):
        return pl.ds(pl.multiple_of(at * block, block), block)

    barrier = pltpu.get_barrier_semaphore()
    for step in range(1, groups):
        peer = lax.rem(me + step, groups)

        @pl.when((me != 0) & ((me != groups - 1) | (peer != 0)))
        def _(peer=peer):
            pl.semaphore_signal(
                barrier, inc=1, device_id={"ctx": peer}, device_id_type=pl.DeviceIdType.MESH
            )


    def remote(kind, head, place, source, target, device):
        return pltpu.make_async_remote_copy(
            src_ref=source,
            dst_ref=target,
            send_sem=send_sem.at[kind, head, place],
            recv_sem=recv_sem.at[kind, head, place],
            device_id={"ctx": device},
            device_id_type=pl.DeviceIdType.MESH,
        )

    following = lax.rem(me + 1, groups)

    def key_copy(head):
        cols = cols_of(head)
        return remote(0, head, 0, key_ref.at[:, cols], prev_key.at[:, cols], following)

    def value_copy(head):
        cols = cols_of(head)
        return remote(1, head, 0, value_ref.at[:, cols], prev_value.at[:, cols], following)

    def query_copy(head, which):
        cols = cols_of(head)
        return remote(
            2, head, half + which, query_ref.at[:, cols], far_query.at[which, :, cols], second
        )

    def taps_refs(head, group):
        return (
            half_taps.at[cols_of(head), :],
            all_taps.at[cols_of(head % 2), rows_of(group)],
        )

    def gated_refs(head, group):
        return (
            gated_buf.at[:, cols_of(head)],
            all_gate.at[rows_of(group), cols_of(head % 2)],
        )

    def mixed_refs(head, group):
        return (
            mixed_buf.at[rows_of(group), cols_of(head % 2)],
            mixed_back.at[:, cols_of(head)],
        )

    refs_of = {3: taps_refs, 4: gated_refs, 7: mixed_refs}

    def hop(kind, head, group, device):
        return remote(kind, head, group, *refs_of[kind](head, group), device)

    def stay(kind, head, group):
        return pltpu.make_async_copy(
            *refs_of[kind](head, group), recv_sem.at[kind, head, group]
        )

    def send_home(kind, head):
        home = home_of(head)
        only_when(me != home, lambda: hop(kind, head, me, home).start())
        only_when(me == home, lambda: stay(kind, head, me).start())

    def wait_home(kind, head):
        for group in range(groups):
            only_when(me != group, lambda: hop(kind, head, group, second).wait_recv())
            only_when(me == group, lambda: stay(kind, head, group).wait())

    def out_copy(head, which):
        cols = cols_of(head)
        return remote(
            5, head, half + which, far_out.at[which, :, cols], low_out.at[:, cols], half + which
        )

    def out_piece(head, which, at):
        cols = cols_of(head)
        part = pl.ds(at * block, block)
        return remote(
            5,
            head,
            half + which,
            far_out.at[which, part, cols],
            low_out.at[part, cols],
            half + which,
        )

    def stat_copy(head, which):
        return remote(
            6, head, half + which, far_stat.at[which, head], low_stat.at[head], half + which
        )

    def pair_rows(pair):
        return pl.ds(pair * 2 * width, 2 * width)

    def taps_in(pair):
        return pltpu.make_async_copy(
            taps_ref.at[pair_rows(pair), :], wide_taps.at[pair_rows(pair), :], taps_sem.at[pair]
        )

    for pair in range(heads // 2 - 1, -1, -1):
        taps_in(pair).start()

    loads = []
    for place, (source, target) in enumerate(
        (
            (query_ref, own_query),
            (key_ref, own_key),
            (value_ref, own_value),
            (gate_ref, own_gate),
        )
    ):
        loads.append(pltpu.make_async_copy(source, target, local_sem.at[place]))
    loads.append(pltpu.make_async_copy(forward_ref, forward_buf, local_sem.at[5]))
    loads.append(pltpu.make_async_copy(inverse_ref, inverse_buf, local_sem.at[6]))
    for load in loads:
        load.start()

    def round_taps(pair):
        taps_in(pair).wait()

        def round_body(at, carry):
            part = pl.ds(pl.multiple_of(pair * 2 * width + at * 64, 64), 64)
            half_taps[part, :] = wide_taps[part, :].astype(jnp.bfloat16)
            return carry

        lax.fori_loop(0, 2 * width // 64, round_body, 0)

    round_taps(1)
    pl.semaphore_wait(barrier, groups - 2)

    @pl.when(me == half)
    def _():
        for head in range(heads):
            query_copy(head, 0).start()

    @pl.when(me == groups - 1)
    def _():
        query_copy(0, 1).start()
        query_copy(1, 1).start()

    @pl.when(jnp.logical_not(odd))
    def _():
        key_copy(0).start()
        value_copy(0).start()

    @pl.when(me == 0)
    def _():
        send_home(3, 2)
        key_copy(1).start()
        value_copy(1).start()
        send_home(3, 3)
        for head in range(2, heads):
            key_copy(head).start()
            value_copy(head).start()

    @pl.when(me == second)
    def _():
        for head in (2, 3):
            send_home(3, head)

    round_taps(0)

    @pl.when(me <= second)
    def _():
        for head in (0, 1):
            send_home(3, head)

    @pl.when(me == half)
    def _():
        for head in range(1, heads):
            key_copy(head).start()
            value_copy(head).start()
        for head in (0, 1, 2, 3):
            send_home(3, head)

    @pl.when(me == groups - 1)
    def _():
        for head in (2, 3):
            send_home(3, head)

    for load in loads:
        load.wait()

    starts = []
    total = 0
    wide_end = 0
    wide_start = 0
    for doc in range(docs_ref.shape[0]):
        starts.append(total)
        begun = total <= rows
        wide_start = jnp.where(begun, total, wide_start)
        total = total + docs_ref[doc]
        wide_end = jnp.where(begun, total, wide_end)

    def start_body(at, carry):
        row_pos = lax.broadcasted_iota(jnp.int32, (block, width), 0) + (me * rows + at * block)
        row_start = jnp.zeros((block, width), jnp.int32)
        for start in starts:
            row_start = jnp.where(row_pos >= start, start, row_start)
        row_starts[part_of(at), :] = row_start
        return carry

    lax.fori_loop(0, per_row, start_body, 0)
    lane_of = lax.broadcasted_iota(jnp.int32, (block, width), 1)
    row_of = lax.broadcasted_iota(jnp.int32, (block, width), 0)

    def attend(slot, query, chunks, between=None):
        top = jnp.full((block, width), masked_score, jnp.float32)
        for place, (key, _, mask) in enumerate(chunks):
            scores = lax.dot_general(
                query,
                key,
                (((1,), (1,)), ((), ())),
                preferred_element_type=jnp.float32,
            )
            for first in range(0, key.shape[0], width):
                piece = mask(scores[:, first : first + width], first)
                score_buf[slot, place, :, first : first + width] = piece
                top = jnp.maximum(top, piece)
        top = jnp.max(top, axis=1, keepdims=True)
        if between is not None:
            between()
        running = jnp.zeros((block, width), jnp.float32)
        weighted = jnp.zeros((block, width), jnp.float32)
        for place, (key, value, _) in enumerate(chunks):
            count = key.shape[0]
            weight = jnp.exp2((score_buf[slot, place, :, :count] - top) * scale)
            for first in range(0, count, width):
                running = running + weight[:, first : first + width]
            weighted = weighted + jnp.dot(
                weight.astype(jnp.bfloat16), value(), preferred_element_type=jnp.float32
            )
        return (top * scale, jnp.sum(running, axis=1, keepdims=True), weighted)

    diagonal = lax.broadcasted_iota(jnp.int32, (width, width), 0) == lax.broadcasted_iota(
        jnp.int32, (width, width), 1
    )

    pieces_of = block // width

    def as_rows(packed, at, column):
        at_row = lax.broadcasted_iota(jnp.int32, (8, width), 0)
        for piece in range(pieces_of):
            spread = jnp.where(diagonal, column[piece * width : (piece + 1) * width, :], 0.0)
            line = jnp.sum(spread, axis=0, keepdims=True)
            packed = jnp.where(at_row == at * pieces_of + piece, line, packed)
        return packed

    def as_column(packed, at):
        pieces = []
        for piece in range(at * pieces_of, (at + 1) * pieces_of):
            spread = jnp.where(diagonal, packed[piece : piece + 1, :], 0.0)
            pieces.append(jnp.sum(spread, axis=1, keepdims=True))
        return jnp.concatenate(pieces, axis=0)

    def far_tiles(head):
        cols = cols_of(head)
        first_lane = lax.broadcasted_iota(jnp.int32, (1, rows), 1)
        outside = jnp.where(first_lane >= wide_start, 0.0, masked_score)

        def first_mask(scores, first):
            return scores + outside[:, first : first + width]

        def no_mask(scores, first):
            return scores

        def which_body(turn, carry):
            which = 1 - turn

            def values_in():
                only_when(turn == 0, lambda: value_copy(head).wait_recv())

            query_copy(head, which).wait_recv()
            packed = jnp.zeros((8, width), jnp.float32)
            for at in range(per_row):
                part = pl.ds(at * block, block)
                top, total_weight, weighted = attend(
                    at,
                    far_query[which, part, cols],
                    (
                        (prev_key[:, cols], lambda: prev_value[:, cols], first_mask),
                        (own_key[:, cols], lambda: own_value[:, cols], no_mask),
                    ),
                    values_in if at == 0 else None,
                )
                far_out[which, part, cols] = (weighted / total_weight).astype(jnp.bfloat16)
                out_piece(head, which, at).start()
                level = top + jnp.log(total_weight) * math.log2(math.e)
                inside = row_of[:, :1] + ((half + which) * rows + at * block) < wide_end
                packed = as_rows(packed, at, jnp.where(inside, level, masked_score))
            far_stat[which, head] = packed
            stat_copy(head, which).start()
            return carry

        lax.fori_loop(0, groups - half, which_body, 0)

    def own_tiles(head, with_prev):
        cols = cols_of(head)
        for at in range(per_row):
            part = pl.ds(at * block, block)
            row_start = row_starts[part, :]
            count = (at + 1) * block

            def own_mask(scores, first, at=at, row_start=row_start):
                allowed = lane_of >= row_start - (me * rows + first)
                if first >= at * block:
                    allowed = allowed & (lane_of <= row_of - (first - at * block))
                return jnp.where(allowed, scores, masked_score)

            def prev_mask(scores, first, row_start=row_start):
                allowed = lane_of >= row_start - ((me - 1) * rows + first)
                return jnp.where(allowed, scores, masked_score)

            chunks = (
                (own_key[:count, cols], lambda count=count: own_value[:count, cols], own_mask),
            )
            if with_prev:
                chunks = ((prev_key[:, cols], lambda: prev_value[:, cols], prev_mask),) + chunks
            top, total_weight, weighted = attend(at, own_query[part, cols], chunks)
            own_out[part, cols] = weighted
            own_top[head, part, :] = jnp.broadcast_to(top, (block, width))
            own_sum[head, part, :] = jnp.broadcast_to(total_weight, (block, width))

    def finish(head, merged):
        cols = cols_of(head)
        for at in range(per_row):
            part = pl.ds(at * block, block)
            weighted = own_out[part, cols]
            total_weight = own_sum[head, part, :]
            if merged:
                own_level = own_top[head, part, :]
                low_level = jnp.broadcast_to(as_column(low_stat[head], at), (block, width))
                level = jnp.maximum(own_level, low_level)
                own_share = jnp.exp2(own_level - level)
                low_share = jnp.exp2(low_level - level)
                total_weight = total_weight * own_share + low_share
                weighted = weighted * own_share + low_share * low_out[part, cols].astype(
                    jnp.float32
                )
            attended = (weighted / total_weight).astype(jnp.bfloat16)
            attn_buf[part, cols] = attended
            gated_buf[part, cols] = (
                own_gate[part, cols].astype(jnp.float32) * attended.astype(jnp.float32)
            ).astype(jnp.bfloat16)
        send_home(4, head)

    def merge(head):
        out_copy(head, me - half).wait_recv()
        stat_copy(head, me - half).wait_recv()
        finish(head, True)

    def head_body(head, carry):
        @pl.when(odd)
        def _():
            key_copy(head).wait_recv()

        only_when(me == groups - 1, lambda: value_copy(head).wait_recv())

        @pl.when((me == groups - 1) & (head < heads - 2))
        def _():
            query_copy(head + 2, 1).start()

        @pl.when((me == groups - 1) & (head == heads - 1))
        def _():
            send_home(3, 0)
            send_home(3, 1)

        only_when(me == second, lambda: far_tiles(head))
        only_when(odd, lambda: own_tiles(head, True))
        only_when(jnp.logical_not(odd), lambda: own_tiles(head, False))
        only_when(low, lambda: finish(head, False))
        only_when(high & (head > 0), lambda: merge(head - 1))
        return carry

    lax.fori_loop(0, heads, head_body, 0)
    only_when(high, lambda: merge(heads - 1))

    attn_done = pltpu.make_async_copy(attn_buf, attn_ref, local_sem.at[7])
    attn_done.start()

    lift = 8

    batch = 4

    def tap_blocks(count, source_of):
        def transform(at):
            tap_spec[at] = lax.dot_general(
                forward_buf[...],
                source_of(at),
                (((1,), (1,)), ((), ())),
                preferred_element_type=jnp.float32,
            )

        if count % batch:
            for at in range(count):
                transform(at)
        else:

            def body(turn, carry):
                for piece in range(batch):
                    transform(turn * batch + piece)
                return carry

            lax.fori_loop(0, count // batch, body, 0)

        uneven = lax.rem(lax.broadcasted_iota(jnp.int32, (lift, width), 0), 2) == 1
        sign = jnp.where(uneven, -1.0, 1.0).astype(jnp.float32)

        def combine_body(at, carry):
            real, imag = planes_of(at)
            for lane in range(2):
                cols = pl.ds(lane * width, width)
                reals = [tap_spec[k, real, cols] for k in range(count)]
                imags = [tap_spec[k, imag, cols] for k in range(count)]
                for k in range(count):
                    now_real = reals[k]
                    now_imag = imags[k]
                    if k > 0:
                        now_real = now_real - sign * imags[k - 1]
                        now_imag = now_imag + sign * reals[k - 1]
                    tap_spec[k, real, cols] = now_real
                    tap_spec[k, imag, cols] = now_imag
            return carry

        lax.fori_loop(0, block // lift, combine_body, 0)

    def planes_of(at):
        return tuple(
            pl.ds(pl.multiple_of(plane * block + at * lift, lift), lift) for plane in range(2)
        )

    def signal_block(at, source):
        sig_spec[at] = jnp.dot(forward_buf[...], source, preferred_element_type=jnp.float32)

    def products(cols, group):
        outs = range(group * per_row, (group + 1) * per_row)

        def product_rows(at):
            real, imag = planes_of(at)
            sums = {out: [jnp.zeros((lift, width), jnp.float32)] * 3 for out in outs}
            taps = {}
            for j in range(outs[-1] + 1):
                sig_real = sig_spec[j, real, :]
                sig_imag = sig_spec[j, imag, :]
                sig_both = sig_real + sig_imag
                for out in outs:
                    k = out - j
                    if k < 0:
                        continue
                    if k not in taps:
                        tap_real = tap_spec[k, real, cols]
                        tap_imag = tap_spec[k, imag, cols]
                        taps[k] = (tap_real, tap_imag - tap_real, tap_imag + tap_real)
                    tap_real, tap_less, tap_more = taps[k]
                    first, second_sum, third = sums[out]
                    sums[out] = [
                        first + sig_both * tap_real,
                        second_sum + sig_real * tap_less,
                        third + sig_imag * tap_more,
                    ]
            for out in outs:
                first, second_sum, third = sums[out]
                prod_spec[out, real, :] = first - third
                prod_spec[out, imag, :] = first + second_sum

        def product_body(turn, carry):
            for piece in range(batch):
                product_rows(turn * batch + piece)
            return carry

        lax.fori_loop(0, block // (lift * batch), product_body, 0)

    def mixed_block(index):
        return jnp.dot(
            inverse_buf[...],
            prod_spec[index].astype(jnp.bfloat16),
            preferred_element_type=jnp.float32,
        ).astype(jnp.bfloat16)

    def convolve(lane, carry):
        head = (me - second) * 2 + lane
        cols = cols_of(lane)
        for turn in range(groups):
            if turn < half:
                group = jnp.where(me == second, second - turn, half + turn)
            else:
                group = jnp.where(me == second, groups + second - turn, turn - half)
            if turn == 0:
                stay(4, head, group).wait()
            else:
                hop(4, head, group, second).wait_recv()
            for piece in range(per_row):
                at = group * per_row + piece
                signal_block(at, all_gate[part_of(at), cols])
        for group in [groups - 1] + list(range(1, groups - 1)):
            products(cols, group)
            for at in range(group * per_row, (group + 1) * per_row):
                mixed_buf[at * block : (at + 1) * block, cols] = mixed_block(at)
            only_when(me != group, lambda: hop(7, head, group, group).start())
            only_when(me == group, lambda: stay(7, head, group).start())
        return carry

    is_home = (me == second) | (me == half)

    @pl.when(is_home)
    def _():
        first = (me - second) * 2
        for lane in range(2):
            wait_home(3, first + lane)
        tap_blocks(blocks, lambda at: all_taps[:, part_of(at)])
        lax.fori_loop(0, 2, convolve, 0)

    @pl.when(me == 0)
    def _():
        def pair_body(pair, carry):
            channels_of = pl.ds(pl.multiple_of(pair * 2 * width, 2 * width), 2 * width)
            tap_blocks(per_row, lambda at: half_taps[channels_of, at * block : (at + 1) * block])

            def lane_body(lane, carry):
                cols = cols_of(pair * 2 + lane)
                for at in range(per_row):
                    signal_block(at, gated_buf[at * block : (at + 1) * block, cols])
                products(cols_of(lane), 0)
                for at in range(per_row):
                    first_mixed[at * block : (at + 1) * block, cols] = mixed_block(at)
                return carry

            lax.fori_loop(0, 2, lane_body, 0)
            return carry

        lax.fori_loop(0, heads // 2, pair_body, 0)
        first_done = pltpu.make_async_copy(first_mixed, mixed_back, local_sem.at[8])
        first_done.start()
        first_done.wait()

    for head in range(heads):
        home = home_of(head)
        only_when((me != home) & (me != 0), lambda: hop(7, head, me, home).wait_recv())
        only_when(me == home, lambda: stay(7, head, me).wait())
    attn_done.wait()

    for head in range(heads):
        home = home_of(head)

        @pl.when(jnp.logical_not(odd))
        def _():
            key_copy(head).wait_send()
            value_copy(head).wait_send()

        only_when(high, lambda: query_copy(head, me - half).wait_send())

        @pl.when(me != home)
        def _():
            hop(3, head, me, home).wait_send()
            hop(4, head, me, home).wait_send()

        for which in range(groups - half):

            @pl.when(me == second)
            def _():
                out_copy(head, which).wait_send()
                stat_copy(head, which).wait_send()

        for group in range(1, groups):
            if group != home:
                only_when(me == home, lambda: hop(7, head, group, group).wait_send())


PIECES = 2


def finish_kernel(
    attn_in,
    mixed_in,
    gate_in,
    attn_out,
    hyena_out,
    attn_buf,
    mixed_buf,
    gate_buf,
    hyena_buf,
    sem,
):
    count = mixed_buf.shape[0] // PIECES

    def move(kind, piece):
        part = pl.ds(piece * count, count)
        source, target = (
            (mixed_in, mixed_buf),
            (gate_in, gate_buf),
            (attn_in, attn_buf),
            (hyena_buf, hyena_out),
            (attn_buf, attn_out),
        )[kind]
        return pltpu.make_async_copy(source.at[part, :], target.at[part, :], sem.at[kind, piece])

    for piece in range(PIECES):
        move(2, piece).start()
    for piece in range(PIECES):
        move(0, piece).start()
        move(1, piece).start()
    for piece in range(PIECES):
        move(2, piece).wait()
        move(4, piece).start()
    for piece in range(PIECES):
        part = pl.ds(piece * count, count)
        move(0, piece).wait()
        move(1, piece).wait()
        hyena_buf[part, :] = (
            gate_buf[part, :].astype(jnp.float32) * mixed_buf[part, :].astype(jnp.float32)
        ).astype(jnp.bfloat16)
        move(3, piece).start()
    for piece in range(PIECES):
        move(3, piece).wait()
        move(4, piece).wait()


def fused_body(queries, key_rows, values, doc_lengths, in_gate, out_gate, filter_taps):
    rows, channels = queries.shape
    groups = lax.axis_size("ctx")
    width = channels // groups
    length = rows * groups
    block = BLOCK
    blocks = length // block
    per_row = rows // block
    heads = groups
    half_groups = groups // 2
    forward, inverse = block_tables(block)
    anywhere = pl.BlockSpec(memory_space=pl.ANY)
    half = jnp.bfloat16
    full = jnp.float32
    flat = (rows, channels)
    attended, mixed = pl.pallas_call(
        fused_kernel,
        out_shape=(
            jax.ShapeDtypeStruct(flat, half),
            jax.ShapeDtypeStruct(flat, half),
        ),
        in_specs=[pl.BlockSpec(memory_space=pltpu.SMEM)] + [anywhere] * 7,
        out_specs=(anywhere, anywhere),
        scratch_shapes=[
            pltpu.VMEM(flat, half),
            pltpu.VMEM(flat, half),
            pltpu.VMEM(flat, half),
            pltpu.VMEM(flat, half),
            pltpu.VMEM(flat, half),
            pltpu.VMEM(flat, half),
            pltpu.VMEM((half_groups,) + flat, half),
            pltpu.VMEM((half_groups,) + flat, half),
            pltpu.VMEM((half_groups, heads, 8, width), full),
            pltpu.VMEM(flat, half),
            pltpu.VMEM((heads, 8, width), full),
            pltpu.VMEM(flat, full),
            pltpu.VMEM((heads, rows, width), full),
            pltpu.VMEM((heads, rows, width), full),
            pltpu.VMEM((rows, width), jnp.int32),
            pltpu.VMEM(flat, half),
            pltpu.VMEM(flat, half),
            pltpu.VMEM(filter_taps.shape, full),
            pltpu.VMEM(filter_taps.shape, half),
            pltpu.VMEM(forward.shape, half),
            pltpu.VMEM(inverse.shape, half),
            pltpu.VMEM((length, 2 * width), half),
            pltpu.VMEM((2 * width, length), half),
            pltpu.VMEM((per_row, 2, block, rows), full),
            pltpu.VMEM((blocks, 2 * block, width), full),
            pltpu.VMEM((blocks, 2 * block, 2 * width), full),
            pltpu.VMEM((blocks, 2 * block, width), full),
            pltpu.VMEM((length, 2 * width), half),
            pltpu.VMEM(flat, half),
            pltpu.SemaphoreType.DMA((8, heads, groups)),
            pltpu.SemaphoreType.DMA((8, heads, groups)),
            pltpu.SemaphoreType.DMA((9,)),
            pltpu.SemaphoreType.DMA((heads // 2,)),
        ],
        compiler_params=pltpu.CompilerParams(
            collective_id=0, has_side_effects=True, vmem_limit_bytes=67043328
        ),
        name="fused_window",
    )(
        doc_lengths,
        queries,
        key_rows,
        values,
        in_gate,
        filter_taps,
        forward,
        inverse,
    )
    return pl.pallas_call(
        finish_kernel,
        out_shape=(
            jax.ShapeDtypeStruct(flat, half),
            jax.ShapeDtypeStruct(flat, half),
        ),
        in_specs=[anywhere] * 3,
        out_specs=(anywhere, anywhere),
        scratch_shapes=[
            pltpu.VMEM(flat, half),
            pltpu.VMEM(flat, half),
            pltpu.VMEM(flat, half),
            pltpu.VMEM(flat, half),
            pltpu.SemaphoreType.DMA((5, PIECES)),
        ],
        compiler_params=pltpu.CompilerParams(vmem_limit_bytes=67043328),
        name="finish_window",
    )(attended, mixed, out_gate)


def fits_fused(queries):
    rows, channels = queries.shape
    groups = lax.axis_size("ctx")
    return (
        groups == 4
        and channels == groups * HEAD_DIM
        and rows % BLOCK == 0
        and rows <= 8 * HEAD_DIM
    )


def either_body(queries, *rest):
    if fits_fused(queries):
        return fused_body(queries, *rest)
    return body(queries, *rest)


def solution(mesh):
    return jax.shard_map(
        either_body,
        mesh=mesh,
        in_specs=(
            P(("dp", "ctx"), "tp"),
            P(("dp", "ctx"), "tp"),
            P(("dp", "ctx"), "tp"),
            P("dp"),
            P(("dp", "ctx"), "tp"),
            P(("dp", "ctx"), "tp"),
            P(("dp", "tp"), "ctx"),
        ),
        out_specs=(P(("dp", "ctx"), "tp"), P(("dp", "ctx"), "tp")),
        check_vma=False,
    )
```
